32 devices in a mesh: grp: 2 (over y), strm: 8 (over z, x), azim: 2 (over core).
Axes of the slice: x: 2, y: 2, z: 4, core: 2. Of those that a mesh axis runs over, the one named last changes fastest.
Arguments:
- fields: bfloat16 [7, 512, 4096], P(None, None, ('grp', 'strm', 'azim')), parts along dimension 2, may hold values from -6 to 6
- elem_map: int32 [16, 128], P(('strm', 'azim')), may hold values from 0 to 127, each once within a row
- metric: float32 [3, 2048], P(None, ('strm', 'azim')), may hold values from 0.5 to 2
- inv_reynolds: float32 [2], P('grp'), parts along dimension 0, may hold values from 0.005 to 0.05
Outputs:
- indicator: float32 [4096], P(('grp', 'strm', 'azim')), parts along dimension 0
The draws below stay inside these ranges and needn't reach their ends.
There are 2 independent parts, one for each index of `grp`. The reference program is written for one: setup_inputs(seed, part) draws one part's arguments, and reference() takes and returns one part's arrays. A program takes and returns all parts, laid end to end along the dimension named above; an argument that names none is the same for every part. Nothing has to cross between parts.
Inputs may be any that keep to these rules, and one draw needn't show every extreme that they name: Each row of elem_map holds each of 0 to 127 once.
All inputs are finite; a program needn't handle non-finite values.
Results may differ from the reference program's by a relative error of at most 0.0003.
Values may be sent and summed in bfloat16 or wider, within the bound.
No kernel may reach another device: no remote copies, remote signals or barrier semaphores. Data moves between devices by JAX's collectives and lax.ppermute only.
A program may use at most 128 MiB of HBM per device.

```python
import math
import jax
import jax.numpy as jnp
import numpy as np
from jax import lax

ORDER_IN = 7
ORDER_OUT = 9
EX = 2
EY = 8
EZ = 8
E_DEV = 128
ELEMENTS = 2048
NODES_IN = 512
N_STRM = 8
N_AZIM = 2


def block_scale(own_key, shape, pieces, least, top_value):
    def one(dim, blocks):
        draws = jax.random.uniform(jax.random.fold_in(jax.random.fold_in(own_key, 6), dim), (blocks,), jnp.float32, least / len(pieces), top_value / len(pieces))
        return jnp.repeat(jnp.exp(draws), shape[dim] // blocks).reshape((-1,) + (1,) * (len(shape) - dim - 1))

    loudness = one(*pieces[0])
    for cut in pieces[1:]:
        loudness = loudness * one(*cut)
    return loudness


def noise(rng, shape, width, reach, shards=(), kind=jnp.bfloat16):
    factor_of = block_scale(rng, shape, shards, -0.22, 0.18) if shards else 1.0
    drawn = jax.random.normal(rng, shape, jnp.float32) * width * factor_of
    return jnp.minimum(jnp.maximum(drawn, -reach), reach).astype(kind)


def setup_inputs(seed: int = 0, part: int = 0) -> dict:
    arg_keys = jax.random.split(jax.random.key(seed), 5)
    part_keys = jax.random.split(jax.random.fold_in(arg_keys[4], part), 5)
    return {
        "fields": noise(part_keys[0], (7, NODES_IN, ELEMENTS), 1.0, 6.0, ((2, 16),)),
        "elem_map": jax.vmap(lambda own: jax.random.permutation(own, E_DEV))(jax.random.split(arg_keys[1], (N_STRM * N_AZIM))).reshape((N_STRM * N_AZIM, E_DEV)).astype(jnp.int32),
        "metric": jnp.clip(jnp.exp(math.log(2.0) - 1.3862944 * jax.random.uniform(arg_keys[2], (3, ELEMENTS), jnp.float32) ** block_scale(arg_keys[2], (3, ELEMENTS), ((1, 16),), -0.2, 0.2)), 0.5, 2.0),
        "inv_reynolds": jnp.clip(jnp.exp(jax.random.uniform(part_keys[3], (1,), jnp.float32, math.log(0.005), math.log(0.05))), 0.005, 0.05),
    }


HIGHEST = lax.Precision.HIGHEST

def gll_table(extent):
    degree = extent - 1
    points = np.cos(np.pi * np.arange(extent) / degree)
    legendre = np.zeros((extent, extent))
    for sweep in range(100):
        legendre[:, 0] = 1.0
        legendre[:, 1] = points
        for level in range(2, extent):
            legendre[:, level] = ((2 * level - 1) * points * legendre[:, level - 1] - (level - 1) * legendre[:, level - 2]) / level
        points = points - (points * legendre[:, degree] - legendre[:, degree - 1]) / (extent * legendre[:, degree])
    legendre[:, 0] = 1.0
    legendre[:, 1] = points
    for level in range(2, extent):
        legendre[:, level] = ((2 * level - 1) * points * legendre[:, level - 1] - (level - 1) * legendre[:, level - 2]) / level
    weights = 2.0 / (degree * extent * legendre[:, degree] ** 2)
    return (points[::-1].copy(), weights[::-1].copy())

def lagrange_matrix(source, target):
    result = np.ones((len(target), len(source)))
    for column in range(len(source)):
        for partner in range(len(source)):
            if partner != column:
                result[:, column] *= (target - source[partner]) / (source[column] - source[partner])
    return result

def derivative_matrix(points):
    extent = len(points)
    identity = np.eye(extent)
    spacing = points[:, None] - points[None, :] + identity
    barycen = 1.0 / np.prod(spacing, axis=1)
    matrix = barycen[None, :] / barycen[:, None] / spacing * (1.0 - identity)
    return matrix - identity * matrix.sum(axis=1)[:, None]

def tables():
    coarse_points, unused = gll_table(ORDER_IN + 1)
    fine_points, fine_weights = gll_table(ORDER_OUT + 1)
    interp = lagrange_matrix(coarse_points, fine_points)
    slopes = derivative_matrix(fine_points)
    quadrature = (fine_weights[:, None, None] * fine_weights[None, :, None] * fine_weights[None, None, :]).reshape(-1)
    return (jnp.asarray(interp, jnp.float32), jnp.asarray(slopes, jnp.float32), jnp.asarray(quadrature, jnp.float32))

def interpolate(interp, coarse):
    section_one = jnp.einsum('ia,cabde->cibde', interp, coarse, precision=HIGHEST)
    section_two = jnp.einsum('ib,cabde->caide', interp, section_one, precision=HIGHEST)
    return jnp.einsum('id,cabde->cabie', interp, section_two, precision=HIGHEST)

def derivatives(slopes, metric, field):
    return (jnp.einsum('ia,cabde->cibde', slopes, field, precision=HIGHEST) * metric[0], jnp.einsum('ib,cabde->caide', slopes, field, precision=HIGHEST) * metric[1], jnp.einsum('id,cabde->cabie', slopes, field, precision=HIGHEST) * metric[2])

def curl_of(grads):
    return jnp.stack([grads[1][2] - grads[2][1], grads[2][0] - grads[0][2], grads[0][1] - grads[1][0]])

def finish(smooth, metric, slopes, quadrature, inv_reynolds, average):
    base_flow = smooth[0:3]
    dual_flow = smooth[3:6]
    pressure_dual = smooth[6:7]
    base_grads = derivatives(slopes, metric, base_flow)
    dual_grads = derivatives(slopes, metric, dual_flow)
    press_grads = derivatives(slopes, metric, pressure_dual)
    vorticity = curl_of(dual_grads)
    vort_avg = average(vorticity)
    viscous = curl_of(derivatives(slopes, metric, vort_avg))
    convect = base_flow[0] * dual_grads[0] + base_flow[1] * dual_grads[1] + base_flow[2] * dual_grads[2]
    transport = jnp.stack([lax.optimization_barrier(jnp.sum(dual_flow * base_grads[0], axis=0)), lax.optimization_barrier(jnp.sum(dual_flow * base_grads[1], axis=0)), lax.optimization_barrier(jnp.sum(dual_flow * base_grads[2], axis=0))])
    pressure = jnp.concatenate([press_grads[0], press_grads[1], press_grads[2]])
    residual = -convect + transport + pressure + inv_reynolds[0] * viscous
    continuity = dual_grads[0][0] + dual_grads[1][1] + dual_grads[2][2]
    energy = lax.optimization_barrier(jnp.sum(residual * residual, axis=0)) + continuity * continuity
    weighted = jnp.dot(quadrature, energy.reshape(quadrature.shape[0], -1), precision=HIGHEST)
    return jnp.sqrt(weighted / 8.0) / float(ORDER_OUT ** 2)

def shared_sum(field_grid, node_axis, periodic):
    extent = field_grid.shape[node_axis]
    elem_axis = node_axis + 3
    length = field_grid.shape[elem_axis]
    lower_face = lax.index_in_dim(field_grid, 0, node_axis)
    upper_face = lax.index_in_dim(field_grid, extent - 1, node_axis)
    if periodic:
        from_before = jnp.roll(upper_face, 1, axis=elem_axis)
        from_after = jnp.roll(lower_face, -1, axis=elem_axis)
    else:
        empty_face = jnp.zeros_like(lax.index_in_dim(upper_face, 0, elem_axis))
        from_before = jnp.concatenate([empty_face, lax.slice_in_dim(upper_face, 0, length - 1, axis=elem_axis)], axis=elem_axis)
        from_after = jnp.concatenate([lax.slice_in_dim(lower_face, 1, length, axis=elem_axis), empty_face], axis=elem_axis)
    middle = lax.slice_in_dim(field_grid, 1, extent - 1, axis=node_axis)
    return jnp.concatenate([lower_face + from_before, middle, upper_face + from_after], axis=node_axis)

def stiffness_sum(field_grid):
    return shared_sum(shared_sum(shared_sum(field_grid, 1, True), 2, True), 3, False)

def reference(fields, elem_map, metric, inv_reynolds):
    interp, slopes, quadrature = tables()
    count_in = ORDER_IN + 1
    count_out = ORDER_OUT + 1
    blocks = N_STRM * N_AZIM
    ordering = jnp.argsort(elem_map, axis=1).astype(jnp.int32)
    total_elements = N_STRM * EX * N_AZIM * EY * EZ

    def to_grid(values, leading):
        blocked = values.reshape(leading + (blocks, E_DEV))
        gather_index = jnp.broadcast_to(ordering, blocked.shape)
        ordered = jnp.take_along_axis(blocked, gather_index, axis=-1)
        ordered = ordered.reshape(leading + (N_STRM, N_AZIM, EX, EY, EZ))
        leading_count = len(leading)
        permutation = tuple(range(leading_count)) + (leading_count, leading_count + 2, leading_count + 1, leading_count + 3, leading_count + 4)
        return jnp.transpose(ordered, permutation).reshape(leading + (total_elements,))
    nodal = to_grid(fields.astype(jnp.float32).reshape(7, count_in, count_in, count_in, ELEMENTS), (7, count_in, count_in, count_in))
    local_metric = to_grid(metric, (3,))
    refined = interpolate(interp, nodal)
    grid_tail = (count_out, count_out, count_out, N_STRM * EX, N_AZIM * EY, EZ)
    weight_inv = 1.0 / stiffness_sum(jnp.ones((1,) + grid_tail, jnp.float32))
    smooth = (stiffness_sum(refined.reshape((7,) + grid_tail)) * weight_inv).reshape(7, count_out, count_out, count_out, total_elements)

    def average(vorticity):
        summed = stiffness_sum(vorticity.reshape((3,) + grid_tail)) * weight_inv
        return summed.reshape(3, count_out, count_out, count_out, total_elements)
    indicator = finish(smooth, local_metric, slopes, quadrature, inv_reynolds, average)
    indicator = indicator.reshape(N_STRM, EX, N_AZIM, EY, EZ)
    indicator = jnp.transpose(indicator, (0, 2, 1, 3, 4)).reshape(blocks, E_DEV)
    return jnp.take_along_axis(indicator, elem_map, axis=1).reshape(ELEMENTS)
```

```python
import functools

import jax
import jax.numpy as jnp
import numpy as np
from jax import lax
from jax.experimental import pallas as pl
from jax.experimental.pallas import tpu as pltpu
from jax.sharding import PartitionSpec as P

ORDER_IN = 7
ORDER_OUT = 9
EY = 8
EZ = 8
NI = ORDER_IN + 1
NO = ORDER_OUT + 1
HI = NI // 2
HO = NO // 2
ROWS = 128
EXT = NI + 2
SEAM = EXT * NI
BF = jnp.bfloat16
F32 = jnp.float32
PLACE = {3: (0, 0), 4: (0, 1), 5: (1, 0), 6: (1, 1), 0: (2, 0), 1: (2, 1), 2: (3, 0)}


def gll_table(extent):
    degree = extent - 1
    points = np.cos(np.pi * np.arange(extent) / degree)
    legendre = np.zeros((extent, extent))

    def fill():
        legendre[:, 0] = 1.0
        legendre[:, 1] = points
        for level in range(2, extent):
            legendre[:, level] = (
                (2 * level - 1) * points * legendre[:, level - 1]
                - (level - 1) * legendre[:, level - 2]
            ) / level

    for sweep in range(100):
        fill()
        points = points - (points * legendre[:, degree] - legendre[:, degree - 1]) / (
            extent * legendre[:, degree]
        )
    fill()
    weights = 2.0 / (degree * extent * legendre[:, degree] ** 2)
    return (points[::-1].copy(), weights[::-1].copy())


def lagrange_matrix(source, target):
    result = np.ones((len(target), len(source)))
    for column in range(len(source)):
        for partner in range(len(source)):
            if partner != column:
                result[:, column] *= (target - source[partner]) / (source[column] - source[partner])
    return result


def derivative_matrix(points):
    extent = len(points)
    identity = np.eye(extent)
    spacing = points[:, None] - points[None, :] + identity
    barycen = 1.0 / np.prod(spacing, axis=1)
    matrix = barycen[None, :] / barycen[:, None] / spacing * (1.0 - identity)
    return matrix - identity * matrix.sum(axis=1)[:, None]


def bf16_parts(matrix):
    high = matrix.astype(jnp.bfloat16)
    low = (matrix - high.astype(np.float64)).astype(jnp.bfloat16)
    return high, low


def pad_rows(matrix, rows):
    return np.concatenate([matrix, np.zeros((rows - matrix.shape[0],) + matrix.shape[1:])])


def two_terms(matrix):
    return np.concatenate(bf16_parts(matrix), axis=-1)


@functools.cache
def tables():
    coarse, unused = gll_table(NI)
    fine, weights = gll_table(NO)
    interp = lagrange_matrix(coarse, fine)
    slopes = derivative_matrix(fine)
    ends = np.eye(NO)[:, [0, NO - 1]]
    value = np.concatenate([interp, ends], axis=1)
    both = slopes @ value

    def folded(matrix, parity):
        sign = 1.0 - 2.0 * parity
        if matrix.shape[1] == EXT and matrix is not slopes:
            left = matrix[:HO, [0, 1, 2, 3, 8]]
            right = matrix[:HO, [7, 6, 5, 4, 9]]
        else:
            left = matrix[:HO, :HO]
            right = matrix[:HO, ::-1][:, :HO]
        return left + sign * right

    refine = []
    for sector in range(8):
        pa, pb, pc = sector // 4, sector // 2 % 2, sector % 2
        blocks = []
        for ta, tb, tc in (
            (value, value, value),
            (both, value, value),
            (value, both, value),
            (value, value, both),
        ):
            block = 0.125 * np.einsum(
                "ap,bq,cr->abcrpq", folded(ta, pa), folded(tb, pb), folded(tc, pc)
            ).reshape(HO**3, HO, HO * HO)
            main = block[:, :, : HO * HO - 1].reshape(HO**3, -1)
            tail = np.pad(block[:, :, HO * HO - 1], ((0, 0), (0, ROWS - main.shape[1] - HO)))
            blocks.append(pad_rows(np.concatenate([main, tail], axis=1), ROWS))
        refine.append(two_terms(np.concatenate(blocks)))
    refine = np.stack(refine)

    second = []
    eye = np.eye(HO)
    for axis in range(3):
        for parity in range(2):
            factors = [eye, eye, eye]
            factors[axis] = folded(slopes, parity)
            block = np.kron(np.kron(factors[0], factors[1]), factors[2])
            edge = ROWS - HO**3
            second.append(two_terms(np.pad(block, ((0, edge), (0, edge)))))
    second = np.stack(second)

    def half(side):
        return value[:HO] if side == 0 else value[::-1][:HO]

    lift_x, lift_y = [], []
    for side in range(2):
        for radial in range(2):
            plain = np.zeros((HO, EXT, HO, NI))
            added = np.zeros((HO, EXT, HO, NI))
            plain[...] = np.einsum("ap,cr->apcr", half(side), half(radial)[:, :NI])
            added[..., 0] = np.einsum("ap,c->apc", half(side), half(radial)[:, NI])
            added[..., NI - 1] = np.einsum("ap,c->apc", half(side), half(radial)[:, NI + 1])
            face = np.stack([plain, added]).transpose(1, 3, 0, 2, 4).reshape(HO, HO, 2 * SEAM)
            lift_x.append(pad_rows(face.reshape(HO * HO, -1), 32))
            spread = np.zeros((HO, HO, HO, 2 * SEAM))
            spread[:, 0] = face
            lift_y.append(pad_rows(spread.reshape(HO**3, -1), ROWS))
    lift_x = two_terms(np.concatenate(lift_x))
    lift_y = two_terms(np.concatenate(lift_y))

    half_weights = weights[:HO]
    quad = np.kron(np.kron(half_weights, half_weights), half_weights)[:, None]
    quad = np.broadcast_to(pad_rows(quad, ROWS), (ROWS, 128)).astype(np.float32)
    line = []
    for end, far in ((0, NO - 1), (NO - 1, 0)):
        weights_in = slopes[end].copy()
        weights_in[[0, NO - 1]] = 0.0
        line.append(([float(v) for v in weights_in @ interp], float(slopes[end, far])))
    ends = (float(slopes[0, 0]), float(slopes[NO - 1, NO - 1]))
    return refine, second, lift_x, lift_y, quad, (line, ends)


def dot(a, b, contract_last=False):
    dims = (((1,), (1 if contract_last else 0,)), ((), ()))
    return lax.dot_general(a, b, dims, preferred_element_type=F32)


def rows3(x):
    return x.reshape(NI, NI, x.shape[-1])


def seam_rows(x):
    return x.reshape(SEAM, x.shape[-1])


def rows2(x):
    return x.reshape(NI * NI, x.shape[-1])


def roll(x, shift):
    count = x.shape[-1]
    return pltpu.roll(x, shift % count, x.ndim - 1)


def positions(shape):
    lane = lax.broadcasted_iota(jnp.int32, shape, len(shape) - 1)
    return lax.div(lane, EY * EZ), lax.rem(lax.div(lane, EZ), EY), lax.rem(lane, EZ)


def split3(x):
    high = x.astype(BF)
    rest = x - high.astype(F32)
    mid = rest.astype(BF)
    low = (rest - mid.astype(F32)).astype(BF)
    return high, mid, low


def slot_matrix(emap_ref, count):
    local = lax.broadcasted_iota(jnp.int32, (count, count), 0)
    return (local == emap_ref[...]).astype(F32).astype(BF)


def radial_added(x):
    axis = x.ndim - 2
    shape = (1,) * axis + x.shape[-2:]
    node = lax.broadcasted_iota(jnp.int32, shape, axis)
    iz = positions(shape)[2]
    last = x.shape[-2] - 1
    before = pltpu.roll(roll(x, 1), 1, axis)
    after = pltpu.roll(roll(x, -1), last, axis)
    low = (node == 0) & (iz > 0)
    high = (node == last) & (iz < EZ - 1)
    other = jnp.where(low, before, jnp.where(high, after, x))
    return 0.5 * (other - x)


def end_lines(line, planes, step):
    (near, near_far), (high, high_far) = line
    first, last = planes[0], planes[-1]
    one = near_far * 0.5 * (last + roll(first, -step))
    two = high_far * 0.5 * (first + roll(last, step))
    for i, plane in enumerate(planes):
        one = one + near[i] * plane
        two = two + high[i] * plane
    return one, two


def first_kernel(line, fields_ref, emap_ref, metric_ref, coarse_ref, metric_out, msg_ref):
    count = fields_ref.shape[-1]
    slots = slot_matrix(emap_ref, count)
    high, mid, low = split3(metric_ref[...])
    pad = jnp.zeros((7, count), F32)
    stacked = jnp.concatenate([high.astype(F32), mid.astype(F32), low.astype(F32), pad], axis=0)
    moved = dot(stacked.astype(BF), slots, True)
    local = moved[0:3] + moved[3:6] + moved[6:9]
    metric_out[...] = jnp.concatenate([local, jnp.zeros((5, count), F32)], axis=0)
    high = local.astype(BF).astype(F32)
    tail = jnp.concatenate([high, local - high, jnp.zeros((10, count), F32)], axis=0)
    msg_ref[9 * 64 : 9 * 64 + 16, :] = tail.astype(BF)
    iy = positions((1, 1, count))[1]
    for f in range(7):
        values = dot(fields_ref[f], slots, True).reshape(NI, NI, NI, count)
        coarse_ref[f] = values
        face = jnp.where(iy == 0, values[:, 0], values[:, NI - 1])
        msg_ref[f * 64 : f * 64 + 64, :] = rows2(face).astype(BF)
        if f in (3, 5):
            low, high = end_lines(line, [values[:, b] for b in range(NI)], EZ)
            at = (7 + (f == 5)) * 64
            msg_ref[at : at + 64, :] = rows2(jnp.where(iy == 0, low, high)).astype(BF)


def from_azim(x, iy):
    gap = (EY - 1) * EZ
    return jnp.where(iy == 0, roll(x, -gap), roll(x, gap))


def metric_classes(x, halo, shift, at_low, at_high):
    low = 0.5 * (x + jnp.where(at_low, halo, roll(x, shift)))
    high = 0.5 * (x + jnp.where(at_high, halo, roll(x, -shift)))
    return [x, low, high]


def radial_classes(x, iz):
    low = jnp.where(iz > 0, 0.5 * (x + roll(x, 1)), x)
    high = jnp.where(iz < EZ - 1, 0.5 * (x + roll(x, -1)), x)
    return [x, low, high]


def second_kernel(
    line, par_ref, coarse_ref, metric_ref, halo_ref, ext_ref, ends_ref, table_ref, a_ref, b_ref
):
    count = coarse_ref.shape[-1]
    layer = EY * EZ
    ix, iy, iz = positions((1, 1, count))
    blocks = []
    lines = []
    for f in range(7):
        values = coarse_ref[f]
        first, last = values[:, 0], values[:, NI - 1]
        halo = from_azim(rows3(halo_ref[f * 64 : f * 64 + 64, :].astype(F32)), iy)
        low = 0.5 * (jnp.where(iy == 0, halo, roll(last, EZ)) - first)
        high = 0.5 * (jnp.where(iy == EY - 1, halo, roll(first, -EZ)) - last)
        values = jnp.concatenate([values, low[:, None], high[:, None]], axis=1)
        ext_ref[f] = values
        blocks.append(seam_rows(jnp.where(ix == 0, values[0], values[NI - 1])))
        if f in (4, 5):
            low, high = end_lines(line, [values[a] for a in range(NI)], layer)
            lines.append(seam_rows(jnp.where(ix == 0, low, high)))
    blocks += lines
    extra = []
    for i in range(2):
        ends = from_azim(rows3(halo_ref[(7 + i) * 64 : (8 + i) * 64, :].astype(F32)), iy)
        ends_ref[i] = ends
        extra.append(jnp.where(ix[0] == 0, ends[0], ends[NI - 1]))

    ix, iy, iz = positions((1, count))
    packed = halo_ref[9 * 64 : 9 * 64 + 16, :].astype(F32)
    other = from_azim(packed[0:3] + packed[3:6], iy)
    own = metric_ref[...]
    lows, highs = iy == 0, iy == EY - 1
    rows = []
    for item in metric_classes(own[0:1], other[0:1], EZ, lows, highs):
        rows += radial_classes(item, iz)
    rows += radial_classes(own[1:2], iz)
    rows += metric_classes(own[2:3], other[2:3], EZ, lows, highs)
    rows += radial_classes(other[1:2], iz)
    table = jnp.concatenate(rows + [jnp.zeros((24 - len(rows), count), F32)], axis=0)
    table_ref[...] = table
    high = table.astype(BF).astype(F32)
    spare = jnp.zeros((SEAM - 64, count), F32)
    blocks.append(jnp.concatenate(extra + [high, table - high, spare], axis=0))

    ix = positions((SEAM, count))[0]
    even = par_ref[0] == 0
    half = len(blocks) // 2
    for i in range(half):
        one, two = blocks[i], blocks[half + i]
        down = jnp.where(ix == 0, one, roll(two, layer))
        up = jnp.where(ix == 0, roll(one, layer), two)
        rows = slice(i * SEAM, (i + 1) * SEAM)
        a_ref[rows, :] = jnp.where(even, up, down).astype(BF)
        b_ref[rows, :] = jnp.where(even, down, up).astype(BF)


def third_kernel(
    ends_value,
    par_ref,
    inv_ref,
    ext_ref,
    ends_ref,
    table_ref,
    metric_ref,
    emap_ref,
    ra_ref,
    rb_ref,
    refine_ref,
    second_ref,
    lift_x_ref,
    lift_y_ref,
    quad_ref,
    out_ref,
    tmp_ref,
    xs_ref,
    gs_ref,
    vort_ref,
    ws_ref,
    factor_ref,
    normal_x_ref,
    normal_y_ref,
):
    count = ext_ref.shape[-1]
    layer = EY * EZ
    even = par_ref[0] == 0
    ix = positions((SEAM, count))[0]
    end_low, end_high = ends_value

    halves = []
    for i in range(5):
        rows = slice(i * SEAM, (i + 1) * SEAM)
        one = ra_ref[rows, :].astype(F32)
        two = rb_ref[rows, :].astype(F32)
        down = jnp.where(even, two, one)
        up = jnp.where(even, one, two)
        halves.append(
            (
                jnp.where(ix == 0, down, roll(up, layer)),
                jnp.where(ix == 0, roll(down, layer), up),
            )
        )
    blocks = [item[0] for item in halves] + [item[1] for item in halves]

    ix3 = positions((1, 1, count))[0]
    iz24 = positions((HO * HO - 1, count))[2]
    iz1 = positions((1, count))[2]

    def signed(one, two, parity):
        return one + two if parity == 0 else one - two

    def radial(rows, iz, parity):
        last = NI - 1
        low = jnp.where(iz > 0, roll(rows[last], 1) - rows[0], 0.0)
        high = jnp.where(iz < EZ - 1, roll(rows[0], -1) - rows[last], 0.0)
        return [signed(rows[c], rows[last - c], parity) for c in range(HI)] + [
            0.5 * signed(low, high, parity)
        ]

    def stream_added(first, last, halo):
        lane = positions((1,) * (first.ndim - 1) + (count,))[0]
        low = 0.5 * (jnp.where(lane == 0, halo, roll(last, layer)) - first)
        high = 0.5 * (jnp.where(lane == 0, roll(first, -layer), halo) - last)
        return low, high

    seam = {}
    for f in range(7):
        pair, side = PLACE[f]
        lanes = slice(side * count, (side + 1) * count)
        values = ext_ref[f]
        halo = blocks[f].reshape(EXT, NI, count)
        first, last = values[0], values[NI - 1]
        low, high = stream_added(first, last, halo)
        if f in (4, 5):
            seam[f] = seam_rows(jnp.where(ix3 == 0, first + low, last + high))
        for pa in range(2):
            mixed = [signed(values[a], values[NI - 1 - a], pa) for a in range(HI)]
            mixed.append(signed(low, high, pa))
            for pb in range(2):
                at = f % 2 * 4 + pa * 2 + pb
                for a in range(HO):
                    for b in range(HO):
                        one = mixed[a][b if b < HI else NI]
                        two = mixed[a][NI - 1 - b if b < HI else NI + 1]
                        row = (a * HO + b) * NI
                        tmp_ref[at, row : row + NI, :] = signed(one, two, pb)
                main = [tmp_ref[at, pl.ds(c, HO * HO - 1, stride=NI), :] for c in range(NI)]
                start = (HO * HO - 1) * NI
                tail = [tmp_ref[at, start + c : start + c + 1, :] for c in range(NI)]
                for pc in range(2):
                    rows = radial(main, iz24, pc) + radial(tail, iz1, pc)
                    rows.append(jnp.zeros((3, count), F32))
                    operand = jnp.concatenate(rows, axis=0).astype(BF)
                    xs_ref[pair, pa * 4 + pb * 2 + pc, :, lanes] = operand

    def refine(sector, carry):
        for pair in range(4):
            width = 2 * count if pair < 3 else count
            source = xs_ref[pair, sector, :, 0:width]
            source = jnp.concatenate([source, source], axis=0)
            for q, flip in enumerate((0, 4, 2, 1)):
                gs_ref[pair, q, sector ^ flip, :, 0:width] = dot(
                    refine_ref[sector, q * ROWS : (q + 1) * ROWS, :], source
                )
        return carry

    lax.fori_loop(0, 8, refine, 0)

    row = lax.broadcasted_iota(jnp.int32, (ROWS, count), 0)
    a_edge = row < HO * HO
    b_edge = lax.rem(row, HO * HO) < HO
    c_edge = lax.rem(row, HO) == 0

    table = table_ref[...]
    packed = blocks[9]
    theirs = packed[16:40] + packed[40:64]
    lane_ix = positions((24, count))[0]
    at_low = 0.5 * (table + jnp.where(lane_ix == 0, theirs, roll(table, layer)))
    at_high = 0.5 * (table + jnp.where(lane_ix == 0, roll(table, -layer), theirs))

    def line_of(source, at):
        return source[at : at + 1]

    def by_radius(source, at, side):
        return jnp.where(c_edge, line_of(source, at + 1 + side), line_of(source, at))

    for one in range(2):
        edge = at_low if one == 0 else at_high
        for two in range(2):
            at = one * 2 + two
            factor_ref[at] = jnp.where(
                b_edge, by_radius(table, 3 + 3 * one, two), by_radius(table, 0, two)
            )
            factor_ref[4 + at] = jnp.where(
                a_edge, by_radius(edge, 9, two), by_radius(table, 9, two)
            )
            inside = jnp.where(b_edge, line_of(table, 13 + two), line_of(table, 12))
            outside = jnp.where(b_edge, line_of(edge, 13 + two), line_of(edge, 12))
            factor_ref[8 + at] = jnp.where(a_edge, outside, inside)

    def with_added(parts):
        halves = []
        for part in parts:
            stacked = part.reshape(EXT, NI, count)
            halves.append(jnp.concatenate([part, seam_rows(radial_added(stacked))], axis=0))
        operand = jnp.concatenate(halves, axis=1).astype(BF)
        return jnp.concatenate([operand, operand], axis=0)

    stream = []
    for i in range(2):
        shared = jnp.where(ix == 0, end_high, end_low) * seam[4 + i]
        stream.append(blocks[7 + i] + shared)
    lifted = dot(lift_x_ref[...], with_added(stream))
    for one in range(2):
        for two in range(2):
            at = one * 2 + two
            scale = jnp.where(
                b_edge, by_radius(theirs, 3 + 3 * one, two), by_radius(theirs, 0, two)
            )[0:32]
            for i in range(2):
                part = lifted[at * 32 : at * 32 + 32, i * count : (i + 1) * count]
                normal_x_ref[i, at] = part * scale

    iy3 = positions((1, 1, count))[1]
    iy2 = iy3[0]
    azim = []
    for i, f in enumerate((3, 5)):
        factor = jnp.where(iy3 == 0, end_high, end_low)
        values = ext_ref[f]
        halo = blocks[f].reshape(EXT, NI, count)
        near = jnp.where(
            iy3 == 0, values[:, 0] + values[:, NI], values[:, NI - 1] + values[:, NI + 1]
        )
        own = ends_ref[i] + factor * near
        near = jnp.where(iy2 == 0, halo[0] + halo[NI], halo[NI - 1] + halo[NI + 1])
        other = blocks[9][8 * i : 8 * i + 8] + factor[0] * near
        low, high = stream_added(own[0], own[NI - 1], other)
        azim.append(jnp.concatenate([rows2(own), low, high], axis=0))
    lifted = dot(lift_y_ref[...], with_added(azim))
    for one in range(2):
        edge = at_low if one == 0 else at_high
        for two in range(2):
            at = one * 2 + two
            scale = jnp.where(a_edge, by_radius(edge, 15, two), by_radius(table, 15, two))
            for i in range(2):
                part = lifted[at * ROWS : (at + 1) * ROWS, i * count : (i + 1) * count]
                normal_y_ref[i, at] = part * scale

    def nodal(f, q, at):
        pair, side = PLACE[f]
        lanes = slice(side * count, (side + 1) * count)
        return unfold([gs_ref[pair, q, sector, at, lanes] for sector in range(8)])

    everything = slice(0, ROWS)
    lane_ix, lane_iy, lane_iz = positions((ROWS, count))
    wide = slice(0, 32)

    def along_x(i, f):
        g = nodal(f, 1, everything)
        g = [g[s] * factor_ref[s % 4] for s in range(8)]
        near = lane_ix[wide] == 0
        inside = a_edge[wide]
        for at in range(4):
            one, two = g[at][wide], g[4 + at][wide]
            normal = normal_x_ref[i, at]
            first = 0.5 * (one + jnp.where(near, normal, roll(two, layer)))
            last = 0.5 * (two + jnp.where(near, roll(one, -layer), normal))
            g[at] = jnp.concatenate([jnp.where(inside, first, one), g[at][32:]], axis=0)
            g[4 + at] = jnp.concatenate([jnp.where(inside, last, two), g[4 + at][32:]], axis=0)
        return g

    def along_y(i, f):
        g = nodal(f, 2, everything)
        g = [g[s] * factor_ref[4 + s // 4 * 2 + s % 2] for s in range(8)]
        for at in range(4):
            here = at // 2 * 4 + at % 2
            one, two = g[here], g[here + 2]
            normal = normal_y_ref[i, at]
            first = 0.5 * (one + jnp.where(lane_iy == 0, normal, roll(two, EZ)))
            last = 0.5 * (two + jnp.where(lane_iy == EY - 1, normal, roll(one, -EZ)))
            g[here] = jnp.where(b_edge, first, one)
            g[here + 2] = jnp.where(b_edge, last, two)
        return g

    def along_z(f):
        g = nodal(f, 3, everything)
        g = [g[s] * factor_ref[8 + s // 2] for s in range(8)]
        low = c_edge & (lane_iz > 0)
        high = c_edge & (lane_iz < EZ - 1)
        for at in range(4):
            one, two = g[2 * at], g[2 * at + 1]
            g[2 * at] = jnp.where(low, 0.5 * (one + roll(two, 1)), one)
            g[2 * at + 1] = jnp.where(high, 0.5 * (two + roll(one, -1)), two)
        return g

    pairs = (
        (lambda: along_y(1, 5), lambda: along_z(4)),
        (lambda: along_z(3), lambda: along_x(1, 5)),
        (lambda: along_x(0, 4), lambda: along_y(0, 3)),
    )
    uses = {0: ((1, 1), (2, 0)), 1: ((0, 0), (2, 1)), 2: ((0, 1), (1, 0))}
    for i, (plus, minus) in enumerate(pairs):
        one, two = plus(), minus()
        folded = unfold([0.125 * (one[s] - two[s]) for s in range(8)])
        for sector in range(8):
            operand = folded[sector].astype(BF)
            for axis, side in uses[i]:
                vort_ref[axis, sector, :, side * count : (side + 1) * count] = operand

    for axis in range(3):
        flip = (4, 2, 1)[axis]
        for sector in range(8):
            source = vort_ref[axis, sector]
            source = jnp.concatenate([source, source], axis=0)
            which = 2 * axis + (1 if sector & flip else 0)
            ws_ref[axis, sector ^ flip] = dot(second_ref[which], source)

    metric = [metric_ref[i : i + 1] for i in range(3)]
    inv = inv_ref[0]
    scaled = [inv * metric[i] for i in range(3)]

    def body(step, total):
        at = pl.ds(pl.multiple_of(step * 8, 8), 8)
        for side in range(2):
            total = total + quad_ref[at, :] * energy_of(at, side)
        return total

    def energy_of(at, side):
        def unfold_half(parts):
            return unfold4([signed(parts[s], parts[4 + s], side) for s in range(4)])

        def part(f, q):
            pair, half = PLACE[f]
            lanes = slice(half * count, (half + 1) * count)
            return unfold_half([gs_ref[pair, q, s, at, lanes] for s in range(8)])

        def curl(axis, half, sector):
            return ws_ref[axis, sector, at, half * count : (half + 1) * count]

        base = [[item * metric[j] for item in part(j, 0)] for j in range(3)]
        dual = [part(3 + j, 0) for j in range(3)]
        energy = spread = None
        terms = (((1, 0), (2, 1)), ((2, 0), (0, 1)), ((0, 0), (1, 1)))
        for i in range(3):
            plus, minus = terms[i]
            linear = []
            for s in range(8):
                viscous = scaled[plus[0]] * curl(plus[0], plus[1], s)
                viscous = viscous - scaled[minus[0]] * curl(minus[0], minus[1], s)
                linear.append(gs_ref[1, 1 + i, s, at, count : 2 * count] * metric[i] + viscous)
            total = unfold_half(linear)
            for j in range(3):
                slope = part(3 + i, 1 + j)
                total = [total[s] - base[j][s] * slope[s] for s in range(4)]
                if i == j:
                    more = [slope[s] * metric[i] for s in range(4)]
                    spread = more if i == 0 else [spread[s] + more[s] for s in range(4)]
            inner = None
            for j in range(3):
                slope = part(j, 1 + i)
                more = [dual[j][s] * slope[s] for s in range(4)]
                inner = more if j == 0 else [inner[s] + more[s] for s in range(4)]
            total = [total[s] + metric[i] * inner[s] for s in range(4)]
            more = [item * item for item in total]
            energy = more if i == 0 else [energy[s] + more[s] for s in range(4)]
        energy = [energy[s] + spread[s] * spread[s] for s in range(4)]
        return (energy[0] + energy[1]) + (energy[2] + energy[3])

    total = lax.fori_loop(0, ROWS // 8, body, jnp.zeros((8, count), F32))
    weighted = jnp.sum(total, axis=0, keepdims=True)
    result = jnp.sqrt(weighted / 8.0) / float(ORDER_OUT**2)
    high, mid, low = split3(result)
    stacked = jnp.concatenate(
        [high.astype(F32), mid.astype(F32), low.astype(F32), jnp.zeros((13, count), F32)], axis=0
    )
    moved = dot(stacked.astype(BF), slot_matrix(emap_ref, count))
    out_ref[...] = moved[0:1] + moved[1:2] + moved[2:3]


def unfold4(parts):
    plus0, minus0 = parts[0] + parts[1], parts[0] - parts[1]
    plus1, minus1 = parts[2] + parts[3], parts[2] - parts[3]
    return [plus0 + plus1, minus0 + minus1, plus0 - plus1, minus0 - minus1]


def unfold(parts):
    plus = unfold4([parts[s] + parts[4 + s] for s in range(4)])
    minus = unfold4([parts[s] - parts[4 + s] for s in range(4)])
    return plus + minus


LIMIT = 60 * 1024 * 1024


def per_device(fields, elem_map, metric, inv_reynolds):
    refine, second, lift_x, lift_y, quad, (line, ends_value) = tables()
    count = fields.shape[-1]
    vmem = pl.BlockSpec(memory_space=pltpu.VMEM)
    smem = pl.BlockSpec(memory_space=pltpu.SMEM)
    params = pltpu.CompilerParams(vmem_limit_bytes=LIMIT)

    def struct(shape, dtype=F32):
        return jax.ShapeDtypeStruct(shape, dtype)

    coarse, local_metric, message = pl.pallas_call(
        functools.partial(first_kernel, line),
        out_shape=(
            struct((7, NI, NI, NI, count)),
            struct((8, count)),
            struct((9 * 64 + 16, count), BF),
        ),
        in_specs=[vmem] * 3,
        out_specs=(vmem,) * 3,
        compiler_params=params,
        name="first",
    )(fields, elem_map, metric)

    azim = lax.axis_size("azim")
    if azim == 2:
        halo = lax.ppermute(message, "azim", [(0, 1), (1, 0)])
    else:
        ahead = lax.ppermute(message, "azim", [(i, (i + 1) % azim) for i in range(azim)])
        behind = lax.ppermute(message, "azim", [((i + 1) % azim, i) for i in range(azim)])
        iy = (jnp.arange(count) // EZ) % EY
        halo = jnp.where(iy >= EY // 2, ahead, behind)

    place = lax.axis_index("strm")
    streams = lax.axis_size("strm")
    parity = lax.rem(place, 2).astype(jnp.int32).reshape(1)
    if streams % 2:
        parity = jnp.zeros((1,), jnp.int32)
    extended, ends, table, to_a, to_b = pl.pallas_call(
        functools.partial(second_kernel, line),
        out_shape=(
            struct((7, NI, EXT, NI, count)),
            struct((2, NI, NI, count)),
            struct((24, count)),
            struct((5 * SEAM, count), BF),
            struct((5 * SEAM, count), BF),
        ),
        in_specs=[smem] + [vmem] * 3,
        out_specs=(vmem,) * 5,
        compiler_params=params,
        name="second",
    )(parity, coarse, local_metric, halo)

    if streams % 2 == 0:
        near = [(i, i ^ 1) for i in range(streams)]
        far = []
        for i in range(1, streams, 2):
            far += [(i, (i + 1) % streams), ((i + 1) % streams, i)]
        got_a = lax.ppermute(to_a, "strm", near)
        got_b = lax.ppermute(to_b, "strm", far)
    else:
        got_b = lax.ppermute(to_a, "strm", [(i, (i + 1) % streams) for i in range(streams)])
        got_a = lax.ppermute(to_b, "strm", [((i + 1) % streams, i) for i in range(streams)])

    result = pl.pallas_call(
        functools.partial(third_kernel, ends_value),
        out_shape=struct((1, count)),
        in_specs=[smem] * 2 + [vmem] * 12,
        out_specs=vmem,
        scratch_shapes=[
            pltpu.VMEM((8, HO * HO * NI, count), F32),
            pltpu.VMEM((4, 8, ROWS, 2 * count), BF),
            pltpu.VMEM((4, 4, 8, ROWS, 2 * count), F32),
            pltpu.VMEM((3, 8, ROWS, 2 * count), BF),
            pltpu.VMEM((3, 8, ROWS, 2 * count), F32),
            pltpu.VMEM((12, ROWS, count), F32),
            pltpu.VMEM((2, 4, 32, count), F32),
            pltpu.VMEM((2, 4, ROWS, count), F32),
        ],
        compiler_params=params,
        name="third",
    )(
        parity,
        inv_reynolds,
        extended,
        ends,
        table,
        local_metric,
        elem_map,
        got_a,
        got_b,
        jnp.asarray(refine),
        jnp.asarray(second),
        jnp.asarray(lift_x),
        jnp.asarray(lift_y),
        jnp.asarray(quad),
    )
    return result.reshape(count)


def solution(mesh):
    return jax.shard_map(
        per_device,
        mesh=mesh,
        in_specs=(
            P(None, None, ("grp", "strm", "azim")),
            P(("strm", "azim"), None),
            P(None, ("strm", "azim")),
            P("grp"),
        ),
        out_specs=P(("grp", "strm", "azim")),
        check_vma=False,
    )
```

```python
import functools

import jax
import jax.numpy as jnp
import numpy as np
from jax import lax
from jax.experimental import pallas as pl
from jax.experimental.pallas import tpu as pltpu
from jax.sharding import PartitionSpec as P

ORDER_IN = 7
ORDER_OUT = 9
EY = 8
EZ = 8
NI = ORDER_IN + 1
NO = ORDER_OUT + 1
HI = NI // 2
HO = NO // 2
ROWS = 128
SEAM_ROWS = ROWS + 3 * 32
EXT = NI + 2
SEAM = EXT * NI
BF = jnp.bfloat16
F32 = jnp.float32
PLACE = {3: (0, 0), 4: (0, 1), 5: (1, 0), 0: (1, 1), 1: (2, 0), 2: (2, 1), 6: (3, 0)}
PAIRS = 4
FLIPS = (0, 4, 2, 1)


def gll_table(extent):
    degree = extent - 1
    points = np.cos(np.pi * np.arange(extent) / degree)
    legendre = np.zeros((extent, extent))

    def fill():
        legendre[:, 0] = 1.0
        legendre[:, 1] = points
        for level in range(2, extent):
            legendre[:, level] = (
                (2 * level - 1) * points * legendre[:, level - 1]
                - (level - 1) * legendre[:, level - 2]
            ) / level

    for sweep in range(100):
        fill()
        points = points - (points * legendre[:, degree] - legendre[:, degree - 1]) / (
            extent * legendre[:, degree]
        )
    fill()
    weights = 2.0 / (degree * extent * legendre[:, degree] ** 2)
    return (points[::-1].copy(), weights[::-1].copy())


def lagrange_matrix(source, target):
    result = np.ones((len(target), len(source)))
    for column in range(len(source)):
        for partner in range(len(source)):
            if partner != column:
                result[:, column] *= (target - source[partner]) / (source[column] - source[partner])
    return result


def derivative_matrix(points):
    extent = len(points)
    identity = np.eye(extent)
    spacing = points[:, None] - points[None, :] + identity
    barycen = 1.0 / np.prod(spacing, axis=1)
    matrix = barycen[None, :] / barycen[:, None] / spacing * (1.0 - identity)
    return matrix - identity * matrix.sum(axis=1)[:, None]


def bf16_parts(matrix):
    high = matrix.astype(jnp.bfloat16)
    low = (matrix - high.astype(np.float64)).astype(jnp.bfloat16)
    return high, low


def pad_rows(matrix, rows):
    return np.concatenate([matrix, np.zeros((rows - matrix.shape[0],) + matrix.shape[1:])])


def two_terms(matrix):
    return np.concatenate(bf16_parts(matrix), axis=-1)


@functools.cache
def tables():
    coarse, unused = gll_table(NI)
    fine, weights = gll_table(NO)
    interp = lagrange_matrix(coarse, fine)
    slopes = derivative_matrix(fine)
    ends = np.eye(NO)[:, [0, NO - 1]]
    value = np.concatenate([interp, ends], axis=1)
    both = slopes @ value

    def folded(matrix, parity):
        sign = 1.0 - 2.0 * parity
        if matrix.shape[1] == EXT and matrix is not slopes:
            left = matrix[:HO, [0, 1, 2, 3, 8]]
            right = matrix[:HO, [7, 6, 5, 4, 9]]
        else:
            left = matrix[:HO, :HO]
            right = matrix[:HO, ::-1][:, :HO]
        return left + sign * right

    refine, seams = [], []
    for sector in range(8):
        pa, pb, pc = sector // 4, sector // 2 % 2, sector % 2
        blocks, ends_of = [], []
        for ta, tb, tc in (
            (value, value, value),
            (both, value, value),
            (value, both, value),
            (value, value, both),
        ):
            block = 0.125 * np.einsum(
                "ap,bq,cr->abcrpq", folded(ta, pa), folded(tb, pb), folded(tc, pc)
            ).reshape(HO**3, HO, HO, HO)
            own = np.zeros((HO**3, HO, 24))
            own[:, :, : HO * HI] = block[:, :, :HI].reshape(HO**3, HO, HO * HI)
            own = np.pad(own.reshape(HO**3, -1), ((0, 0), (0, ROWS - 24 * HO)))
            blocks.append(pad_rows(own, ROWS))
            added = np.zeros((HO**3, 48))
            added[:, : 8 * HO] = np.pad(block[:, :, HI], ((0, 0), (0, 0), (0, 3))).reshape(HO**3, -1)
            ends_of.append(added)
        refine.append(two_terms(np.concatenate(blocks)))
        rows = [pad_rows(ends_of[1], ROWS)]
        rows += [pad_rows(ends_of[q][: HO * HO], 32) for q in (0, 2, 3)]
        seams.append(np.pad(two_terms(np.concatenate(rows)), ((0, 0), (0, ROWS - 96))))
    refine = np.stack(refine)
    seams = [np.concatenate(seams[2 * i : 2 * i + 2], axis=1) for i in range(4)]

    second = []
    eye = np.eye(HO)
    for axis in range(3):
        for parity in range(2):
            factors = [eye, eye, eye]
            factors[axis] = folded(slopes, parity)
            block = np.kron(np.kron(factors[0], factors[1]), factors[2])
            edge = ROWS - HO**3
            second.append(two_terms(np.pad(block, ((0, edge), (0, edge)))))
    second = np.stack(second)

    def half(side):
        return value[:HO] if side == 0 else value[::-1][:HO]

    lift_x, lift_y = [], []
    for side in range(2):
        for radial in range(2):
            plain = np.zeros((HO, EXT, HO, NI))
            added = np.zeros((HO, EXT, HO, NI))
            plain[...] = np.einsum("ap,cr->apcr", half(side), half(radial)[:, :NI])
            added[..., 0] = np.einsum("ap,c->apc", half(side), half(radial)[:, NI])
            added[..., NI - 1] = np.einsum("ap,c->apc", half(side), half(radial)[:, NI + 1])
            face = np.stack([plain, added]).transpose(1, 3, 0, 2, 4).reshape(HO, HO, 2 * SEAM)
            lift_x.append(pad_rows(face.reshape(HO * HO, -1), 32))
            spread = np.zeros((HO, HO, HO, 2 * SEAM))
            spread[:, 0] = face
            lift_y.append(pad_rows(spread.reshape(HO**3, -1), ROWS))

    def one_term(parts):
        matrix = np.concatenate(parts)
        return np.pad(matrix, ((0, 0), (0, 2 * ROWS - matrix.shape[1]))).astype(jnp.bfloat16)

    const = np.concatenate(
        [refine.reshape(-1, 2 * ROWS)]
        + seams
        + [second.reshape(-1, 2 * ROWS), one_term(lift_x), one_term(lift_y)]
    )
    half_weights = [float(v) for v in weights[:HO]]
    line = []
    for end, far in ((0, NO - 1), (NO - 1, 0)):
        weights_in = slopes[end].copy()
        weights_in[[0, NO - 1]] = 0.0
        line.append(([float(v) for v in weights_in @ interp], float(slopes[end, far])))
    ends = (float(slopes[0, 0]), float(slopes[NO - 1, NO - 1]))
    return const, half_weights, (line, ends)


def dot(a, b, contract_last=False):
    dims = (((1,), (1 if contract_last else 0,)), ((), ()))
    return lax.dot_general(a, b, dims, preferred_element_type=F32)


def rows3(x):
    return x.reshape(NI, NI, x.shape[-1])


def seam_rows(x):
    return x.reshape(SEAM, x.shape[-1])


def rows2(x):
    return x.reshape(NI * NI, x.shape[-1])


def roll(x, shift):
    count = x.shape[-1]
    return pltpu.roll(x, shift % count, x.ndim - 1)


def positions(shape):
    lane = lax.broadcasted_iota(jnp.int32, shape, len(shape) - 1)
    return lax.div(lane, EY * EZ), lax.rem(lax.div(lane, EZ), EY), lax.rem(lane, EZ)


def split3(x):
    high = x.astype(BF)
    rest = x - high.astype(F32)
    mid = rest.astype(BF)
    low = (rest - mid.astype(F32)).astype(BF)
    return high, mid, low


def radial_added(x):
    axis = x.ndim - 2
    shape = (1,) * axis + x.shape[-2:]
    node = lax.broadcasted_iota(jnp.int32, shape, axis)
    iz = positions(shape)[2]
    last = x.shape[-2] - 1
    before = pltpu.roll(roll(x, 1), 1, axis)
    after = pltpu.roll(roll(x, -1), last, axis)
    low = (node == 0) & (iz > 0)
    high = (node == last) & (iz < EZ - 1)
    other = jnp.where(low, before, jnp.where(high, after, x))
    return 0.5 * (other - x)


def end_lines(line, planes, step):
    (near, near_far), (high, high_far) = line
    first, last = planes[0], planes[-1]
    one = near_far * 0.5 * (last + roll(first, -step))
    two = high_far * 0.5 * (first + roll(last, step))
    for i, plane in enumerate(planes):
        one = one + near[i] * plane
        two = two + high[i] * plane
    return one, two


def first_kernel(line, fields, small_ref, slots_ref, metric_out, msg_ref):
    count = fields.shape[-1]
    local = lax.broadcasted_iota(jnp.int32, (count, count), 0).astype(F32)
    slots = (local == small_ref[0:1]).astype(F32).astype(BF)
    slots_ref[...] = slots
    high, mid, low = split3(small_ref[1:4])
    pad = jnp.zeros((7, count), F32)
    stacked = jnp.concatenate([high.astype(F32), mid.astype(F32), low.astype(F32), pad], axis=0)
    moved = dot(stacked.astype(BF), slots, True)
    local = moved[0:3] + moved[3:6] + moved[6:9]
    metric_out[...] = jnp.concatenate([local, jnp.zeros((5, count), F32)], axis=0)
    high = local.astype(BF).astype(F32)
    tail = jnp.concatenate([high, local - high, jnp.zeros((10, count), F32)], axis=0)
    msg_ref[9 * 64 : 9 * 64 + 16, :] = tail.astype(BF)
    iy = positions((1, 1, count))[1]
    for f in range(7):
        values = dot(fields[f], slots, True).reshape(NI, NI, NI, count)
        face = jnp.where(iy == 0, values[:, 0], values[:, NI - 1])
        msg_ref[f * 64 : f * 64 + 64, :] = rows2(face).astype(BF)
        if f in (3, 5):
            low, high = end_lines(line, [values[:, b] for b in range(NI)], EZ)
            at = (7 + (f == 5)) * 64
            msg_ref[at : at + 64, :] = rows2(jnp.where(iy == 0, low, high)).astype(BF)


def own_kernel(fields_ref, slots_ref, coarse_ref):
    count = fields_ref.shape[-1]
    for f in range(7):
        values = dot(fields_ref[f], slots_ref[...], True)
        coarse_ref[f] = values.reshape(NI, NI, NI, count)


def from_azim(x, iy):
    gap = (EY - 1) * EZ
    return jnp.where(iy == 0, roll(x, -gap), roll(x, gap))


def metric_classes(x, halo, shift, at_low, at_high):
    low = 0.5 * (x + jnp.where(at_low, halo, roll(x, shift)))
    high = 0.5 * (x + jnp.where(at_high, halo, roll(x, -shift)))
    return [x, low, high]


def radial_classes(x, iz):
    low = jnp.where(iz > 0, 0.5 * (x + roll(x, 1)), x)
    high = jnp.where(iz < EZ - 1, 0.5 * (x + roll(x, -1)), x)
    return [x, low, high]


def second_kernel(
    line, par_ref, coarse_ref, metric_ref, halo_ref, ext_ref, ends_ref, table_ref, a_ref, b_ref
):
    count = coarse_ref.shape[-1]
    layer = EY * EZ
    ix, iy, iz = positions((1, 1, count))
    blocks = []
    lines = []
    for f in range(7):
        values = coarse_ref[f]
        first, last = values[:, 0], values[:, NI - 1]
        halo = from_azim(rows3(halo_ref[f * 64 : f * 64 + 64, :].astype(F32)), iy)
        low = 0.5 * (jnp.where(iy == 0, halo, roll(last, EZ)) - first)
        high = 0.5 * (jnp.where(iy == EY - 1, halo, roll(first, -EZ)) - last)
        values = jnp.concatenate([values, low[:, None], high[:, None]], axis=1)
        ext_ref[f] = values
        blocks.append(seam_rows(jnp.where(ix == 0, values[0], values[NI - 1])))
        if f in (4, 5):
            low, high = end_lines(line, [values[a] for a in range(NI)], layer)
            lines.append(seam_rows(jnp.where(ix == 0, low, high)))
    blocks += lines
    extra = []
    for i in range(2):
        ends = from_azim(rows3(halo_ref[(7 + i) * 64 : (8 + i) * 64, :].astype(F32)), iy)
        ends_ref[i] = ends
        extra.append(jnp.where(ix[0] == 0, ends[0], ends[NI - 1]))

    ix, iy, iz = positions((1, count))
    packed = halo_ref[9 * 64 : 9 * 64 + 16, :].astype(F32)
    other = from_azim(packed[0:3] + packed[3:6], iy)
    own = metric_ref[...]
    lows, highs = iy == 0, iy == EY - 1
    rows = []
    for item in metric_classes(own[0:1], other[0:1], EZ, lows, highs):
        rows += radial_classes(item, iz)
    rows += radial_classes(own[1:2], iz)
    rows += metric_classes(own[2:3], other[2:3], EZ, lows, highs)
    rows += radial_classes(other[1:2], iz)
    table = jnp.concatenate(rows + [jnp.zeros((24 - len(rows), count), F32)], axis=0)
    table_ref[...] = table
    high = table.astype(BF).astype(F32)
    spare = jnp.zeros((SEAM - 64, count), F32)
    blocks.append(jnp.concatenate(extra + [high, table - high, spare], axis=0))

    ix = positions((SEAM, count))[0]
    even = par_ref[0] == 0
    half = len(blocks) // 2
    for i in range(half):
        one, two = blocks[i], blocks[half + i]
        down = jnp.where(ix == 0, one, roll(two, layer))
        up = jnp.where(ix == 0, roll(one, layer), two)
        rows = slice(i * SEAM, (i + 1) * SEAM)
        a_ref[rows, :] = jnp.where(even, up, down).astype(BF)
        b_ref[rows, :] = jnp.where(even, down, up).astype(BF)


def signed(one, two, parity):
    return one + two if parity == 0 else one - two


def radial_fold(rows, iz, parity):
    last = NI - 1
    low = jnp.where(iz > 0, roll(rows[last], 1) - rows[0], 0.0)
    high = jnp.where(iz < EZ - 1, roll(rows[0], -1) - rows[last], 0.0)
    return [signed(rows[c], rows[last - c], parity) for c in range(HI)] + [
        0.5 * signed(low, high, parity)
    ]


def azim_fold(plane, parity):
    return [
        signed(
            plane[b if b < HI else NI], plane[NI - 1 - b if b < HI else NI + 1], parity
        )
        for b in range(HO)
    ]


def third_kernel(ext_ref, const_ref, gs_ref, tmp_ref, xs_ref):
    count = ext_ref.shape[-1]
    width = HO * HI
    iz = positions((width, count))[2]
    zeros = jnp.zeros((HI, count), F32)
    for f in range(7):
        pair, side = PLACE[f]
        lanes = slice(side * count, (side + 1) * count)
        values = ext_ref[f]
        for pa in range(2):
            mixed = [signed(values[a], values[NI - 1 - a], pa) for a in range(HI)]
            for pb in range(2):
                at = f % 2 * 4 + pa * 2 + pb
                for a in range(HI):
                    for b, item in enumerate(azim_fold(mixed[a], pb)):
                        row = (a * HO + b) * NI
                        tmp_ref[at, row : row + NI, :] = item
                main = [tmp_ref[at, pl.ds(c, width, stride=NI), :] for c in range(NI)]
                for pc in range(2):
                    rows = []
                    for item in radial_fold(main, iz, pc):
                        rows += [item, zeros]
                    rows.append(jnp.zeros((8, count), F32))
                    operand = jnp.concatenate(rows, axis=0).astype(BF)
                    xs_ref[pair, pa * 4 + pb * 2 + pc, :, lanes] = operand

    def refine(sector, carry):
        for pair in range(PAIRS):
            width = 2 * count if pair < PAIRS - 1 else count
            source = xs_ref[pair, sector, :, 0:width]
            source = jnp.concatenate([source, source], axis=0)
            for q in range(0 if pair < PAIRS - 1 else 1, 4):
                rows = pl.ds(sector * 4 * ROWS + q * ROWS, ROWS)
                gs_ref[pair, q, sector ^ FLIPS[q], :, 0:width] = dot(const_ref[rows, :], source)
        return carry

    lax.fori_loop(0, 8, refine, 0)


def fourth_kernel(
    ends_value,
    weights,
    par_ref,
    inv_ref,
    gs_ref,
    ext_ref,
    ends_ref,
    table_ref,
    metric_ref,
    slots_ref,
    ra_ref,
    rb_ref,
    const_ref,
    out_ref,
    tmp_ref,
    along_ref,
    edge_ref,
    vort_ref,
    linear_ref,
    factor_ref,
    normal_x_ref,
    normal_y_ref,
    quad_ref,
    xt_ref,
):
    count = ext_ref.shape[-1]
    layer = EY * EZ
    even = par_ref[0] == 0
    ix = positions((SEAM, count))[0]
    end_low, end_high = ends_value
    seam_at = 8 * 4 * ROWS
    second_at = seam_at + 4 * SEAM_ROWS
    lift_x_at = second_at + 6 * ROWS
    lift_y_at = lift_x_at + ROWS

    halves = []
    for i in range(5):
        rows = slice(i * SEAM, (i + 1) * SEAM)
        one = ra_ref[rows, :].astype(F32)
        two = rb_ref[rows, :].astype(F32)
        down = jnp.where(even, two, one)
        up = jnp.where(even, one, two)
        halves.append(
            (
                jnp.where(ix == 0, down, roll(up, layer)),
                jnp.where(ix == 0, roll(down, layer), up),
            )
        )
    blocks = [item[0] for item in halves] + [item[1] for item in halves]

    ix3 = positions((1, 1, count))[0]
    iz8 = positions((NI, count))[2]

    def stream_added(first, last, halo):
        lane = positions((1,) * (first.ndim - 1) + (count,))[0]
        low = 0.5 * (jnp.where(lane == 0, halo, roll(last, layer)) - first)
        high = 0.5 * (jnp.where(lane == 0, roll(first, -layer), halo) - last)
        return low, high

    seam = {}
    tmp_ref[...] = jnp.zeros(tmp_ref.shape, F32)
    for f in range(7):
        pair, side = PLACE[f]
        lanes = slice(side * count, (side + 1) * count)
        halo = blocks[f].reshape(EXT, NI, count)
        first, last = ext_ref[f, 0], ext_ref[f, NI - 1]
        low, high = stream_added(first, last, halo)
        if f in (4, 5):
            seam[f] = seam_rows(jnp.where(ix3 == 0, first + low, last + high))
        for pa in range(2):
            mixed = signed(low, high, pa)
            for pb in range(2):
                at = f % 2 * 4 + pa * 2 + pb
                for b, item in enumerate(azim_fold(mixed, pb)):
                    tmp_ref[at, b * NI : (b + 1) * NI, :] = item
                main = [tmp_ref[at, pl.ds(c, NI, stride=NI), :] for c in range(NI)]
                for pc in range(2):
                    rows = radial_fold(main, iz8, pc)
                    rows.append(jnp.zeros((NI, count), F32))
                    operand = jnp.concatenate(rows, axis=0).astype(BF)
                    xt_ref[pair, pa * 4 + pb * 2 + pc, :, lanes] = operand

    def refine_seam(pa, pb, pc):
        sector = pa * 4 + pb * 2 + pc
        at = seam_at + (sector // 2) * SEAM_ROWS
        matrix = const_ref[at : at + SEAM_ROWS, pc * ROWS : pc * ROWS + 2 * 48]
        for pair in range(PAIRS):
            width = 2 * count if pair < PAIRS - 1 else count
            source = xt_ref[pair, sector, :, 0:width]
            added = dot(matrix, jnp.concatenate([source, source], axis=0))
            target = sector ^ 4
            along_ref[pair, target, :, 0:width] = (
                gs_ref[pair, 1, target, :, 0:width] + added[0:ROWS]
            )
            for q, slot in ((0, 0), (2, 1), (3, 2)):
                if q or pair < PAIRS - 1:
                    target = sector ^ FLIPS[q]
                    edge_ref[pair, slot, target, :, 0:width] = (
                        gs_ref[pair, q, target, 0:32, 0:width]
                        + added[ROWS + 32 * slot : ROWS + 32 * slot + 32]
                    )

    for sector in range(8):
        refine_seam(sector // 4, sector // 2 % 2, sector % 2)

    row = lax.broadcasted_iota(jnp.int32, (ROWS, count), 0)
    a_edge = row < HO * HO
    b_edge = lax.rem(row, HO * HO) < HO
    c_edge = lax.rem(row, HO) == 0

    def weight_of(index):
        result = jnp.full((ROWS, count), weights[0], F32)
        for i in range(1, HO):
            result = jnp.where(index == i, weights[i], result)
        return result

    a_pos = lax.div(row, HO * HO)
    quad = weight_of(a_pos) * weight_of(lax.rem(lax.div(row, HO), HO)) * weight_of(lax.rem(row, HO))
    quad_ref[...] = jnp.where(row < HO**3, quad, 0.0)

    table = table_ref[...]
    packed = blocks[9]
    theirs = packed[16:40] + packed[40:64]
    lane_ix = positions((24, count))[0]
    at_low = 0.5 * (table + jnp.where(lane_ix == 0, theirs, roll(table, layer)))
    at_high = 0.5 * (table + jnp.where(lane_ix == 0, roll(table, -layer), theirs))

    def line_of(source, at):
        return source[at : at + 1]

    def by_radius(source, at, side):
        return jnp.where(c_edge, line_of(source, at + 1 + side), line_of(source, at))

    for one in range(2):
        edge = at_low if one == 0 else at_high
        for two in range(2):
            at = one * 2 + two
            factor_ref[at] = jnp.where(
                b_edge, by_radius(table, 3 + 3 * one, two), by_radius(table, 0, two)
            )
            factor_ref[4 + at] = jnp.where(
                a_edge, by_radius(edge, 9, two), by_radius(table, 9, two)
            )
            inside = jnp.where(b_edge, line_of(table, 13 + two), line_of(table, 12))
            outside = jnp.where(b_edge, line_of(edge, 13 + two), line_of(edge, 12))
            factor_ref[8 + at] = jnp.where(a_edge, outside, inside)

    def with_added(parts):
        halves = []
        for part in parts:
            stacked = part.reshape(EXT, NI, count)
            halves.append(jnp.concatenate([part, seam_rows(radial_added(stacked))], axis=0))
        return jnp.concatenate(halves, axis=1).astype(BF)

    def lift(at, rows, operand):
        return dot(const_ref[at : at + rows, 0 : 2 * SEAM], operand)

    stream = []
    for i in range(2):
        shared = jnp.where(ix == 0, end_high, end_low) * seam[4 + i]
        stream.append(blocks[7 + i] + shared)
    lifted = lift(lift_x_at, ROWS, with_added(stream))
    for one in range(2):
        for two in range(2):
            at = one * 2 + two
            scale = jnp.where(
                b_edge, by_radius(theirs, 3 + 3 * one, two), by_radius(theirs, 0, two)
            )[0:32]
            for i in range(2):
                part = lifted[at * 32 : at * 32 + 32, i * count : (i + 1) * count]
                normal_x_ref[i, at] = part * scale

    iy3 = positions((1, 1, count))[1]
    iy2 = iy3[0]
    azim = []
    for i, f in enumerate((3, 5)):
        factor = jnp.where(iy3 == 0, end_high, end_low)
        values = ext_ref[f]
        halo = blocks[f].reshape(EXT, NI, count)
        near = jnp.where(
            iy3 == 0, values[:, 0] + values[:, NI], values[:, NI - 1] + values[:, NI + 1]
        )
        own = ends_ref[i] + factor * near
        near = jnp.where(iy2 == 0, halo[0] + halo[NI], halo[NI - 1] + halo[NI + 1])
        other = blocks[9][8 * i : 8 * i + 8] + factor[0] * near
        low, high = stream_added(own[0], own[NI - 1], other)
        azim.append(jnp.concatenate([rows2(own), low, high], axis=0))
    lifted = lift(lift_y_at, 4 * ROWS, with_added(azim))
    for one in range(2):
        edge = at_low if one == 0 else at_high
        for two in range(2):
            at = one * 2 + two
            scale = jnp.where(a_edge, by_radius(edge, 15, two), by_radius(table, 15, two))
            for i in range(2):
                part = lifted[at * ROWS : (at + 1) * ROWS, i * count : (i + 1) * count]
                normal_y_ref[i, at] = part * scale

    def parts_of(f, q, at, edge):
        pair, side = PLACE[f]
        lanes = slice(side * count, (side + 1) * count)
        if q == 1:
            return [along_ref[pair, sector, at, lanes] for sector in range(8)]
        if edge:
            slot = (0, None, 1, 2)[q]
            return [edge_ref[pair, slot, sector, at, lanes] for sector in range(8)]
        return [gs_ref[pair, q, sector, at, lanes] for sector in range(8)]

    chunk = 16

    def vorticity(at, start, edge):
        shape = (chunk, count)
        lane_ix, lane_iy, lane_iz = positions(shape)
        rows = lax.broadcasted_iota(jnp.int32, shape, 0) + start
        on_a = rows < HO * HO
        on_b = lax.rem(rows, HO * HO) < HO
        on_c = lax.rem(rows, HO) == 0

        def nodal(f, q, factor):
            g = unfold(parts_of(f, q, at, edge))
            return [g[s] * factor_ref[factor(s), at, :] for s in range(8)]

        def along_x(i, f):
            g = nodal(f, 1, lambda s: s % 4)
            if edge:
                for two in range(4):
                    low, high = g[two], g[4 + two]
                    normal = normal_x_ref[i, two, at, :]
                    near = lane_ix == 0
                    first = 0.5 * (low + jnp.where(near, normal, roll(high, layer)))
                    last = 0.5 * (high + jnp.where(near, roll(low, -layer), normal))
                    g[two] = jnp.where(on_a, first, low)
                    g[4 + two] = jnp.where(on_a, last, high)
            return g

        def along_y(i, f):
            g = nodal(f, 2, lambda s: 4 + s // 4 * 2 + s % 2)
            for two in range(4):
                here = two // 2 * 4 + two % 2
                low, high = g[here], g[here + 2]
                normal = normal_y_ref[i, two, at, :]
                first = 0.5 * (low + jnp.where(lane_iy == 0, normal, roll(high, EZ)))
                last = 0.5 * (high + jnp.where(lane_iy == EY - 1, normal, roll(low, -EZ)))
                g[here] = jnp.where(on_b, first, low)
                g[here + 2] = jnp.where(on_b, last, high)
            return g

        def along_z(f):
            g = nodal(f, 3, lambda s: 8 + s // 2)
            lower = on_c & (lane_iz > 0)
            upper = on_c & (lane_iz < EZ - 1)
            for two in range(4):
                low, high = g[2 * two], g[2 * two + 1]
                g[2 * two] = jnp.where(lower, 0.5 * (low + roll(high, 1)), low)
                g[2 * two + 1] = jnp.where(upper, 0.5 * (high + roll(low, -1)), high)
            return g

        pairs = (
            (lambda: along_y(1, 5), lambda: along_z(4)),
            (lambda: along_z(3), lambda: along_x(1, 5)),
            (lambda: along_x(0, 4), lambda: along_y(0, 3)),
        )
        for i, (plus, minus) in enumerate(pairs):
            one, two = plus(), minus()
            folded = unfold([0.125 * (one[s] - two[s]) for s in range(8)])
            for sector in range(8):
                vort_ref[i, sector, at, :] = folded[sector].astype(BF)

    for step in range(2):
        vorticity(slice(step * chunk, (step + 1) * chunk), step * chunk, True)

    def vorticity_step(step, carry):
        start = pl.multiple_of(step * chunk, chunk)
        vorticity(pl.ds(start, chunk), start, False)
        return carry

    lax.fori_loop(2, ROWS // chunk, vorticity_step, 0)

    metric = [metric_ref[i : i + 1] for i in range(3)]
    inv = inv_ref[0]
    scaled = [inv * metric[i] for i in range(3)]
    taken = ((1, 2), (2, 0), (0, 1))
    terms = (((1, 0), (2, 1)), ((2, 0), (0, 1)), ((0, 0), (1, 1)))
    for target in range(8):
        slope = []
        for axis in range(3):
            flip = FLIPS[1 + axis]
            sector = target ^ flip
            source = jnp.concatenate([vort_ref[i, sector] for i in taken[axis]], axis=1)
            source = jnp.concatenate([source, source], axis=0)
            at = second_at + (2 * axis + (1 if sector & flip else 0)) * ROWS
            slope.append(dot(const_ref[at : at + ROWS, :], source))
        for i in range(3):
            (one, half), (two, other) = terms[i]
            plus = scaled[one] * slope[one][:, half * count : (half + 1) * count]
            minus = scaled[two] * slope[two][:, other * count : (other + 1) * count]
            if i == 0:
                linear_ref[i, target] = along_ref[3, target, :, 0:count] * metric[0] + (plus - minus)
            else:
                near = edge_ref[3, i, target, :, 0:count] * metric[i]
                far = gs_ref[3, 1 + i, target, 32:, 0:count] * metric[i]
                linear_ref[i, target, 0:32, :] = near + (plus - minus)[0:32]
                linear_ref[i, target, 32:, :] = far + (plus - minus)[32:]

    def body(edge, step, total):
        at = pl.ds(pl.multiple_of(step * 8, 8), 8)
        for side in range(2):
            total = total + quad_ref[at, :] * energy_of(at, side, edge)
        return total

    def energy_of(at, side, edge):
        def unfold_half(parts):
            return unfold4([signed(parts[s], parts[4 + s], side) for s in range(4)])

        def part(f, q):
            return unfold_half(parts_of(f, q, at, edge))

        base = [[item * metric[j] for item in part(j, 0)] for j in range(3)]
        dual = [part(3 + j, 0) for j in range(3)]
        energy = spread = None
        for i in range(3):
            total = unfold_half([linear_ref[i, s, at, :] for s in range(8)])
            for j in range(3):
                slope = part(3 + i, 1 + j)
                total = [total[s] - base[j][s] * slope[s] for s in range(4)]
                if i == j:
                    more = [slope[s] * metric[i] for s in range(4)]
                    spread = more if i == 0 else [spread[s] + more[s] for s in range(4)]
            inner = None
            for j in range(3):
                slope = part(j, 1 + i)
                more = [dual[j][s] * slope[s] for s in range(4)]
                inner = more if j == 0 else [inner[s] + more[s] for s in range(4)]
            total = [total[s] + metric[i] * inner[s] for s in range(4)]
            more = [item * item for item in total]
            energy = more if i == 0 else [energy[s] + more[s] for s in range(4)]
        energy = [energy[s] + spread[s] * spread[s] for s in range(4)]
        return (energy[0] + energy[1]) + (energy[2] + energy[3])

    total = jnp.zeros((8, count), F32)
    total = lax.fori_loop(0, 4, functools.partial(body, True), total)
    total = lax.fori_loop(4, ROWS // 8, functools.partial(body, False), total)
    weighted = jnp.sum(total, axis=0, keepdims=True)
    result = jnp.sqrt(weighted / 8.0) / float(ORDER_OUT**2)
    high, mid, low = split3(result)
    stacked = jnp.concatenate(
        [high.astype(F32), mid.astype(F32), low.astype(F32), jnp.zeros((13, count), F32)], axis=0
    )
    moved = dot(stacked.astype(BF), slots_ref[...])
    out_ref[...] = moved[0:1] + moved[1:2] + moved[2:3]


def unfold4(parts):
    plus0, minus0 = parts[0] + parts[1], parts[0] - parts[1]
    plus1, minus1 = parts[2] + parts[3], parts[2] - parts[3]
    return [plus0 + plus1, minus0 + minus1, plus0 - plus1, minus0 - minus1]


def unfold(parts):
    plus = unfold4([parts[s] + parts[4 + s] for s in range(4)])
    minus = unfold4([parts[s] - parts[4 + s] for s in range(4)])
    return plus + minus


MIB = 1024 * 1024


def per_device(fields, elem_map, metric, inv_reynolds):
    const, weights, (line, ends_value) = tables()
    count = fields.shape[-1]
    vmem = pl.BlockSpec(memory_space=pltpu.VMEM)
    smem = pl.BlockSpec(memory_space=pltpu.SMEM)

    def params(mib):
        return pltpu.CompilerParams(vmem_limit_bytes=mib * MIB)

    def struct(shape, dtype=F32):
        return jax.ShapeDtypeStruct(shape, dtype)

    small = jnp.concatenate([elem_map.astype(F32), metric], axis=0)
    slots, local_metric, message = pl.pallas_call(
        functools.partial(first_kernel, line),
        out_shape=(
            struct((count, count), BF),
            struct((8, count)),
            struct((9 * 64 + 16, count), BF),
        ),
        in_specs=[vmem] * 2,
        out_specs=(vmem,) * 3,
        compiler_params=params(6),
        name="first",
    )(fields, small)
    coarse = pl.pallas_call(
        own_kernel,
        out_shape=struct((7, NI, NI, NI, count)),
        in_specs=[vmem] * 2,
        out_specs=vmem,
        compiler_params=params(6),
        cost_estimate=pl.CostEstimate(
            flops=2 * fields.size * count, bytes_accessed=3 * 10**6, transcendentals=0
        ),
        name="own",
    )(fields, slots)

    azim = lax.axis_size("azim")
    if azim == 2:
        halo = lax.ppermute(message, "azim", [(0, 1), (1, 0)])
    else:
        ahead = lax.ppermute(message, "azim", [(i, (i + 1) % azim) for i in range(azim)])
        behind = lax.ppermute(message, "azim", [((i + 1) % azim, i) for i in range(azim)])
        iy = (jnp.arange(count) // EZ) % EY
        halo = jnp.where(iy >= EY // 2, ahead, behind)

    place = lax.axis_index("strm")
    streams = lax.axis_size("strm")
    parity = lax.rem(place, 2).astype(jnp.int32).reshape(1)
    if streams % 2:
        parity = jnp.zeros((1,), jnp.int32)
    extended, ends, table, to_a, to_b = pl.pallas_call(
        functools.partial(second_kernel, line),
        out_shape=(
            struct((7, NI, EXT, NI, count)),
            struct((2, NI, NI, count)),
            struct((24, count)),
            struct((5 * SEAM, count), BF),
            struct((5 * SEAM, count), BF),
        ),
        in_specs=[smem] + [vmem] * 3,
        out_specs=(vmem,) * 5,
        compiler_params=params(12),
        name="second",
    )(parity, coarse, local_metric, halo)

    if streams % 2 == 0:
        near = [(i, i ^ 1) for i in range(streams)]
        far = []
        for i in range(1, streams, 2):
            far += [(i, (i + 1) % streams), ((i + 1) % streams, i)]
        got_a = lax.ppermute(to_a, "strm", near)
        got_b = lax.ppermute(to_b, "strm", far)
    else:
        got_b = lax.ppermute(to_a, "strm", [(i, (i + 1) % streams) for i in range(streams)])
        got_a = lax.ppermute(to_b, "strm", [((i + 1) % streams, i) for i in range(streams)])

    table_of = jnp.asarray(const)
    raw = pl.pallas_call(
        third_kernel,
        out_shape=struct((PAIRS, 4, 8, ROWS, 2 * count)),
        in_specs=[vmem] * 2,
        out_specs=vmem,
        scratch_shapes=[
            pltpu.VMEM((8, HO * HI * NI, count), F32),
            pltpu.VMEM((PAIRS, 8, ROWS, 2 * count), BF),
        ],
        compiler_params=params(6),
        cost_estimate=pl.CostEstimate(
            flops=4 * 10**9, bytes_accessed=20 * 10**6, transcendentals=0
        ),
        name="third",
    )(extended, table_of)

    result = pl.pallas_call(
        functools.partial(fourth_kernel, ends_value, weights),
        out_shape=struct((1, count)),
        in_specs=[smem] * 2 + [vmem] * 9,
        out_specs=vmem,
        scratch_shapes=[
            pltpu.VMEM((8, NI * NI, count), F32),
            pltpu.VMEM((PAIRS, 8, ROWS, 2 * count), F32),
            pltpu.VMEM((PAIRS, 3, 8, 32, 2 * count), F32),
            pltpu.VMEM((3, 8, ROWS, count), BF),
            pltpu.VMEM((3, 8, ROWS, count), F32),
            pltpu.VMEM((12, ROWS, count), F32),
            pltpu.VMEM((2, 4, 32, count), F32),
            pltpu.VMEM((2, 4, ROWS, count), F32),
            pltpu.VMEM((ROWS, count), F32),
            pltpu.VMEM((PAIRS, 8, 48, 2 * count), BF),
        ],
        compiler_params=params(20),
        name="fourth",
    )(
        parity,
        inv_reynolds,
        raw,
        extended,
        ends,
        table,
        local_metric,
        slots,
        got_a,
        got_b,
        table_of,
    )
    return result.reshape(count)


def solution(mesh):
    return jax.shard_map(
        per_device,
        mesh=mesh,
        in_specs=(
            P(None, None, ("grp", "strm", "azim")),
            P(("strm", "azim"), None),
            P(None, ("strm", "azim")),
            P("grp"),
        ),
        out_specs=P(("grp", "strm", "azim")),
        check_vma=False,
    )
```

```python
import functools

import jax
import jax.numpy as jnp
import numpy as np
from jax import lax
from jax.experimental import pallas as pl
from jax.experimental.pallas import tpu as pltpu
from jax.sharding import PartitionSpec as P

ORDER_IN = 7
ORDER_OUT = 9
EY = 8
EZ = 8
NI = ORDER_IN + 1
NO = ORDER_OUT + 1
HI = NI // 2
HO = NO // 2
ROWS = 128
SEAM_ROWS = ROWS + 3 * 32
EXT = NI + 2
SEAM = EXT * NI
BF = jnp.bfloat16
F32 = jnp.float32
PLACE = {3: (0, 0), 4: (0, 1), 5: (1, 0), 0: (1, 1), 1: (2, 0), 2: (2, 1), 6: (3, 0)}
PAIRS = 4
FLIPS = (0, 4, 2, 1)


def gll_table(extent):
    degree = extent - 1
    points = np.cos(np.pi * np.arange(extent) / degree)
    legendre = np.zeros((extent, extent))

    def fill():
        legendre[:, 0] = 1.0
        legendre[:, 1] = points
        for level in range(2, extent):
            legendre[:, level] = (
                (2 * level - 1) * points * legendre[:, level - 1]
                - (level - 1) * legendre[:, level - 2]
            ) / level

    for sweep in range(100):
        fill()
        points = points - (points * legendre[:, degree] - legendre[:, degree - 1]) / (
            extent * legendre[:, degree]
        )
    fill()
    weights = 2.0 / (degree * extent * legendre[:, degree] ** 2)
    return (points[::-1].copy(), weights[::-1].copy())


def lagrange_matrix(source, target):
    result = np.ones((len(target), len(source)))
    for column in range(len(source)):
        for partner in range(len(source)):
            if partner != column:
                result[:, column] *= (target - source[partner]) / (source[column] - source[partner])
    return result


def derivative_matrix(points):
    extent = len(points)
    identity = np.eye(extent)
    spacing = points[:, None] - points[None, :] + identity
    barycen = 1.0 / np.prod(spacing, axis=1)
    matrix = barycen[None, :] / barycen[:, None] / spacing * (1.0 - identity)
    return matrix - identity * matrix.sum(axis=1)[:, None]


def bf16_parts(matrix):
    high = matrix.astype(jnp.bfloat16)
    low = (matrix - high.astype(np.float64)).astype(jnp.bfloat16)
    return high, low


def pad_rows(matrix, rows):
    return np.concatenate([matrix, np.zeros((rows - matrix.shape[0],) + matrix.shape[1:])])


def two_terms(matrix):
    return np.concatenate(bf16_parts(matrix), axis=-1)


@functools.cache
def tables():
    coarse, unused = gll_table(NI)
    fine, weights = gll_table(NO)
    interp = lagrange_matrix(coarse, fine)
    slopes = derivative_matrix(fine)
    ends = np.eye(NO)[:, [0, NO - 1]]
    value = np.concatenate([interp, ends], axis=1)
    both = slopes @ value

    def folded(matrix, parity):
        sign = 1.0 - 2.0 * parity
        if matrix.shape[1] == EXT and matrix is not slopes:
            left = matrix[:HO, [0, 1, 2, 3, 8]]
            right = matrix[:HO, [7, 6, 5, 4, 9]]
        else:
            left = matrix[:HO, :HO]
            right = matrix[:HO, ::-1][:, :HO]
        return left + sign * right

    refine, seams = [], []
    for sector in range(8):
        pa, pb, pc = sector // 4, sector // 2 % 2, sector % 2
        blocks, ends_of = [], []
        for ta, tb, tc in (
            (value, value, value),
            (both, value, value),
            (value, both, value),
            (value, value, both),
        ):
            block = 0.125 * np.einsum(
                "ap,bq,cr->abcrpq", folded(ta, pa), folded(tb, pb), folded(tc, pc)
            ).reshape(HO**3, HO, HO, HO)
            own = np.zeros((HO**3, HO, 24))
            own[:, :, : HO * HI] = block[:, :, :HI].reshape(HO**3, HO, HO * HI)
            own = np.pad(own.reshape(HO**3, -1), ((0, 0), (0, ROWS - 24 * HO)))
            blocks.append(pad_rows(own, ROWS))
            added = np.zeros((HO**3, 48))
            added[:, : 8 * HO] = np.pad(block[:, :, HI], ((0, 0), (0, 0), (0, 3))).reshape(HO**3, -1)
            ends_of.append(added)
        refine.append(two_terms(np.concatenate(blocks)))
        rows = [pad_rows(ends_of[1], ROWS)]
        rows += [pad_rows(ends_of[q][: HO * HO], 32) for q in (0, 2, 3)]
        seams.append(np.pad(two_terms(np.concatenate(rows)), ((0, 0), (0, ROWS - 96))))
    refine = np.stack(refine)
    seams = [np.concatenate(seams[2 * i : 2 * i + 2], axis=1) for i in range(4)]

    second = []
    eye = np.eye(HO)
    for axis in range(3):
        for parity in range(2):
            factors = [eye, eye, eye]
            factors[axis] = folded(slopes, parity)
            block = np.kron(np.kron(factors[0], factors[1]), factors[2])
            edge = ROWS - HO**3
            second.append(two_terms(np.pad(block, ((0, edge), (0, edge)))))
    second = np.stack(second)

    def half(side):
        return value[:HO] if side == 0 else value[::-1][:HO]

    lift_x, lift_y = [], []
    for side in range(2):
        for radial in range(2):
            plain = np.zeros((HO, EXT, HO, NI))
            added = np.zeros((HO, EXT, HO, NI))
            plain[...] = np.einsum("ap,cr->apcr", half(side), half(radial)[:, :NI])
            added[..., 0] = np.einsum("ap,c->apc", half(side), half(radial)[:, NI])
            added[..., NI - 1] = np.einsum("ap,c->apc", half(side), half(radial)[:, NI + 1])
            face = np.stack([plain, added]).transpose(1, 3, 0, 2, 4).reshape(HO, HO, 2 * SEAM)
            lift_x.append(pad_rows(face.reshape(HO * HO, -1), 32))
            spread = np.zeros((HO, HO, HO, 2 * SEAM))
            spread[:, 0] = face
            lift_y.append(pad_rows(spread.reshape(HO**3, -1), ROWS))

    def one_term(parts):
        matrix = np.concatenate(parts)
        return np.pad(matrix, ((0, 0), (0, 2 * ROWS - matrix.shape[1]))).astype(jnp.bfloat16)

    refine = refine.reshape(-1, 2 * ROWS)
    const = np.concatenate(
        seams + [second.reshape(-1, 2 * ROWS), one_term(lift_x), one_term(lift_y)]
    )
    half_weights = [float(v) for v in weights[:HO]]
    line = []
    for end, far in ((0, NO - 1), (NO - 1, 0)):
        weights_in = slopes[end].copy()
        weights_in[[0, NO - 1]] = 0.0
        line.append(([float(v) for v in weights_in @ interp], float(slopes[end, far])))
    ends = (float(slopes[0, 0]), float(slopes[NO - 1, NO - 1]))
    return refine, const, half_weights, (line, ends)


def dot(a, b, contract_last=False):
    dims = (((1,), (1 if contract_last else 0,)), ((), ()))
    return lax.dot_general(a, b, dims, preferred_element_type=F32)


def is_even(even_ring):
    return lax.rem(lax.axis_index("strm"), 2) == 0 if even_ring else True


def rows3(x):
    return x.reshape(NI, NI, x.shape[-1])


def seam_rows(x):
    return x.reshape(SEAM, x.shape[-1])


def rows2(x):
    return x.reshape(NI * NI, x.shape[-1])


def roll(x, shift):
    count = x.shape[-1]
    return pltpu.roll(x, shift % count, x.ndim - 1)


def positions(shape):
    lane = lax.broadcasted_iota(jnp.int32, shape, len(shape) - 1)
    return lax.div(lane, EY * EZ), lax.rem(lax.div(lane, EZ), EY), lax.rem(lane, EZ)


def split3(x):
    high = x.astype(BF)
    rest = x - high.astype(F32)
    mid = rest.astype(BF)
    low = (rest - mid.astype(F32)).astype(BF)
    return high, mid, low


def radial_added(x):
    axis = x.ndim - 2
    shape = (1,) * axis + x.shape[-2:]
    node = lax.broadcasted_iota(jnp.int32, shape, axis)
    iz = positions(shape)[2]
    last = x.shape[-2] - 1
    before = pltpu.roll(roll(x, 1), 1, axis)
    after = pltpu.roll(roll(x, -1), last, axis)
    low = (node == 0) & (iz > 0)
    high = (node == last) & (iz < EZ - 1)
    other = jnp.where(low, before, jnp.where(high, after, x))
    return 0.5 * (other - x)


def end_lines(line, planes, step):
    (near, near_far), (high, high_far) = line
    first, last = planes[0], planes[-1]
    one = near_far * 0.5 * (last + roll(first, -step))
    two = high_far * 0.5 * (first + roll(last, step))
    for i, plane in enumerate(planes):
        one = one + near[i] * plane
        two = two + high[i] * plane
    return one, two


def chunks(source, target, sem, count=8):
    step = source.shape[0] // count
    return [
        pltpu.make_async_copy(
            source.at[i * step : (i + 1) * step], target.at[i * step : (i + 1) * step], sem.at[i]
        )
        for i in range(count)
    ]


def first_kernel(
    line,
    fields_hbm,
    emap_hbm,
    metric_hbm,
    table_hbm,
    slots_ref,
    metric_out,
    msg_ref,
    coarse_ref,
    table_ref,
    fields,
    emap,
    metric,
    sem,
):
    count = fields.shape[-1]
    order = (3, 5, 4, 0, 1, 2, 6)
    small = [
        pltpu.make_async_copy(emap_hbm, emap, sem.at[7]),
        pltpu.make_async_copy(metric_hbm, metric, sem.at[8]),
    ]
    large = [pltpu.make_async_copy(fields_hbm.at[f], fields.at[f], sem.at[f]) for f in order]
    tables_copies = chunks(table_hbm, table_ref, sem.at[pl.ds(9, 8)])
    for copy in small + large + tables_copies:
        copy.start()
    for copy in small:
        copy.wait()
    local = lax.broadcasted_iota(jnp.int32, (count, count), 0)
    slots = (local == emap[...]).astype(F32).astype(BF)
    slots_ref[...] = slots
    high, mid, low = split3(metric[...])
    pad = jnp.zeros((7, count), F32)
    stacked = jnp.concatenate([high.astype(F32), mid.astype(F32), low.astype(F32), pad], axis=0)
    moved = dot(stacked.astype(BF), slots, True)
    local = moved[0:3] + moved[3:6] + moved[6:9]
    metric_out[...] = jnp.concatenate([local, jnp.zeros((5, count), F32)], axis=0)
    high = local.astype(BF).astype(F32)
    tail = jnp.concatenate([high, local - high, jnp.zeros((10, count), F32)], axis=0)
    msg_ref[9 * 64 : 9 * 64 + 16, :] = tail.astype(BF)
    iy = positions((1, 1, count))[1]
    for f, copy in zip(order, large):
        copy.wait()
        values = dot(fields[f], slots, True).reshape(NI, NI, NI, count)
        coarse_ref[f] = values
        face = jnp.where(iy == 0, values[:, 0], values[:, NI - 1])
        msg_ref[f * 64 : f * 64 + 64, :] = rows2(face).astype(BF)
        if f in (3, 5):
            low, high = end_lines(line, [values[:, b] for b in range(NI)], EZ)
            at = (7 + (f == 5)) * 64
            msg_ref[at : at + 64, :] = rows2(jnp.where(iy == 0, low, high)).astype(BF)
    for copy in tables_copies:
        copy.wait()


def from_azim(x, iy):
    gap = (EY - 1) * EZ
    return jnp.where(iy == 0, roll(x, -gap), roll(x, gap))


def metric_classes(x, halo, shift, at_low, at_high):
    low = 0.5 * (x + jnp.where(at_low, halo, roll(x, shift)))
    high = 0.5 * (x + jnp.where(at_high, halo, roll(x, -shift)))
    return [x, low, high]


def radial_classes(x, iz):
    low = jnp.where(iz > 0, 0.5 * (x + roll(x, 1)), x)
    high = jnp.where(iz < EZ - 1, 0.5 * (x + roll(x, -1)), x)
    return [x, low, high]


def second_kernel(
    line, even_ring, coarse_ref, metric_ref, halo_ref, ext_ref, ends_ref, table_ref, a_ref, b_ref
):
    count = coarse_ref.shape[-1]
    layer = EY * EZ
    ix, iy, iz = positions((1, 1, count))
    blocks = []
    lines = []
    for f in range(7):
        values = coarse_ref[f]
        first, last = values[:, 0], values[:, NI - 1]
        halo = from_azim(rows3(halo_ref[f * 64 : f * 64 + 64, :].astype(F32)), iy)
        low = 0.5 * (jnp.where(iy == 0, halo, roll(last, EZ)) - first)
        high = 0.5 * (jnp.where(iy == EY - 1, halo, roll(first, -EZ)) - last)
        values = jnp.concatenate([values, low[:, None], high[:, None]], axis=1)
        ext_ref[f] = values
        blocks.append(seam_rows(jnp.where(ix == 0, values[0], values[NI - 1])))
        if f in (4, 5):
            low, high = end_lines(line, [values[a] for a in range(NI)], layer)
            lines.append(seam_rows(jnp.where(ix == 0, low, high)))
    blocks += lines
    extra = []
    for i in range(2):
        ends = from_azim(rows3(halo_ref[(7 + i) * 64 : (8 + i) * 64, :].astype(F32)), iy)
        ends_ref[i] = ends
        extra.append(jnp.where(ix[0] == 0, ends[0], ends[NI - 1]))

    ix, iy, iz = positions((1, count))
    packed = halo_ref[9 * 64 : 9 * 64 + 16, :].astype(F32)
    other = from_azim(packed[0:3] + packed[3:6], iy)
    own = metric_ref[...]
    lows, highs = iy == 0, iy == EY - 1
    rows = []
    for item in metric_classes(own[0:1], other[0:1], EZ, lows, highs):
        rows += radial_classes(item, iz)
    rows += radial_classes(own[1:2], iz)
    rows += metric_classes(own[2:3], other[2:3], EZ, lows, highs)
    rows += radial_classes(other[1:2], iz)
    table = jnp.concatenate(rows + [jnp.zeros((24 - len(rows), count), F32)], axis=0)
    table_ref[...] = table
    high = table.astype(BF).astype(F32)
    spare = jnp.zeros((SEAM - 64, count), F32)
    blocks.append(jnp.concatenate(extra + [high, table - high, spare], axis=0))

    ix = positions((SEAM, count))[0]
    even = is_even(even_ring)
    half = len(blocks) // 2
    for i in range(half):
        one, two = blocks[i], blocks[half + i]
        down = jnp.where(ix == 0, one, roll(two, layer))
        up = jnp.where(ix == 0, roll(one, layer), two)
        rows = slice(i * SEAM, (i + 1) * SEAM)
        a_ref[rows, :] = jnp.where(even, up, down).astype(BF)
        b_ref[rows, :] = jnp.where(even, down, up).astype(BF)


def signed(one, two, parity):
    return one + two if parity == 0 else one - two


def radial_fold(rows, iz, parity):
    last = NI - 1
    low = jnp.where(iz > 0, roll(rows[last], 1) - rows[0], 0.0)
    high = jnp.where(iz < EZ - 1, roll(rows[0], -1) - rows[last], 0.0)
    return [signed(rows[c], rows[last - c], parity) for c in range(HI)] + [
        0.5 * signed(low, high, parity)
    ]


def azim_fold(plane, parity):
    return [
        signed(
            plane[b if b < HI else NI], plane[NI - 1 - b if b < HI else NI + 1], parity
        )
        for b in range(HO)
    ]


def third_kernel(ext_ref, const_ref, later_hbm, gs_ref, later_ref, tmp_ref, xs_ref, sem):
    count = ext_ref.shape[-1]
    width = HO * HI
    iz = positions((width, count))[2]
    zeros = jnp.zeros((HI, count), F32)

    copies = chunks(later_hbm, later_ref, sem)
    for copy in copies:
        copy.start()
    for f in range(7):
        pair, side = PLACE[f]
        lanes = slice(side * count, (side + 1) * count)
        values = ext_ref[f]
        for pa in range(2):
            mixed = [signed(values[a], values[NI - 1 - a], pa) for a in range(HI)]
            for pb in range(2):
                at = f % 2 * 4 + pa * 2 + pb
                for a in range(HI):
                    for b, item in enumerate(azim_fold(mixed[a], pb)):
                        row = (a * HO + b) * NI
                        tmp_ref[at, row : row + NI, :] = item
                main = [tmp_ref[at, pl.ds(c, width, stride=NI), :] for c in range(NI)]
                for pc in range(2):
                    rows = []
                    for item in radial_fold(main, iz, pc):
                        rows += [item, zeros]
                    rows.append(jnp.zeros((8, count), F32))
                    operand = jnp.concatenate(rows, axis=0).astype(BF)
                    xs_ref[pair, pa * 4 + pb * 2 + pc, :, lanes] = operand

    def refine(sector, carry):
        for pair in range(PAIRS):
            width = 2 * count if pair < PAIRS - 1 else count
            source = xs_ref[pair, sector, :, 0:width]
            source = jnp.concatenate([source, source], axis=0)
            for q in range(0 if pair < PAIRS - 1 else 1, 4):
                rows = pl.ds(sector * 4 * ROWS + q * ROWS, ROWS)
                gs_ref[pair, q, sector ^ FLIPS[q], :, 0:width] = dot(const_ref[rows, :], source)
        return carry

    lax.fori_loop(0, 8, refine, 0)
    for copy in copies:
        copy.wait()


def fourth_kernel(
    ends_value,
    weights,
    even_ring,
    inv_ref,
    gs_ref,
    ext_ref,
    ends_ref,
    table_ref,
    metric_ref,
    slots_ref,
    ra_ref,
    rb_ref,
    const_ref,
    out_ref,
    tmp_ref,
    along_ref,
    edge_ref,
    vort_ref,
    linear_ref,
    factor_ref,
    normal_x_ref,
    normal_y_ref,
    quad_ref,
    xt_ref,
):
    count = ext_ref.shape[-1]
    layer = EY * EZ
    even = is_even(even_ring)
    ix = positions((SEAM, count))[0]
    end_low, end_high = ends_value
    seam_at = 0
    second_at = seam_at + 4 * SEAM_ROWS
    lift_x_at = second_at + 6 * ROWS
    lift_y_at = lift_x_at + ROWS

    halves = []
    for i in range(5):
        rows = slice(i * SEAM, (i + 1) * SEAM)
        one = ra_ref[rows, :].astype(F32)
        two = rb_ref[rows, :].astype(F32)
        down = jnp.where(even, two, one)
        up = jnp.where(even, one, two)
        halves.append(
            (
                jnp.where(ix == 0, down, roll(up, layer)),
                jnp.where(ix == 0, roll(down, layer), up),
            )
        )
    blocks = [item[0] for item in halves] + [item[1] for item in halves]

    ix3 = positions((1, 1, count))[0]
    iz8 = positions((NI, count))[2]

    def stream_added(first, last, halo):
        lane = positions((1,) * (first.ndim - 1) + (count,))[0]
        low = 0.5 * (jnp.where(lane == 0, halo, roll(last, layer)) - first)
        high = 0.5 * (jnp.where(lane == 0, roll(first, -layer), halo) - last)
        return low, high

    seam = {}
    tmp_ref[...] = jnp.zeros(tmp_ref.shape, F32)
    for f in range(7):
        pair, side = PLACE[f]
        lanes = slice(side * count, (side + 1) * count)
        halo = blocks[f].reshape(EXT, NI, count)
        first, last = ext_ref[f, 0], ext_ref[f, NI - 1]
        low, high = stream_added(first, last, halo)
        if f in (4, 5):
            seam[f] = seam_rows(jnp.where(ix3 == 0, first + low, last + high))
        for pa in range(2):
            mixed = signed(low, high, pa)
            for pb in range(2):
                at = f % 2 * 4 + pa * 2 + pb
                for b, item in enumerate(azim_fold(mixed, pb)):
                    tmp_ref[at, b * NI : (b + 1) * NI, :] = item
                main = [tmp_ref[at, pl.ds(c, NI, stride=NI), :] for c in range(NI)]
                for pc in range(2):
                    rows = radial_fold(main, iz8, pc)
                    rows.append(jnp.zeros((NI, count), F32))
                    operand = jnp.concatenate(rows, axis=0).astype(BF)
                    xt_ref[pair, pa * 4 + pb * 2 + pc, :, lanes] = operand

    def refine_seam(pa, pb, pc):
        sector = pa * 4 + pb * 2 + pc
        at = seam_at + (sector // 2) * SEAM_ROWS
        matrix = const_ref[at : at + SEAM_ROWS, pc * ROWS : pc * ROWS + 2 * 48]
        for pair in range(PAIRS):
            width = 2 * count if pair < PAIRS - 1 else count
            source = xt_ref[pair, sector, :, 0:width]
            added = dot(matrix, jnp.concatenate([source, source], axis=0))
            target = sector ^ 4
            along_ref[pair, target, :, 0:width] = (
                gs_ref[pair, 1, target, :, 0:width] + added[0:ROWS]
            )
            for q, slot in ((0, 0), (2, 1), (3, 2)):
                if q or pair < PAIRS - 1:
                    target = sector ^ FLIPS[q]
                    edge_ref[pair, slot, target, :, 0:width] = (
                        gs_ref[pair, q, target, 0:32, 0:width]
                        + added[ROWS + 32 * slot : ROWS + 32 * slot + 32]
                    )

    for sector in range(8):
        refine_seam(sector // 4, sector // 2 % 2, sector % 2)

    row = lax.broadcasted_iota(jnp.int32, (ROWS, count), 0)
    a_edge = row < HO * HO
    b_edge = lax.rem(row, HO * HO) < HO
    c_edge = lax.rem(row, HO) == 0

    def weight_of(index):
        result = jnp.full((ROWS, count), weights[0], F32)
        for i in range(1, HO):
            result = jnp.where(index == i, weights[i], result)
        return result

    a_pos = lax.div(row, HO * HO)
    quad = weight_of(a_pos) * weight_of(lax.rem(lax.div(row, HO), HO)) * weight_of(lax.rem(row, HO))
    quad_ref[...] = jnp.where(row < HO**3, quad, 0.0)

    table = table_ref[...]
    packed = blocks[9]
    theirs = packed[16:40] + packed[40:64]
    lane_ix = positions((24, count))[0]
    at_low = 0.5 * (table + jnp.where(lane_ix == 0, theirs, roll(table, layer)))
    at_high = 0.5 * (table + jnp.where(lane_ix == 0, roll(table, -layer), theirs))

    def line_of(source, at):
        return source[at : at + 1]

    def by_radius(source, at, side):
        return jnp.where(c_edge, line_of(source, at + 1 + side), line_of(source, at))

    for one in range(2):
        edge = at_low if one == 0 else at_high
        for two in range(2):
            at = one * 2 + two
            factor_ref[at] = jnp.where(
                b_edge, by_radius(table, 3 + 3 * one, two), by_radius(table, 0, two)
            )
            factor_ref[4 + at] = jnp.where(
                a_edge, by_radius(edge, 9, two), by_radius(table, 9, two)
            )
            inside = jnp.where(b_edge, line_of(table, 13 + two), line_of(table, 12))
            outside = jnp.where(b_edge, line_of(edge, 13 + two), line_of(edge, 12))
            factor_ref[8 + at] = jnp.where(a_edge, outside, inside)

    def with_added(parts):
        halves = []
        for part in parts:
            stacked = part.reshape(EXT, NI, count)
            halves.append(jnp.concatenate([part, seam_rows(radial_added(stacked))], axis=0))
        return jnp.concatenate(halves, axis=1).astype(BF)

    def lift(at, rows, operand):
        return dot(const_ref[at : at + rows, 0 : 2 * SEAM], operand)

    stream = []
    for i in range(2):
        shared = jnp.where(ix == 0, end_high, end_low) * seam[4 + i]
        stream.append(blocks[7 + i] + shared)
    lifted = lift(lift_x_at, ROWS, with_added(stream))
    for one in range(2):
        for two in range(2):
            at = one * 2 + two
            scale = jnp.where(
                b_edge, by_radius(theirs, 3 + 3 * one, two), by_radius(theirs, 0, two)
            )[0:32]
            for i in range(2):
                part = lifted[at * 32 : at * 32 + 32, i * count : (i + 1) * count]
                normal_x_ref[i, at] = part * scale

    iy3 = positions((1, 1, count))[1]
    iy2 = iy3[0]
    azim = []
    for i, f in enumerate((3, 5)):
        factor = jnp.where(iy3 == 0, end_high, end_low)
        values = ext_ref[f]
        halo = blocks[f].reshape(EXT, NI, count)
        near = jnp.where(
            iy3 == 0, values[:, 0] + values[:, NI], values[:, NI - 1] + values[:, NI + 1]
        )
        own = ends_ref[i] + factor * near
        near = jnp.where(iy2 == 0, halo[0] + halo[NI], halo[NI - 1] + halo[NI + 1])
        other = blocks[9][8 * i : 8 * i + 8] + factor[0] * near
        low, high = stream_added(own[0], own[NI - 1], other)
        azim.append(jnp.concatenate([rows2(own), low, high], axis=0))
    lifted = lift(lift_y_at, 4 * ROWS, with_added(azim))
    for one in range(2):
        edge = at_low if one == 0 else at_high
        for two in range(2):
            at = one * 2 + two
            scale = jnp.where(a_edge, by_radius(edge, 15, two), by_radius(table, 15, two))
            for i in range(2):
                part = lifted[at * ROWS : (at + 1) * ROWS, i * count : (i + 1) * count]
                normal_y_ref[i, at] = part * scale

    def parts_of(f, q, at, edge):
        pair, side = PLACE[f]
        lanes = slice(side * count, (side + 1) * count)
        if q == 1:
            return [along_ref[pair, sector, at, lanes] for sector in range(8)]
        if edge:
            slot = (0, None, 1, 2)[q]
            return [edge_ref[pair, slot, sector, at, lanes] for sector in range(8)]
        return [gs_ref[pair, q, sector, at, lanes] for sector in range(8)]

    chunk = 16

    def vorticity(at, start, edge):
        shape = (chunk, count)
        lane_ix, lane_iy, lane_iz = positions(shape)
        rows = lax.broadcasted_iota(jnp.int32, shape, 0) + start
        on_a = rows < HO * HO
        on_b = lax.rem(rows, HO * HO) < HO
        on_c = lax.rem(rows, HO) == 0

        def nodal(f, q, factor):
            g = unfold(parts_of(f, q, at, edge))
            return [g[s] * factor_ref[factor(s), at, :] for s in range(8)]

        def along_x(i, f):
            g = nodal(f, 1, lambda s: s % 4)
            if edge:
                for two in range(4):
                    low, high = g[two], g[4 + two]
                    normal = normal_x_ref[i, two, at, :]
                    near = lane_ix == 0
                    first = 0.5 * (low + jnp.where(near, normal, roll(high, layer)))
                    last = 0.5 * (high + jnp.where(near, roll(low, -layer), normal))
                    g[two] = jnp.where(on_a, first, low)
                    g[4 + two] = jnp.where(on_a, last, high)
            return g

        def along_y(i, f):
            g = nodal(f, 2, lambda s: 4 + s // 4 * 2 + s % 2)
            for two in range(4):
                here = two // 2 * 4 + two % 2
                low, high = g[here], g[here + 2]
                normal = normal_y_ref[i, two, at, :]
                first = 0.5 * (low + jnp.where(lane_iy == 0, normal, roll(high, EZ)))
                last = 0.5 * (high + jnp.where(lane_iy == EY - 1, normal, roll(low, -EZ)))
                g[here] = jnp.where(on_b, first, low)
                g[here + 2] = jnp.where(on_b, last, high)
            return g

        def along_z(f):
            g = nodal(f, 3, lambda s: 8 + s // 2)
            lower = on_c & (lane_iz > 0)
            upper = on_c & (lane_iz < EZ - 1)
            for two in range(4):
                low, high = g[2 * two], g[2 * two + 1]
                g[2 * two] = jnp.where(lower, 0.5 * (low + roll(high, 1)), low)
                g[2 * two + 1] = jnp.where(upper, 0.5 * (high + roll(low, -1)), high)
            return g

        pairs = (
            (lambda: along_y(1, 5), lambda: along_z(4)),
            (lambda: along_z(3), lambda: along_x(1, 5)),
            (lambda: along_x(0, 4), lambda: along_y(0, 3)),
        )
        for i, (plus, minus) in enumerate(pairs):
            one, two = plus(), minus()
            folded = unfold([0.125 * (one[s] - two[s]) for s in range(8)])
            for sector in range(8):
                vort_ref[i, sector, at, :] = folded[sector].astype(BF)

    for step in range(2):
        vorticity(slice(step * chunk, (step + 1) * chunk), step * chunk, True)

    def vorticity_step(step, carry):
        start = pl.multiple_of(step * chunk, chunk)
        vorticity(pl.ds(start, chunk), start, False)
        return carry

    lax.fori_loop(2, ROWS // chunk, vorticity_step, 0)

    metric = [metric_ref[i : i + 1] for i in range(3)]
    inv = inv_ref[0]
    scaled = [inv * metric[i] for i in range(3)]
    taken = ((1, 2), (2, 0), (0, 1))
    terms = (((1, 0), (2, 1)), ((2, 0), (0, 1)), ((0, 0), (1, 1)))
    for target in range(8):
        slope = []
        for axis in range(3):
            flip = FLIPS[1 + axis]
            sector = target ^ flip
            source = jnp.concatenate([vort_ref[i, sector] for i in taken[axis]], axis=1)
            source = jnp.concatenate([source, source], axis=0)
            at = second_at + (2 * axis + (1 if sector & flip else 0)) * ROWS
            slope.append(dot(const_ref[at : at + ROWS, :], source))
        for i in range(3):
            (one, half), (two, other) = terms[i]
            plus = scaled[one] * slope[one][:, half * count : (half + 1) * count]
            minus = scaled[two] * slope[two][:, other * count : (other + 1) * count]
            if i == 0:
                linear_ref[i, target] = along_ref[3, target, :, 0:count] * metric[0] + (plus - minus)
            else:
                near = edge_ref[3, i, target, :, 0:count] * metric[i]
                far = gs_ref[3, 1 + i, target, 32:, 0:count] * metric[i]
                linear_ref[i, target, 0:32, :] = near + (plus - minus)[0:32]
                linear_ref[i, target, 32:, :] = far + (plus - minus)[32:]

    def body(edge, step, total):
        at = pl.ds(pl.multiple_of(step * 8, 8), 8)
        for side in range(2):
            total = total + quad_ref[at, :] * energy_of(at, side, edge)
        return total

    def energy_of(at, side, edge):
        def unfold_half(parts):
            return unfold4([signed(parts[s], parts[4 + s], side) for s in range(4)])

        def part(f, q):
            return unfold_half(parts_of(f, q, at, edge))

        base = [[item * metric[j] for item in part(j, 0)] for j in range(3)]
        dual = [part(3 + j, 0) for j in range(3)]
        energy = spread = None
        for i in range(3):
            total = unfold_half([linear_ref[i, s, at, :] for s in range(8)])
            for j in range(3):
                slope = part(3 + i, 1 + j)
                total = [total[s] - base[j][s] * slope[s] for s in range(4)]
                if i == j:
                    more = [slope[s] * metric[i] for s in range(4)]
                    spread = more if i == 0 else [spread[s] + more[s] for s in range(4)]
            inner = None
            for j in range(3):
                slope = part(j, 1 + i)
                more = [dual[j][s] * slope[s] for s in range(4)]
                inner = more if j == 0 else [inner[s] + more[s] for s in range(4)]
            total = [total[s] + metric[i] * inner[s] for s in range(4)]
            more = [item * item for item in total]
            energy = more if i == 0 else [energy[s] + more[s] for s in range(4)]
        energy = [energy[s] + spread[s] * spread[s] for s in range(4)]
        return (energy[0] + energy[1]) + (energy[2] + energy[3])

    total = jnp.zeros((8, count), F32)
    total = lax.fori_loop(0, 4, functools.partial(body, True), total)
    total = lax.fori_loop(4, ROWS // 8, functools.partial(body, False), total)
    weighted = jnp.sum(total, axis=0, keepdims=True)
    result = jnp.sqrt(weighted / 8.0) / float(ORDER_OUT**2)
    high, mid, low = split3(result)
    stacked = jnp.concatenate(
        [high.astype(F32), mid.astype(F32), low.astype(F32), jnp.zeros((13, count), F32)], axis=0
    )
    moved = dot(stacked.astype(BF), slots_ref[...])
    out_ref[...] = moved[0:1] + moved[1:2] + moved[2:3]


def unfold4(parts):
    plus0, minus0 = parts[0] + parts[1], parts[0] - parts[1]
    plus1, minus1 = parts[2] + parts[3], parts[2] - parts[3]
    return [plus0 + plus1, minus0 + minus1, plus0 - plus1, minus0 - minus1]


def unfold(parts):
    plus = unfold4([parts[s] + parts[4 + s] for s in range(4)])
    minus = unfold4([parts[s] - parts[4 + s] for s in range(4)])
    return plus + minus


MIB = 1024 * 1024


def per_device(fields, elem_map, metric, inv_reynolds):
    refine, const, weights, (line, ends_value) = tables()
    count = fields.shape[-1]
    vmem = pl.BlockSpec(memory_space=pltpu.VMEM)

    def params(mib):
        return pltpu.CompilerParams(vmem_limit_bytes=mib * MIB)

    def struct(shape, dtype=F32):
        return jax.ShapeDtypeStruct(shape, dtype)

    hbm = pl.BlockSpec(memory_space=pltpu.HBM)
    inputs = [
        pltpu.with_memory_space_constraint(item, pltpu.HBM)
        for item in (fields, elem_map, metric, jnp.asarray(refine), jnp.asarray(const))
    ]
    slots, local_metric, message, coarse, refine = pl.pallas_call(
        functools.partial(first_kernel, line),
        out_shape=(
            struct((count, count), BF),
            struct((8, count)),
            struct((9 * 64 + 16, count), BF),
            struct((7, NI, NI, NI, count)),
            struct(refine.shape, BF),
        ),
        in_specs=[hbm] * 4,
        out_specs=(vmem,) * 5,
        scratch_shapes=[
            pltpu.VMEM(fields.shape, BF),
            pltpu.VMEM(elem_map.shape, jnp.int32),
            pltpu.VMEM(metric.shape, F32),
            pltpu.SemaphoreType.DMA((17,)),
        ],
        compiler_params=params(6),
        name="first",
    )(*inputs[:4])

    azim = lax.axis_size("azim")
    if azim == 2:
        halo = lax.ppermute(message, "azim", [(0, 1), (1, 0)])
    else:
        ahead = lax.ppermute(message, "azim", [(i, (i + 1) % azim) for i in range(azim)])
        behind = lax.ppermute(message, "azim", [((i + 1) % azim, i) for i in range(azim)])
        iy = (jnp.arange(count) // EZ) % EY
        halo = jnp.where(iy >= EY // 2, ahead, behind)

    streams = lax.axis_size("strm")
    even_ring = streams % 2 == 0
    extended, ends, table, to_a, to_b = pl.pallas_call(
        functools.partial(second_kernel, line, even_ring),
        out_shape=(
            struct((7, NI, EXT, NI, count)),
            struct((2, NI, NI, count)),
            struct((24, count)),
            struct((5 * SEAM, count), BF),
            struct((5 * SEAM, count), BF),
        ),
        in_specs=[vmem] * 3,
        out_specs=(vmem,) * 5,
        compiler_params=params(12),
        name="second",
    )(coarse, local_metric, halo)

    if even_ring:
        near = [(i, i ^ 1) for i in range(streams)]
        far = []
        for i in range(1, streams, 2):
            far += [(i, (i + 1) % streams), ((i + 1) % streams, i)]
        got_a = lax.ppermute(to_a, "strm", near)
        got_b = lax.ppermute(to_b, "strm", far)
    else:
        got_b = lax.ppermute(to_a, "strm", [(i, (i + 1) % streams) for i in range(streams)])
        got_a = lax.ppermute(to_b, "strm", [((i + 1) % streams, i) for i in range(streams)])

    raw, const = pl.pallas_call(
        third_kernel,
        out_shape=(struct((PAIRS, 4, 8, ROWS, 2 * count)), struct(const.shape, BF)),
        in_specs=[vmem, vmem, hbm],
        out_specs=(vmem, vmem),
        scratch_shapes=[
            pltpu.VMEM((8, HO * HI * NI, count), F32),
            pltpu.VMEM((PAIRS, 8, ROWS, 2 * count), BF),
            pltpu.SemaphoreType.DMA((8,)),
        ],
        compiler_params=params(8),
        cost_estimate=pl.CostEstimate(
            flops=4 * 10**9, bytes_accessed=20 * 10**6, transcendentals=0
        ),
        name="third",
    )(extended, refine, inputs[4])

    result = pl.pallas_call(
        functools.partial(fourth_kernel, ends_value, weights, even_ring),
        out_shape=struct((1, count)),
        in_specs=[pl.BlockSpec(memory_space=pltpu.SMEM)] + [vmem] * 9,
        out_specs=vmem,
        scratch_shapes=[
            pltpu.VMEM((8, NI * NI, count), F32),
            pltpu.VMEM((PAIRS, 8, ROWS, 2 * count), F32),
            pltpu.VMEM((PAIRS, 3, 8, 32, 2 * count), F32),
            pltpu.VMEM((3, 8, ROWS, count), BF),
            pltpu.VMEM((3, 8, ROWS, count), F32),
            pltpu.VMEM((12, ROWS, count), F32),
            pltpu.VMEM((2, 4, 32, count), F32),
            pltpu.VMEM((2, 4, ROWS, count), F32),
            pltpu.VMEM((ROWS, count), F32),
            pltpu.VMEM((PAIRS, 8, 48, 2 * count), BF),
        ],
        compiler_params=params(20),
        name="fourth",
    )(
        inv_reynolds,
        raw,
        extended,
        ends,
        table,
        local_metric,
        slots,
        got_a,
        got_b,
        const,
    )
    return result.reshape(count)


def solution(mesh):
    return jax.shard_map(
        per_device,
        mesh=mesh,
        in_specs=(
            P(None, None, ("grp", "strm", "azim")),
            P(("strm", "azim"), None),
            P(None, ("strm", "azim")),
            P("grp"),
        ),
        out_specs=P(("grp", "strm", "azim")),
        check_vma=False,
    )
```

```python
import functools

import jax
import jax.numpy as jnp
import numpy as np
from jax import lax
from jax.experimental import pallas as pl
from jax.experimental.pallas import tpu as pltpu
from jax.sharding import PartitionSpec as P

ORDER_IN = 7
ORDER_OUT = 9
EY = 8
EZ = 8
NI = ORDER_IN + 1
NO = ORDER_OUT + 1
HI = NI // 2
HO = NO // 2
ROWS = 128
SEAM_ROWS = ROWS + 3 * 32
EXT = NI + 2
SEAM = EXT * NI
BF = jnp.bfloat16
F32 = jnp.float32
PLACE = {3: (0, 0), 4: (0, 1), 5: (1, 0), 0: (1, 1), 1: (2, 0), 2: (2, 1), 6: (3, 0)}
PAIRS = 4
FLIPS = (0, 4, 2, 1)


def gll_table(extent):
    degree = extent - 1
    points = np.cos(np.pi * np.arange(extent) / degree)
    legendre = np.zeros((extent, extent))

    def fill():
        legendre[:, 0] = 1.0
        legendre[:, 1] = points
        for level in range(2, extent):
            legendre[:, level] = (
                (2 * level - 1) * points * legendre[:, level - 1]
                - (level - 1) * legendre[:, level - 2]
            ) / level

    for sweep in range(100):
        fill()
        points = points - (points * legendre[:, degree] - legendre[:, degree - 1]) / (
            extent * legendre[:, degree]
        )
    fill()
    weights = 2.0 / (degree * extent * legendre[:, degree] ** 2)
    return (points[::-1].copy(), weights[::-1].copy())


def lagrange_matrix(source, target):
    result = np.ones((len(target), len(source)))
    for column in range(len(source)):
        for partner in range(len(source)):
            if partner != column:
                result[:, column] *= (target - source[partner]) / (source[column] - source[partner])
    return result


def derivative_matrix(points):
    extent = len(points)
    identity = np.eye(extent)
    spacing = points[:, None] - points[None, :] + identity
    barycen = 1.0 / np.prod(spacing, axis=1)
    matrix = barycen[None, :] / barycen[:, None] / spacing * (1.0 - identity)
    return matrix - identity * matrix.sum(axis=1)[:, None]


def bf16_parts(matrix):
    high = matrix.astype(jnp.bfloat16)
    low = (matrix - high.astype(np.float64)).astype(jnp.bfloat16)
    return high, low


def pad_rows(matrix, rows):
    return np.concatenate([matrix, np.zeros((rows - matrix.shape[0],) + matrix.shape[1:])])


def two_terms(matrix):
    return np.concatenate(bf16_parts(matrix), axis=-1)


@functools.cache
def tables():
    coarse, unused = gll_table(NI)
    fine, weights = gll_table(NO)
    interp = lagrange_matrix(coarse, fine)
    slopes = derivative_matrix(fine)
    ends = np.eye(NO)[:, [0, NO - 1]]
    value = np.concatenate([interp, ends], axis=1)
    both = slopes @ value

    def folded(matrix, parity):
        sign = 1.0 - 2.0 * parity
        if matrix.shape[1] == EXT and matrix is not slopes:
            left = matrix[:HO, [0, 1, 2, 3, 8]]
            right = matrix[:HO, [7, 6, 5, 4, 9]]
        else:
            left = matrix[:HO, :HO]
            right = matrix[:HO, ::-1][:, :HO]
        return left + sign * right

    refine, seams = [], []
    for sector in range(8):
        pa, pb, pc = sector // 4, sector // 2 % 2, sector % 2
        blocks, ends_of = [], []
        for ta, tb, tc in (
            (value, value, value),
            (both, value, value),
            (value, both, value),
            (value, value, both),
        ):
            block = 0.125 * np.einsum(
                "ap,bq,cr->abcrpq", folded(ta, pa), folded(tb, pb), folded(tc, pc)
            ).reshape(HO**3, HO, HO, HO)
            own = np.zeros((HO**3, HO, 24))
            own[:, :, : HO * HI] = block[:, :, :HI].reshape(HO**3, HO, HO * HI)
            own = np.pad(own.reshape(HO**3, -1), ((0, 0), (0, ROWS - 24 * HO)))
            blocks.append(pad_rows(own, ROWS))
            added = np.zeros((HO**3, 48))
            added[:, : 8 * HO] = np.pad(block[:, :, HI], ((0, 0), (0, 0), (0, 3))).reshape(HO**3, -1)
            ends_of.append(added)
        refine.append(two_terms(np.concatenate(blocks)))
        rows = [pad_rows(ends_of[1], ROWS)]
        rows += [pad_rows(ends_of[q][: HO * HO], 32) for q in (0, 2, 3)]
        seams.append(np.pad(two_terms(np.concatenate(rows)), ((0, 0), (0, ROWS - 96))))
    refine = np.stack(refine)
    seams = [np.concatenate(seams[2 * i : 2 * i + 2], axis=1) for i in range(4)]

    second = []
    eye = np.eye(HO)
    for axis in range(3):
        for parity in range(2):
            factors = [eye, eye, eye]
            factors[axis] = folded(slopes, parity)
            block = np.kron(np.kron(factors[0], factors[1]), factors[2])
            edge = ROWS - HO**3
            second.append(two_terms(np.pad(block, ((0, edge), (0, edge)))))
    second = np.stack(second)

    def half(side):
        return value[:HO] if side == 0 else value[::-1][:HO]

    lift_x, lift_y = [], []
    for side in range(2):
        for radial in range(2):
            plain = np.zeros((HO, EXT, HO, NI))
            added = np.zeros((HO, EXT, HO, NI))
            plain[...] = np.einsum("ap,cr->apcr", half(side), half(radial)[:, :NI])
            added[..., 0] = np.einsum("ap,c->apc", half(side), half(radial)[:, NI])
            added[..., NI - 1] = np.einsum("ap,c->apc", half(side), half(radial)[:, NI + 1])
            face = np.stack([plain, added]).transpose(1, 3, 0, 2, 4).reshape(HO, HO, 2 * SEAM)
            lift_x.append(pad_rows(face.reshape(HO * HO, -1), 32))
            spread = np.zeros((HO, HO, HO, 2 * SEAM))
            spread[:, 0] = face
            lift_y.append(pad_rows(spread.reshape(HO**3, -1), ROWS))

    def one_term(parts):
        matrix = np.concatenate(parts)
        return np.pad(matrix, ((0, 0), (0, 2 * ROWS - matrix.shape[1]))).astype(jnp.bfloat16)

    refine = refine.reshape(-1, 2 * ROWS)
    const = np.concatenate(
        seams + [second.reshape(-1, 2 * ROWS), one_term(lift_x), one_term(lift_y)]
    )
    half_weights = [float(v) for v in weights[:HO]]
    line = []
    for end, far in ((0, NO - 1), (NO - 1, 0)):
        weights_in = slopes[end].copy()
        weights_in[[0, NO - 1]] = 0.0
        line.append(([float(v) for v in weights_in @ interp], float(slopes[end, far])))
    ends = (float(slopes[0, 0]), float(slopes[NO - 1, NO - 1]))
    return refine, const, half_weights, (line, ends)


def dot(a, b, contract_last=False):
    dims = (((1,), (1 if contract_last else 0,)), ((), ()))
    return lax.dot_general(a, b, dims, preferred_element_type=F32)


def is_even(even_ring):
    return lax.rem(lax.axis_index("strm"), 2) == 0 if even_ring else True


def rows3(x):
    return x.reshape(NI, NI, x.shape[-1])


def seam_rows(x):
    return x.reshape(SEAM, x.shape[-1])


def rows2(x):
    return x.reshape(NI * NI, x.shape[-1])


def roll(x, shift):
    count = x.shape[-1]
    return pltpu.roll(x, shift % count, x.ndim - 1)


def positions(shape):
    lane = lax.broadcasted_iota(jnp.int32, shape, len(shape) - 1)
    return lax.div(lane, EY * EZ), lax.rem(lax.div(lane, EZ), EY), lax.rem(lane, EZ)


def split3(x):
    high = x.astype(BF)
    rest = x - high.astype(F32)
    mid = rest.astype(BF)
    low = (rest - mid.astype(F32)).astype(BF)
    return high, mid, low


def radial_added(x):
    axis = x.ndim - 2
    shape = (1,) * axis + x.shape[-2:]
    node = lax.broadcasted_iota(jnp.int32, shape, axis)
    iz = positions(shape)[2]
    last = x.shape[-2] - 1
    before = pltpu.roll(roll(x, 1), 1, axis)
    after = pltpu.roll(roll(x, -1), last, axis)
    low = (node == 0) & (iz > 0)
    high = (node == last) & (iz < EZ - 1)
    other = jnp.where(low, before, jnp.where(high, after, x))
    return 0.5 * (other - x)


def end_lines(line, planes, step):
    (near, near_far), (high, high_far) = line
    first, last = planes[0], planes[-1]
    one = near_far * 0.5 * (last + roll(first, -step))
    two = high_far * 0.5 * (first + roll(last, step))
    for i, plane in enumerate(planes):
        one = one + near[i] * plane
        two = two + high[i] * plane
    return one, two


def chunks(source, target, sem, count=8):
    step = source.shape[0] // count
    return [
        pltpu.make_async_copy(
            source.at[i * step : (i + 1) * step], target.at[i * step : (i + 1) * step], sem.at[i]
        )
        for i in range(count)
    ]


def first_kernel(
    line,
    fields_hbm,
    emap_hbm,
    metric_hbm,
    table_hbm,
    slots_ref,
    metric_out,
    msg_ref,
    fields,
    table_ref,
    emap,
    metric,
    sem,
):
    count = fields.shape[-1]
    order = (3, 5, 4, 0, 1, 2, 6)
    small = [
        pltpu.make_async_copy(emap_hbm, emap, sem.at[7]),
        pltpu.make_async_copy(metric_hbm, metric, sem.at[8]),
    ]
    large = [pltpu.make_async_copy(fields_hbm.at[f], fields.at[f], sem.at[f]) for f in order]
    tables_copies = chunks(table_hbm, table_ref, sem.at[pl.ds(9, 8)])
    for copy in small + large + tables_copies:
        copy.start()
    for copy in small:
        copy.wait()
    local = lax.broadcasted_iota(jnp.int32, (count, count), 0)
    slots = (local == emap[...]).astype(F32).astype(BF)
    slots_ref[...] = slots
    high, mid, low = split3(metric[...])
    pad = jnp.zeros((7, count), F32)
    stacked = jnp.concatenate([high.astype(F32), mid.astype(F32), low.astype(F32), pad], axis=0)
    moved = dot(stacked.astype(BF), slots, True)
    local = moved[0:3] + moved[3:6] + moved[6:9]
    metric_out[...] = jnp.concatenate([local, jnp.zeros((5, count), F32)], axis=0)
    high = local.astype(BF).astype(F32)
    tail = jnp.concatenate([high, local - high, jnp.zeros((10, count), F32)], axis=0)
    msg_ref[9 * 64 : 9 * 64 + 16, :] = tail.astype(BF)
    iy = positions((1, 1, count))[1]
    for f, copy in zip(order, large):
        copy.wait()
        if f in (3, 5):
            values = dot(fields[f], slots, True).reshape(NI, NI, NI, count)
            first, last = values[:, 0], values[:, NI - 1]
        else:
            planes = fields[f].reshape(NI, NI, NI, count)
            planes = jnp.concatenate([planes[:, 0], planes[:, NI - 1]], axis=0)
            planes = dot(planes.reshape(2 * NI * NI, count), slots, True)
            first, last = rows3(planes[0:64]), rows3(planes[64:128])
        face = jnp.where(iy == 0, first, last)
        msg_ref[f * 64 : f * 64 + 64, :] = rows2(face).astype(BF)
        if f in (3, 5):
            low, high = end_lines(line, [values[:, b] for b in range(NI)], EZ)
            at = (7 + (f == 5)) * 64
            msg_ref[at : at + 64, :] = rows2(jnp.where(iy == 0, low, high)).astype(BF)
    for copy in tables_copies:
        copy.wait()


def own_kernel(fields_ref, slots_ref, coarse_ref):
    count = fields_ref.shape[-1]
    for f in range(7):
        values = dot(fields_ref[f], slots_ref[...], True)
        coarse_ref[f] = values.reshape(NI, NI, NI, count)


def from_azim(x, iy):
    gap = (EY - 1) * EZ
    return jnp.where(iy == 0, roll(x, -gap), roll(x, gap))


def metric_classes(x, halo, shift, at_low, at_high):
    low = 0.5 * (x + jnp.where(at_low, halo, roll(x, shift)))
    high = 0.5 * (x + jnp.where(at_high, halo, roll(x, -shift)))
    return [x, low, high]


def radial_classes(x, iz):
    low = jnp.where(iz > 0, 0.5 * (x + roll(x, 1)), x)
    high = jnp.where(iz < EZ - 1, 0.5 * (x + roll(x, -1)), x)
    return [x, low, high]


def second_kernel(
    line, even_ring, coarse_ref, metric_ref, halo_ref, ext_ref, ends_ref, table_ref, a_ref, b_ref
):
    count = coarse_ref.shape[-1]
    layer = EY * EZ
    ix, iy, iz = positions((1, 1, count))
    blocks = []
    lines = []
    for f in range(7):
        values = coarse_ref[f]
        first, last = values[:, 0], values[:, NI - 1]
        halo = from_azim(rows3(halo_ref[f * 64 : f * 64 + 64, :].astype(F32)), iy)
        low = 0.5 * (jnp.where(iy == 0, halo, roll(last, EZ)) - first)
        high = 0.5 * (jnp.where(iy == EY - 1, halo, roll(first, -EZ)) - last)
        values = jnp.concatenate([values, low[:, None], high[:, None]], axis=1)
        ext_ref[f] = values
        blocks.append(seam_rows(jnp.where(ix == 0, values[0], values[NI - 1])))
        if f in (4, 5):
            low, high = end_lines(line, [values[a] for a in range(NI)], layer)
            lines.append(seam_rows(jnp.where(ix == 0, low, high)))
    blocks += lines
    extra = []
    for i in range(2):
        ends = from_azim(rows3(halo_ref[(7 + i) * 64 : (8 + i) * 64, :].astype(F32)), iy)
        ends_ref[i] = ends
        extra.append(jnp.where(ix[0] == 0, ends[0], ends[NI - 1]))

    ix, iy, iz = positions((1, count))
    packed = halo_ref[9 * 64 : 9 * 64 + 16, :].astype(F32)
    other = from_azim(packed[0:3] + packed[3:6], iy)
    own = metric_ref[...]
    lows, highs = iy == 0, iy == EY - 1
    rows = []
    for item in metric_classes(own[0:1], other[0:1], EZ, lows, highs):
        rows += radial_classes(item, iz)
    rows += radial_classes(own[1:2], iz)
    rows += metric_classes(own[2:3], other[2:3], EZ, lows, highs)
    rows += radial_classes(other[1:2], iz)
    table = jnp.concatenate(rows + [jnp.zeros((24 - len(rows), count), F32)], axis=0)
    table_ref[...] = table
    high = table.astype(BF).astype(F32)
    spare = jnp.zeros((SEAM - 64, count), F32)
    blocks.append(jnp.concatenate(extra + [high, table - high, spare], axis=0))

    ix = positions((SEAM, count))[0]
    even = is_even(even_ring)
    half = len(blocks) // 2
    for i in range(half):
        one, two = blocks[i], blocks[half + i]
        down = jnp.where(ix == 0, one, roll(two, layer))
        up = jnp.where(ix == 0, roll(one, layer), two)
        rows = slice(i * SEAM, (i + 1) * SEAM)
        a_ref[rows, :] = jnp.where(even, up, down).astype(BF)
        b_ref[rows, :] = jnp.where(even, down, up).astype(BF)


def signed(one, two, parity):
    return one + two if parity == 0 else one - two


def radial_fold(rows, iz, parity):
    last = NI - 1
    low = jnp.where(iz > 0, roll(rows[last], 1) - rows[0], 0.0)
    high = jnp.where(iz < EZ - 1, roll(rows[0], -1) - rows[last], 0.0)
    return [signed(rows[c], rows[last - c], parity) for c in range(HI)] + [
        0.5 * signed(low, high, parity)
    ]


def azim_fold(plane, parity):
    return [
        signed(
            plane[b if b < HI else NI], plane[NI - 1 - b if b < HI else NI + 1], parity
        )
        for b in range(HO)
    ]


def third_kernel(ext_ref, const_ref, later_hbm, gs_ref, later_ref, tmp_ref, xs_ref, sem):
    count = ext_ref.shape[-1]
    width = HO * HI
    iz = positions((width, count))[2]
    zeros = jnp.zeros((HI, count), F32)

    copies = chunks(later_hbm, later_ref, sem)
    for copy in copies:
        copy.start()
    for f in range(7):
        pair, side = PLACE[f]
        lanes = slice(side * count, (side + 1) * count)
        values = ext_ref[f]
        for pa in range(2):
            mixed = [signed(values[a], values[NI - 1 - a], pa) for a in range(HI)]
            for pb in range(2):
                at = f % 2 * 4 + pa * 2 + pb
                for a in range(HI):
                    for b, item in enumerate(azim_fold(mixed[a], pb)):
                        row = (a * HO + b) * NI
                        tmp_ref[at, row : row + NI, :] = item
                main = [tmp_ref[at, pl.ds(c, width, stride=NI), :] for c in range(NI)]
                for pc in range(2):
                    rows = []
                    for item in radial_fold(main, iz, pc):
                        rows += [item, zeros]
                    rows.append(jnp.zeros((8, count), F32))
                    operand = jnp.concatenate(rows, axis=0).astype(BF)
                    xs_ref[pair, pa * 4 + pb * 2 + pc, :, lanes] = operand

    def refine(sector, carry):
        for pair in range(PAIRS):
            width = 2 * count if pair < PAIRS - 1 else count
            source = xs_ref[pair, sector, :, 0:width]
            source = jnp.concatenate([source, source], axis=0)
            for q in range(0 if pair < PAIRS - 1 else 1, 4):
                rows = pl.ds(sector * 4 * ROWS + q * ROWS, ROWS)
                gs_ref[pair, q, sector ^ FLIPS[q], :, 0:width] = dot(const_ref[rows, :], source)
        return carry

    lax.fori_loop(0, 8, refine, 0, unroll=2)
    for copy in copies:
        copy.wait()


def fourth_kernel(
    ends_value,
    weights,
    even_ring,
    inv_ref,
    gs_ref,
    ext_ref,
    ends_ref,
    table_ref,
    metric_ref,
    slots_ref,
    ra_ref,
    rb_ref,
    const_ref,
    out_ref,
    tmp_ref,
    along_ref,
    edge_ref,
    vort_ref,
    linear_ref,
    factor_ref,
    normal_x_ref,
    normal_y_ref,
    quad_ref,
    xt_ref,
    nodal_ref,
):
    count = ext_ref.shape[-1]
    layer = EY * EZ
    even = is_even(even_ring)
    ix = positions((SEAM, count))[0]
    end_low, end_high = ends_value
    seam_at = 0
    second_at = seam_at + 4 * SEAM_ROWS
    lift_x_at = second_at + 6 * ROWS
    lift_y_at = lift_x_at + ROWS

    halves = []
    for i in range(5):
        rows = slice(i * SEAM, (i + 1) * SEAM)
        one = ra_ref[rows, :].astype(F32)
        two = rb_ref[rows, :].astype(F32)
        down = jnp.where(even, two, one)
        up = jnp.where(even, one, two)
        halves.append(
            (
                jnp.where(ix == 0, down, roll(up, layer)),
                jnp.where(ix == 0, roll(down, layer), up),
            )
        )
    blocks = [item[0] for item in halves] + [item[1] for item in halves]

    ix3 = positions((1, 1, count))[0]
    iz8 = positions((NI, count))[2]

    def stream_added(first, last, halo):
        lane = positions((1,) * (first.ndim - 1) + (count,))[0]
        low = 0.5 * (jnp.where(lane == 0, halo, roll(last, layer)) - first)
        high = 0.5 * (jnp.where(lane == 0, roll(first, -layer), halo) - last)
        return low, high

    seam = {}
    tmp_ref[...] = jnp.zeros(tmp_ref.shape, F32)
    for f in range(7):
        pair, side = PLACE[f]
        lanes = slice(side * count, (side + 1) * count)
        halo = blocks[f].reshape(EXT, NI, count)
        first, last = ext_ref[f, 0], ext_ref[f, NI - 1]
        low, high = stream_added(first, last, halo)
        if f in (4, 5):
            seam[f] = seam_rows(jnp.where(ix3 == 0, first + low, last + high))
        for pa in range(2):
            mixed = signed(low, high, pa)
            for pb in range(2):
                at = f % 2 * 4 + pa * 2 + pb
                for b, item in enumerate(azim_fold(mixed, pb)):
                    tmp_ref[at, b * NI : (b + 1) * NI, :] = item
                main = [tmp_ref[at, pl.ds(c, NI, stride=NI), :] for c in range(NI)]
                for pc in range(2):
                    rows = radial_fold(main, iz8, pc)
                    rows.append(jnp.zeros((NI, count), F32))
                    operand = jnp.concatenate(rows, axis=0).astype(BF)
                    xt_ref[pair, pa * 4 + pb * 2 + pc, :, lanes] = operand

    def refine_seam(pa, pb, pc):
        sector = pa * 4 + pb * 2 + pc
        at = seam_at + (sector // 2) * SEAM_ROWS
        matrix = const_ref[at : at + SEAM_ROWS, pc * ROWS : pc * ROWS + 2 * 48]
        for pair in range(PAIRS):
            width = 2 * count if pair < PAIRS - 1 else count
            source = xt_ref[pair, sector, :, 0:width]
            added = dot(matrix, jnp.concatenate([source, source], axis=0))
            target = sector ^ 4
            along_ref[pair, target, :, 0:width] = (
                gs_ref[pair, 1, target, :, 0:width] + added[0:ROWS]
            )
            for q, slot in ((0, 0), (2, 1), (3, 2)):
                if q or pair < PAIRS - 1:
                    target = sector ^ FLIPS[q]
                    edge_ref[pair, slot, target, :, 0:width] = (
                        gs_ref[pair, q, target, 0:32, 0:width]
                        + added[ROWS + 32 * slot : ROWS + 32 * slot + 32]
                    )

    for sector in range(8):
        refine_seam(sector // 4, sector // 2 % 2, sector % 2)

    row = lax.broadcasted_iota(jnp.int32, (ROWS, count), 0)
    a_edge = row < HO * HO
    b_edge = lax.rem(row, HO * HO) < HO
    c_edge = lax.rem(row, HO) == 0

    def weight_of(index):
        result = jnp.full((ROWS, count), weights[0], F32)
        for i in range(1, HO):
            result = jnp.where(index == i, weights[i], result)
        return result

    a_pos = lax.div(row, HO * HO)
    quad = weight_of(a_pos) * weight_of(lax.rem(lax.div(row, HO), HO)) * weight_of(lax.rem(row, HO))
    quad_ref[...] = jnp.where(row < HO**3, quad, 0.0)

    table = table_ref[...]
    packed = blocks[9]
    theirs = packed[16:40] + packed[40:64]
    lane_ix = positions((24, count))[0]
    at_low = 0.5 * (table + jnp.where(lane_ix == 0, theirs, roll(table, layer)))
    at_high = 0.5 * (table + jnp.where(lane_ix == 0, roll(table, -layer), theirs))

    def line_of(source, at):
        return source[at : at + 1]

    def by_radius(source, at, side):
        return jnp.where(c_edge, line_of(source, at + 1 + side), line_of(source, at))

    for one in range(2):
        edge = at_low if one == 0 else at_high
        for two in range(2):
            at = one * 2 + two
            factor_ref[at] = jnp.where(
                b_edge, by_radius(table, 3 + 3 * one, two), by_radius(table, 0, two)
            )
            factor_ref[4 + at] = jnp.where(
                a_edge, by_radius(edge, 9, two), by_radius(table, 9, two)
            )
            inside = jnp.where(b_edge, line_of(table, 13 + two), line_of(table, 12))
            outside = jnp.where(b_edge, line_of(edge, 13 + two), line_of(edge, 12))
            factor_ref[8 + at] = jnp.where(a_edge, outside, inside)

    def with_added(parts):
        halves = []
        for part in parts:
            stacked = part.reshape(EXT, NI, count)
            halves.append(jnp.concatenate([part, seam_rows(radial_added(stacked))], axis=0))
        return jnp.concatenate(halves, axis=1).astype(BF)

    def lift(at, rows, operand):
        return dot(const_ref[at : at + rows, 0 : 2 * SEAM], operand)

    stream = []
    for i in range(2):
        shared = jnp.where(ix == 0, end_high, end_low) * seam[4 + i]
        stream.append(blocks[7 + i] + shared)
    lifted = lift(lift_x_at, ROWS, with_added(stream))
    for one in range(2):
        for two in range(2):
            at = one * 2 + two
            scale = jnp.where(
                b_edge, by_radius(theirs, 3 + 3 * one, two), by_radius(theirs, 0, two)
            )[0:32]
            for i in range(2):
                part = lifted[at * 32 : at * 32 + 32, i * count : (i + 1) * count]
                normal_x_ref[i, at] = part * scale

    iy3 = positions((1, 1, count))[1]
    iy2 = iy3[0]
    azim = []
    for i, f in enumerate((3, 5)):
        factor = jnp.where(iy3 == 0, end_high, end_low)
        values = ext_ref[f]
        halo = blocks[f].reshape(EXT, NI, count)
        near = jnp.where(
            iy3 == 0, values[:, 0] + values[:, NI], values[:, NI - 1] + values[:, NI + 1]
        )
        own = ends_ref[i] + factor * near
        near = jnp.where(iy2 == 0, halo[0] + halo[NI], halo[NI - 1] + halo[NI + 1])
        other = blocks[9][8 * i : 8 * i + 8] + factor[0] * near
        low, high = stream_added(own[0], own[NI - 1], other)
        azim.append(jnp.concatenate([rows2(own), low, high], axis=0))
    lifted = lift(lift_y_at, 4 * ROWS, with_added(azim))
    for one in range(2):
        edge = at_low if one == 0 else at_high
        for two in range(2):
            at = one * 2 + two
            scale = jnp.where(a_edge, by_radius(edge, 15, two), by_radius(table, 15, two))
            for i in range(2):
                part = lifted[at * ROWS : (at + 1) * ROWS, i * count : (i + 1) * count]
                normal_y_ref[i, at] = part * scale

    def parts_of(f, q, at, edge):
        pair, side = PLACE[f]
        lanes = slice(side * count, (side + 1) * count)
        if q == 1:
            return [along_ref[pair, sector, at, lanes] for sector in range(8)]
        if edge:
            slot = (0, None, 1, 2)[q]
            return [edge_ref[pair, slot, sector, at, lanes] for sector in range(8)]
        return [gs_ref[pair, q, sector, at, lanes] for sector in range(8)]

    chunk = 16

    def vorticity(at, start, edge):
        shape = (chunk, count)
        lane_ix, lane_iy, lane_iz = positions(shape)
        rows = lax.broadcasted_iota(jnp.int32, shape, 0) + start
        on_a = rows < HO * HO
        on_b = lax.rem(rows, HO * HO) < HO
        on_c = lax.rem(rows, HO) == 0

        def nodal(f, q, factor):
            g = unfold(parts_of(f, q, at, edge))
            for s in range(8):
                nodal_ref[kept(f - 3, q - 1), s, at, :] = g[s]
            return [g[s] * factor_ref[factor(s), at, :] for s in range(8)]

        def along_x(i, f):
            g = nodal(f, 1, lambda s: s % 4)
            if edge:
                for two in range(4):
                    low, high = g[two], g[4 + two]
                    normal = normal_x_ref[i, two, at, :]
                    near = lane_ix == 0
                    first = 0.5 * (low + jnp.where(near, normal, roll(high, layer)))
                    last = 0.5 * (high + jnp.where(near, roll(low, -layer), normal))
                    g[two] = jnp.where(on_a, first, low)
                    g[4 + two] = jnp.where(on_a, last, high)
            return g

        def along_y(i, f):
            g = nodal(f, 2, lambda s: 4 + s // 4 * 2 + s % 2)
            for two in range(4):
                here = two // 2 * 4 + two % 2
                low, high = g[here], g[here + 2]
                normal = normal_y_ref[i, two, at, :]
                first = 0.5 * (low + jnp.where(lane_iy == 0, normal, roll(high, EZ)))
                last = 0.5 * (high + jnp.where(lane_iy == EY - 1, normal, roll(low, -EZ)))
                g[here] = jnp.where(on_b, first, low)
                g[here + 2] = jnp.where(on_b, last, high)
            return g

        def along_z(f):
            g = nodal(f, 3, lambda s: 8 + s // 2)
            lower = on_c & (lane_iz > 0)
            upper = on_c & (lane_iz < EZ - 1)
            for two in range(4):
                low, high = g[2 * two], g[2 * two + 1]
                g[2 * two] = jnp.where(lower, 0.5 * (low + roll(high, 1)), low)
                g[2 * two + 1] = jnp.where(upper, 0.5 * (high + roll(low, -1)), high)
            return g

        pairs = (
            (lambda: along_y(1, 5), lambda: along_z(4)),
            (lambda: along_z(3), lambda: along_x(1, 5)),
            (lambda: along_x(0, 4), lambda: along_y(0, 3)),
        )
        for i, (plus, minus) in enumerate(pairs):
            one, two = plus(), minus()
            folded = unfold([0.125 * (one[s] - two[s]) for s in range(8)])
            for sector in range(8):
                vort_ref[i, sector, at, :] = folded[sector].astype(BF)

    for step in range(2):
        vorticity(slice(step * chunk, (step + 1) * chunk), step * chunk, True)

    def vorticity_step(step, carry):
        start = pl.multiple_of(step * chunk, chunk)
        vorticity(pl.ds(start, chunk), start, False)
        return carry

    lax.fori_loop(2, ROWS // chunk, vorticity_step, 0)

    metric = [metric_ref[i : i + 1] for i in range(3)]
    inv = inv_ref[0]
    scaled = [inv * metric[i] for i in range(3)]
    taken = ((1, 2), (2, 0), (0, 1))
    terms = (((1, 0), (2, 1)), ((2, 0), (0, 1)), ((0, 0), (1, 1)))
    for target in range(8):
        slope = []
        for axis in range(3):
            flip = FLIPS[1 + axis]
            sector = target ^ flip
            source = jnp.concatenate([vort_ref[i, sector] for i in taken[axis]], axis=1)
            source = jnp.concatenate([source, source], axis=0)
            at = second_at + (2 * axis + (1 if sector & flip else 0)) * ROWS
            slope.append(dot(const_ref[at : at + ROWS, :], source))
        for i in range(3):
            (one, half), (two, other) = terms[i]
            plus = scaled[one] * slope[one][:, half * count : (half + 1) * count]
            minus = scaled[two] * slope[two][:, other * count : (other + 1) * count]
            if i == 0:
                linear_ref[i, target] = along_ref[3, target, :, 0:count] * metric[0] + (plus - minus)
            else:
                near = edge_ref[3, i, target, :, 0:count] * metric[i]
                far = gs_ref[3, 1 + i, target, 32:, 0:count] * metric[i]
                linear_ref[i, target, 0:32, :] = near + (plus - minus)[0:32]
                linear_ref[i, target, 32:, :] = far + (plus - minus)[32:]

    def body(edge, step, total):
        at = pl.ds(pl.multiple_of(step * 8, 8), 8)
        for side in range(2):
            total = total + quad_ref[at, :] * energy_of(at, side, edge)
        return total

    def energy_of(at, side, edge):
        def unfold_half(parts):
            return unfold4([signed(parts[s], parts[4 + s], side) for s in range(4)])

        def part(f, q):
            return unfold_half(parts_of(f, q, at, edge))

        base = [[item * metric[j] for item in part(j, 0)] for j in range(3)]
        dual = [part(3 + j, 0) for j in range(3)]
        energy = spread = None
        for i in range(3):
            total = unfold_half([linear_ref[i, s, at, :] for s in range(8)])
            for j in range(3):
                if i == j:
                    slope = part(3 + i, 1 + j)
                else:
                    slope = [nodal_ref[kept(i, j), side * 4 + s, at, :] for s in range(4)]
                total = [total[s] - base[j][s] * slope[s] for s in range(4)]
                if i == j:
                    more = [slope[s] * metric[i] for s in range(4)]
                    spread = more if i == 0 else [spread[s] + more[s] for s in range(4)]
            inner = None
            for j in range(3):
                slope = part(j, 1 + i)
                more = [dual[j][s] * slope[s] for s in range(4)]
                inner = more if j == 0 else [inner[s] + more[s] for s in range(4)]
            total = [total[s] + metric[i] * inner[s] for s in range(4)]
            more = [item * item for item in total]
            energy = more if i == 0 else [energy[s] + more[s] for s in range(4)]
        energy = [energy[s] + spread[s] * spread[s] for s in range(4)]
        return (energy[0] + energy[1]) + (energy[2] + energy[3])

    total = jnp.zeros((8, count), F32)
    total = lax.fori_loop(0, 4, functools.partial(body, True), total)
    total = lax.fori_loop(4, ROWS // 8, functools.partial(body, False), total)
    weighted = jnp.sum(total, axis=0, keepdims=True)
    result = jnp.sqrt(weighted / 8.0) / float(ORDER_OUT**2)
    high, mid, low = split3(result)
    stacked = jnp.concatenate(
        [high.astype(F32), mid.astype(F32), low.astype(F32), jnp.zeros((13, count), F32)], axis=0
    )
    moved = dot(stacked.astype(BF), slots_ref[...])
    out_ref[...] = moved[0:1] + moved[1:2] + moved[2:3]


def kept(component, axis):
    return component * 2 + (axis if axis < component else axis - 1)


def unfold4(parts):
    plus0, minus0 = parts[0] + parts[1], parts[0] - parts[1]
    plus1, minus1 = parts[2] + parts[3], parts[2] - parts[3]
    return [plus0 + plus1, minus0 + minus1, plus0 - plus1, minus0 - minus1]


def unfold(parts):
    plus = unfold4([parts[s] + parts[4 + s] for s in range(4)])
    minus = unfold4([parts[s] - parts[4 + s] for s in range(4)])
    return plus + minus


MIB = 1024 * 1024


def per_device(fields, elem_map, metric, inv_reynolds):
    refine, const, weights, (line, ends_value) = tables()
    count = fields.shape[-1]
    vmem = pl.BlockSpec(memory_space=pltpu.VMEM)

    def params(mib):
        return pltpu.CompilerParams(vmem_limit_bytes=mib * MIB)

    def struct(shape, dtype=F32):
        return jax.ShapeDtypeStruct(shape, dtype)

    hbm = pl.BlockSpec(memory_space=pltpu.HBM)
    inputs = [
        pltpu.with_memory_space_constraint(item, pltpu.HBM)
        for item in (fields, elem_map, metric, jnp.asarray(refine), jnp.asarray(const))
    ]
    slots, local_metric, message, near_fields, refine = pl.pallas_call(
        functools.partial(first_kernel, line),
        out_shape=(
            struct((count, count), BF),
            struct((8, count)),
            struct((9 * 64 + 16, count), BF),
            struct(fields.shape, BF),
            struct(refine.shape, BF),
        ),
        in_specs=[hbm] * 4,
        out_specs=(vmem,) * 5,
        scratch_shapes=[
            pltpu.VMEM(elem_map.shape, jnp.int32),
            pltpu.VMEM(metric.shape, F32),
            pltpu.SemaphoreType.DMA((17,)),
        ],
        compiler_params=params(6),
        name="first",
    )(*inputs[:4])

    coarse = pl.pallas_call(
        own_kernel,
        out_shape=struct((7, NI, NI, NI, count)),
        in_specs=[vmem] * 2,
        out_specs=vmem,
        compiler_params=params(6),
        cost_estimate=pl.CostEstimate(
            flops=2 * fields.size * count, bytes_accessed=3 * 10**6, transcendentals=0
        ),
        name="own",
    )(near_fields, slots)

    azim = lax.axis_size("azim")
    if azim == 2:
        halo = lax.ppermute(message, "azim", [(0, 1), (1, 0)])
    else:
        ahead = lax.ppermute(message, "azim", [(i, (i + 1) % azim) for i in range(azim)])
        behind = lax.ppermute(message, "azim", [((i + 1) % azim, i) for i in range(azim)])
        iy = (jnp.arange(count) // EZ) % EY
        halo = jnp.where(iy >= EY // 2, ahead, behind)

    streams = lax.axis_size("strm")
    even_ring = streams % 2 == 0
    extended, ends, table, to_a, to_b = pl.pallas_call(
        functools.partial(second_kernel, line, even_ring),
        out_shape=(
            struct((7, NI, EXT, NI, count)),
            struct((2, NI, NI, count)),
            struct((24, count)),
            struct((5 * SEAM, count), BF),
            struct((5 * SEAM, count), BF),
        ),
        in_specs=[vmem] * 3,
        out_specs=(vmem,) * 5,
        compiler_params=params(12),
        name="second",
    )(coarse, local_metric, halo)

    if even_ring:
        near = [(i, i ^ 1) for i in range(streams)]
        far = []
        for i in range(1, streams, 2):
            far += [(i, (i + 1) % streams), ((i + 1) % streams, i)]
        got_a = lax.ppermute(to_a, "strm", near)
        got_b = lax.ppermute(to_b, "strm", far)
    else:
        got_b = lax.ppermute(to_a, "strm", [(i, (i + 1) % streams) for i in range(streams)])
        got_a = lax.ppermute(to_b, "strm", [((i + 1) % streams, i) for i in range(streams)])

    raw, const = pl.pallas_call(
        third_kernel,
        out_shape=(struct((PAIRS, 4, 8, ROWS, 2 * count)), struct(const.shape, BF)),
        in_specs=[vmem, vmem, hbm],
        out_specs=(vmem, vmem),
        scratch_shapes=[
            pltpu.VMEM((8, HO * HI * NI, count), F32),
            pltpu.VMEM((PAIRS, 8, ROWS, 2 * count), BF),
            pltpu.SemaphoreType.DMA((8,)),
        ],
        compiler_params=params(8),
        cost_estimate=pl.CostEstimate(
            flops=4 * 10**9, bytes_accessed=20 * 10**6, transcendentals=0
        ),
        name="third",
    )(extended, refine, inputs[4])

    result = pl.pallas_call(
        functools.partial(fourth_kernel, ends_value, weights, even_ring),
        out_shape=struct((1, count)),
        in_specs=[pl.BlockSpec(memory_space=pltpu.SMEM)] + [vmem] * 9,
        out_specs=vmem,
        scratch_shapes=[
            pltpu.VMEM((8, NI * NI, count), F32),
            pltpu.VMEM((PAIRS, 8, ROWS, 2 * count), F32),
            pltpu.VMEM((PAIRS, 3, 8, 32, 2 * count), F32),
            pltpu.VMEM((3, 8, ROWS, count), BF),
            pltpu.VMEM((3, 8, ROWS, count), F32),
            pltpu.VMEM((12, ROWS, count), F32),
            pltpu.VMEM((2, 4, 32, count), F32),
            pltpu.VMEM((2, 4, ROWS, count), F32),
            pltpu.VMEM((ROWS, count), F32),
            pltpu.VMEM((PAIRS, 8, 48, 2 * count), BF),
            pltpu.VMEM((6, 8, ROWS, count), F32),
        ],
        compiler_params=params(20),
        name="fourth",
    )(
        inv_reynolds,
        raw,
        extended,
        ends,
        table,
        local_metric,
        slots,
        got_a,
        got_b,
        const,
    )
    return result.reshape(count)


def solution(mesh):
    return jax.shard_map(
        per_device,
        mesh=mesh,
        in_specs=(
            P(None, None, ("grp", "strm", "azim")),
            P(("strm", "azim"), None),
            P(None, ("strm", "azim")),
            P("grp"),
        ),
        out_specs=P(("grp", "strm", "azim")),
        check_vma=False,
    )
```

```python
import functools

import jax
import jax.numpy as jnp
import numpy as np
from jax import lax
from jax.experimental import pallas as pl
from jax.experimental.pallas import tpu as pltpu
from jax.sharding import PartitionSpec as P

ORDER_IN = 7
ORDER_OUT = 9
EY = 8
EZ = 8
NI = ORDER_IN + 1
NO = ORDER_OUT + 1
HI = NI // 2
HO = NO // 2
ROWS = 128
SEAM_ROWS = ROWS + 2 * 32
GROUPS = sorted({row // 8 * 8 for row in range(HO**3) if row % (HO * HO) < HO})
EXT = NI + 2
SEAM = EXT * NI
BF = jnp.bfloat16
F32 = jnp.float32
PLACE = {3: (0, 0), 4: (0, 1), 5: (1, 0), 0: (1, 1), 1: (2, 0), 2: (2, 1), 6: (3, 0)}
PAIRS = 4
FLIPS = (0, 4, 2, 1)


def gll_table(extent):
    degree = extent - 1
    points = np.cos(np.pi * np.arange(extent) / degree)
    legendre = np.zeros((extent, extent))

    def fill():
        legendre[:, 0] = 1.0
        legendre[:, 1] = points
        for level in range(2, extent):
            legendre[:, level] = (
                (2 * level - 1) * points * legendre[:, level - 1]
                - (level - 1) * legendre[:, level - 2]
            ) / level

    for sweep in range(100):
        fill()
        points = points - (points * legendre[:, degree] - legendre[:, degree - 1]) / (
            extent * legendre[:, degree]
        )
    fill()
    weights = 2.0 / (degree * extent * legendre[:, degree] ** 2)
    return (points[::-1].copy(), weights[::-1].copy())


def lagrange_matrix(source, target):
    result = np.ones((len(target), len(source)))
    for column in range(len(source)):
        for partner in range(len(source)):
            if partner != column:
                result[:, column] *= (target - source[partner]) / (source[column] - source[partner])
    return result


def derivative_matrix(points):
    extent = len(points)
    identity = np.eye(extent)
    spacing = points[:, None] - points[None, :] + identity
    barycen = 1.0 / np.prod(spacing, axis=1)
    matrix = barycen[None, :] / barycen[:, None] / spacing * (1.0 - identity)
    return matrix - identity * matrix.sum(axis=1)[:, None]


def bf16_parts(matrix):
    high = matrix.astype(jnp.bfloat16)
    low = (matrix - high.astype(np.float64)).astype(jnp.bfloat16)
    return high, low


def pad_rows(matrix, rows):
    return np.concatenate([matrix, np.zeros((rows - matrix.shape[0],) + matrix.shape[1:])])


def two_terms(matrix):
    return np.concatenate(bf16_parts(matrix), axis=-1)


@functools.cache
def tables():
    coarse, unused = gll_table(NI)
    fine, weights = gll_table(NO)
    interp = lagrange_matrix(coarse, fine)
    slopes = derivative_matrix(fine)
    ends = np.eye(NO)[:, [0, NO - 1]]
    value = np.concatenate([interp, ends], axis=1)
    both = slopes @ value

    def folded(matrix, parity):
        sign = 1.0 - 2.0 * parity
        if matrix.shape[1] == EXT and matrix is not slopes:
            left = matrix[:HO, [0, 1, 2, 3, 8]]
            right = matrix[:HO, [7, 6, 5, 4, 9]]
        else:
            left = matrix[:HO, :HO]
            right = matrix[:HO, ::-1][:, :HO]
        return left + sign * right

    refine, seams = [], []
    for sector in range(8):
        pa, pb, pc = sector // 4, sector // 2 % 2, sector % 2
        blocks, ends_of = [], []
        for ta, tb, tc in (
            (value, value, value),
            (both, value, value),
            (value, both, value),
            (value, value, both),
        ):
            block = 0.125 * np.einsum(
                "ap,bq,cr->abcrpq", folded(ta, pa), folded(tb, pb), folded(tc, pc)
            ).reshape(HO**3, HO, HO, HO)
            own = np.zeros((HO**3, HO, 24))
            own[:, :, : HO * HI] = block[:, :, :HI].reshape(HO**3, HO, HO * HI)
            own = np.pad(own.reshape(HO**3, -1), ((0, 0), (0, ROWS - 24 * HO)))
            blocks.append(pad_rows(own, ROWS))
            added = np.zeros((HO**3, 48))
            added[:, : 8 * HO] = np.pad(block[:, :, HI], ((0, 0), (0, 0), (0, 3))).reshape(HO**3, -1)
            ends_of.append(added)
        refine.append(two_terms(np.concatenate(blocks)))
        rows = [pad_rows(ends_of[1], ROWS)]
        rows += [pad_rows(ends_of[q][: HO * HO], 32) for q in (2, 3)]
        seams.append(np.pad(two_terms(np.concatenate(rows)), ((0, 0), (0, ROWS - 96))))
    refine = np.stack(refine)
    seams = [np.concatenate(seams[2 * i : 2 * i + 2], axis=1) for i in range(4)]

    second = []
    eye = np.eye(HO)
    for axis in range(3):
        for parity in range(2):
            factors = [eye, eye, eye]
            factors[axis] = folded(slopes, parity)
            block = np.kron(np.kron(factors[0], factors[1]), factors[2])
            edge = ROWS - HO**3
            second.append(two_terms(np.pad(block, ((0, edge), (0, edge)))))
    second = np.stack(second)

    def half(side):
        return value[:HO] if side == 0 else value[::-1][:HO]

    lift_x, lift_y = [], []
    for side in range(2):
        for radial in range(2):
            plain = np.zeros((HO, EXT, HO, NI))
            added = np.zeros((HO, EXT, HO, NI))
            plain[...] = np.einsum("ap,cr->apcr", half(side), half(radial)[:, :NI])
            added[..., 0] = np.einsum("ap,c->apc", half(side), half(radial)[:, NI])
            added[..., NI - 1] = np.einsum("ap,c->apc", half(side), half(radial)[:, NI + 1])
            face = np.stack([plain, added]).transpose(1, 3, 0, 2, 4).reshape(HO, HO, 2 * SEAM)
            lift_x.append(pad_rows(face.reshape(HO * HO, -1), 32))
            spread = np.zeros((HO, HO, HO, 2 * SEAM))
            spread[:, 0] = face
            spread = pad_rows(spread.reshape(HO**3, -1), ROWS)
            lift_y.append(np.concatenate([spread[at : at + 8] for at in GROUPS]))

    def one_term(parts):
        matrix = np.concatenate(parts)
        edge = 2 * ROWS - matrix.shape[1]
        return np.pad(matrix, ((0, 0), (0, edge))).astype(jnp.bfloat16)

    refine = refine.reshape(-1, 2 * ROWS)
    const = np.concatenate(
        seams + [second.reshape(-1, 2 * ROWS), one_term(lift_x), one_term(lift_y)]
    )
    half_weights = [float(v) for v in weights[:HO]]
    line = []
    for end, far in ((0, NO - 1), (NO - 1, 0)):
        weights_in = slopes[end].copy()
        weights_in[[0, NO - 1]] = 0.0
        line.append(([float(v) for v in weights_in @ interp], float(slopes[end, far])))
    ratio = [1.0 / float(both[0, NI] + sign * both[0, NI + 1]) for sign in (1.0, -1.0)]
    ends = (float(slopes[0, 0]), float(slopes[NO - 1, NO - 1]), ratio)
    return refine, const, half_weights, (line, ends)


def dot(a, b, contract_last=False):
    dims = (((1,), (1 if contract_last else 0,)), ((), ()))
    return lax.dot_general(a, b, dims, preferred_element_type=F32)


def is_even(even_ring):
    return lax.rem(lax.axis_index("strm"), 2) == 0 if even_ring else True


def rows3(x):
    return x.reshape(NI, NI, x.shape[-1])


def seam_rows(x):
    return x.reshape(SEAM, x.shape[-1])


def rows2(x):
    return x.reshape(NI * NI, x.shape[-1])


def roll(x, shift):
    count = x.shape[-1]
    return pltpu.roll(x, shift % count, x.ndim - 1)


def positions(shape):
    lane = lax.broadcasted_iota(jnp.int32, shape, len(shape) - 1)
    return lax.div(lane, EY * EZ), lax.rem(lax.div(lane, EZ), EY), lax.rem(lane, EZ)


def split3(x):
    high = x.astype(BF)
    rest = x - high.astype(F32)
    mid = rest.astype(BF)
    low = (rest - mid.astype(F32)).astype(BF)
    return high, mid, low


def radial_added(x):
    axis = x.ndim - 2
    shape = (1,) * axis + x.shape[-2:]
    node = lax.broadcasted_iota(jnp.int32, shape, axis)
    iz = positions(shape)[2]
    last = x.shape[-2] - 1
    before = pltpu.roll(roll(x, 1), 1, axis)
    after = pltpu.roll(roll(x, -1), last, axis)
    low = (node == 0) & (iz > 0)
    high = (node == last) & (iz < EZ - 1)
    other = jnp.where(low, before, jnp.where(high, after, x))
    return 0.5 * (other - x)


def end_lines(line, planes, step):
    (near, near_far), (high, high_far) = line
    first, last = planes[0], planes[-1]
    one = near_far * 0.5 * (last + roll(first, -step))
    two = high_far * 0.5 * (first + roll(last, step))
    for i, plane in enumerate(planes):
        one = one + near[i] * plane
        two = two + high[i] * plane
    return one, two


def chunks(source, target, sem, count=8):
    step = source.shape[0] // count
    return [
        pltpu.make_async_copy(
            source.at[i * step : (i + 1) * step], target.at[i * step : (i + 1) * step], sem.at[i]
        )
        for i in range(count)
    ]


def first_kernel(
    line,
    fields_hbm,
    emap_hbm,
    metric_hbm,
    table_hbm,
    slots_ref,
    metric_out,
    msg_ref,
    fields,
    table_ref,
    emap,
    metric,
    sem,
):
    count = fields.shape[-1]
    order = (3, 5, 4, 0, 1, 2, 6)
    small = [
        pltpu.make_async_copy(emap_hbm, emap, sem.at[7]),
        pltpu.make_async_copy(metric_hbm, metric, sem.at[8]),
    ]
    large = [pltpu.make_async_copy(fields_hbm.at[f], fields.at[f], sem.at[f]) for f in order]
    tables_copies = chunks(table_hbm, table_ref, sem.at[pl.ds(9, 8)])
    for copy in small + large + tables_copies:
        copy.start()
    for copy in small:
        copy.wait()
    local = lax.broadcasted_iota(jnp.int32, (count, count), 0)
    slots = (local == emap[...]).astype(F32).astype(BF)
    slots_ref[...] = slots
    high, mid, low = split3(metric[...])
    pad = jnp.zeros((7, count), F32)
    stacked = jnp.concatenate([high.astype(F32), mid.astype(F32), low.astype(F32), pad], axis=0)
    moved = dot(stacked.astype(BF), slots, True)
    local = moved[0:3] + moved[3:6] + moved[6:9]
    metric_out[...] = jnp.concatenate([local, jnp.zeros((5, count), F32)], axis=0)
    high = local.astype(BF).astype(F32)
    tail = jnp.concatenate([high, local - high, jnp.zeros((10, count), F32)], axis=0)
    msg_ref[9 * 64 : 9 * 64 + 16, :] = tail.astype(BF)
    iy = positions((1, 1, count))[1]
    for f, copy in zip(order, large):
        copy.wait()
        if f in (3, 5):
            values = dot(fields[f], slots, True).reshape(NI, NI, NI, count)
            first, last = values[:, 0], values[:, NI - 1]
        else:
            planes = fields[f].reshape(NI, NI, NI, count)
            planes = jnp.concatenate([planes[:, 0], planes[:, NI - 1]], axis=0)
            planes = dot(planes.reshape(2 * NI * NI, count), slots, True)
            first, last = rows3(planes[0:64]), rows3(planes[64:128])
        face = jnp.where(iy == 0, first, last)
        msg_ref[f * 64 : f * 64 + 64, :] = rows2(face).astype(BF)
        if f in (3, 5):
            low, high = end_lines(line, [values[:, b] for b in range(NI)], EZ)
            at = (7 + (f == 5)) * 64
            msg_ref[at : at + 64, :] = rows2(jnp.where(iy == 0, low, high)).astype(BF)
    for copy in tables_copies:
        copy.wait()


def own_kernel(fields_ref, slots_ref, coarse_ref):
    count = fields_ref.shape[-1]
    for f in range(7):
        values = dot(fields_ref[f], slots_ref[...], True)
        coarse_ref[f] = values.reshape(NI, NI, NI, count)


def from_azim(x, iy):
    gap = (EY - 1) * EZ
    return jnp.where(iy == 0, roll(x, -gap), roll(x, gap))


def metric_classes(x, halo, shift, at_low, at_high):
    low = 0.5 * (x + jnp.where(at_low, halo, roll(x, shift)))
    high = 0.5 * (x + jnp.where(at_high, halo, roll(x, -shift)))
    return [x, low, high]


def radial_classes(x, iz):
    low = jnp.where(iz > 0, 0.5 * (x + roll(x, 1)), x)
    high = jnp.where(iz < EZ - 1, 0.5 * (x + roll(x, -1)), x)
    return [x, low, high]


def second_kernel(
    line, even_ring, coarse_ref, metric_ref, halo_ref, ext_ref, ends_ref, table_ref, a_ref, b_ref
):
    count = coarse_ref.shape[-1]
    layer = EY * EZ
    ix, iy, iz = positions((1, 1, count))
    blocks = []
    lines = []
    for f in range(7):
        values = coarse_ref[f]
        first, last = values[:, 0], values[:, NI - 1]
        halo = from_azim(rows3(halo_ref[f * 64 : f * 64 + 64, :].astype(F32)), iy)
        low = 0.5 * (jnp.where(iy == 0, halo, roll(last, EZ)) - first)
        high = 0.5 * (jnp.where(iy == EY - 1, halo, roll(first, -EZ)) - last)
        values = jnp.concatenate([values, low[:, None], high[:, None]], axis=1)
        ext_ref[f] = values
        blocks.append(seam_rows(jnp.where(ix == 0, values[0], values[NI - 1])))
        if f in (4, 5):
            low, high = end_lines(line, [values[a] for a in range(NI)], layer)
            lines.append(seam_rows(jnp.where(ix == 0, low, high)))
    blocks += lines
    extra = []
    for i in range(2):
        ends = from_azim(rows3(halo_ref[(7 + i) * 64 : (8 + i) * 64, :].astype(F32)), iy)
        ends_ref[i] = ends
        extra.append(jnp.where(ix[0] == 0, ends[0], ends[NI - 1]))

    ix, iy, iz = positions((1, count))
    packed = halo_ref[9 * 64 : 9 * 64 + 16, :].astype(F32)
    other = from_azim(packed[0:3] + packed[3:6], iy)
    own = metric_ref[...]
    lows, highs = iy == 0, iy == EY - 1
    rows = []
    for item in metric_classes(own[0:1], other[0:1], EZ, lows, highs):
        rows += radial_classes(item, iz)
    rows += radial_classes(own[1:2], iz)
    rows += metric_classes(own[2:3], other[2:3], EZ, lows, highs)
    rows += radial_classes(other[1:2], iz)
    table = jnp.concatenate(rows + [jnp.zeros((24 - len(rows), count), F32)], axis=0)
    table_ref[...] = table
    high = table.astype(BF).astype(F32)
    spare = jnp.zeros((SEAM - 64, count), F32)
    blocks.append(jnp.concatenate(extra + [high, table - high, spare], axis=0))

    ix = positions((SEAM, count))[0]
    even = is_even(even_ring)
    half = len(blocks) // 2
    for i in range(half):
        one, two = blocks[i], blocks[half + i]
        down = jnp.where(ix == 0, one, roll(two, layer))
        up = jnp.where(ix == 0, roll(one, layer), two)
        rows = slice(i * SEAM, (i + 1) * SEAM)
        a_ref[rows, :] = jnp.where(even, up, down).astype(BF)
        b_ref[rows, :] = jnp.where(even, down, up).astype(BF)


def signed(one, two, parity):
    return one + two if parity == 0 else one - two


def radial_fold(rows, iz, parity):
    last = NI - 1
    low = jnp.where(iz > 0, roll(rows[last], 1) - rows[0], 0.0)
    high = jnp.where(iz < EZ - 1, roll(rows[0], -1) - rows[last], 0.0)
    return [signed(rows[c], rows[last - c], parity) for c in range(HI)] + [
        0.5 * signed(low, high, parity)
    ]


def azim_fold(plane, parity):
    return [
        signed(
            plane[b if b < HI else NI], plane[NI - 1 - b if b < HI else NI + 1], parity
        )
        for b in range(HO)
    ]


def row_kinds(count):
    row = lax.broadcasted_iota(jnp.int32, (ROWS, count), 0)
    return row, row < HO * HO, lax.rem(row, HO * HO) < HO, lax.rem(row, HO) == 0


def line_of(source, at):
    return source[at : at + 1]


def row_tables(weights, table, factor_ref, quad_ref):
    count = table.shape[-1]
    row, a_edge, b_edge, c_edge = row_kinds(count)

    def weight_of(index):
        result = jnp.full((ROWS, count), weights[0], F32)
        for i in range(1, HO):
            result = jnp.where(index == i, weights[i], result)
        return result

    a_pos = lax.div(row, HO * HO)
    b_pos = lax.rem(lax.div(row, HO), HO)
    quad = weight_of(a_pos) * weight_of(b_pos) * weight_of(lax.rem(row, HO))
    quad_ref[...] = jnp.where(row < HO**3, quad, 0.0)

    def by_radius(at, side):
        return jnp.where(c_edge, line_of(table, at + 1 + side), line_of(table, at))

    for one in range(2):
        for two in range(2):
            at = one * 2 + two
            factor_ref[at] = jnp.where(b_edge, by_radius(3 + 3 * one, two), by_radius(0, two))
            factor_ref[4 + at] = by_radius(9, two)
            factor_ref[8 + at] = jnp.where(b_edge, line_of(table, 13 + two), line_of(table, 12))


def third_kernel(
    weights,
    ext_ref,
    table_ref,
    const_ref,
    later_hbm,
    gs_ref,
    later_ref,
    factor_ref,
    quad_ref,
    tmp_ref,
    xs_ref,
    sem,
):
    count = ext_ref.shape[-1]
    width = HO * HI
    iz = positions((width, count))[2]
    zeros = jnp.zeros((HI, count), F32)

    copies = chunks(later_hbm, later_ref, sem)
    for copy in copies:
        copy.start()
    row_tables(weights, table_ref[...], factor_ref, quad_ref)
    for f in range(7):
        pair, side = PLACE[f]
        lanes = slice(side * count, (side + 1) * count)
        values = ext_ref[f]
        for pa in range(2):
            mixed = [signed(values[a], values[NI - 1 - a], pa) for a in range(HI)]
            for pb in range(2):
                at = f % 2 * 4 + pa * 2 + pb
                for a in range(HI):
                    for b, item in enumerate(azim_fold(mixed[a], pb)):
                        row = (a * HO + b) * NI
                        tmp_ref[at, row : row + NI, :] = item
                main = [tmp_ref[at, pl.ds(c, width, stride=NI), :] for c in range(NI)]
                for pc in range(2):
                    rows = []
                    for item in radial_fold(main, iz, pc):
                        rows += [item, zeros]
                    rows.append(jnp.zeros((8, count), F32))
                    operand = jnp.concatenate(rows, axis=0).astype(BF)
                    xs_ref[pair, pa * 4 + pb * 2 + pc, :, lanes] = operand

    def refine(sector, carry):
        for pair in range(PAIRS):
            width = 2 * count if pair < PAIRS - 1 else count
            source = xs_ref[pair, sector, :, 0:width]
            source = jnp.concatenate([source, source], axis=0)
            for q in range(0 if pair < PAIRS - 1 else 1, 4):
                rows = pl.ds(sector * 4 * ROWS + q * ROWS, ROWS)
                gs_ref[pair, q, sector ^ FLIPS[q], :, 0:width] = dot(const_ref[rows, :], source)
        return carry

    lax.fori_loop(0, 8, refine, 0, unroll=2)
    for copy in copies:
        copy.wait()


def fourth_kernel(
    ends_value,
    even_ring,
    inv_ref,
    gs_ref,
    factor_ref,
    quad_ref,
    ext_ref,
    ends_ref,
    table_ref,
    metric_ref,
    slots_ref,
    ra_ref,
    rb_ref,
    const_ref,
    out_ref,
    tmp_ref,
    along_ref,
    edge_ref,
    vort_ref,
    linear_ref,
    edge_factor_ref,
    normal_x_ref,
    normal_y_ref,
    xt_ref,
    nodal_ref,
):
    count = ext_ref.shape[-1]
    layer = EY * EZ
    even = is_even(even_ring)
    ix = positions((SEAM, count))[0]
    end_low, end_high, value_of_slope = ends_value
    seam_at = 0
    second_at = seam_at + 4 * SEAM_ROWS
    lift_x_at = second_at + 6 * ROWS
    lift_y_at = lift_x_at + ROWS

    halves = []
    for i in range(5):
        rows = slice(i * SEAM, (i + 1) * SEAM)
        one = ra_ref[rows, :].astype(F32)
        two = rb_ref[rows, :].astype(F32)
        down = jnp.where(even, two, one)
        up = jnp.where(even, one, two)
        halves.append(
            (
                jnp.where(ix == 0, down, roll(up, layer)),
                jnp.where(ix == 0, roll(down, layer), up),
            )
        )
    blocks = [item[0] for item in halves] + [item[1] for item in halves]

    ix3 = positions((1, 1, count))[0]
    iz8 = positions((NI, count))[2]

    def stream_added(first, last, halo):
        lane = positions((1,) * (first.ndim - 1) + (count,))[0]
        low = 0.5 * (jnp.where(lane == 0, halo, roll(last, layer)) - first)
        high = 0.5 * (jnp.where(lane == 0, roll(first, -layer), halo) - last)
        return low, high

    seam = {}
    tmp_ref[...] = jnp.zeros(tmp_ref.shape, F32)
    for f in range(7):
        pair, side = PLACE[f]
        lanes = slice(side * count, (side + 1) * count)
        halo = blocks[f].reshape(EXT, NI, count)
        first, last = ext_ref[f, 0], ext_ref[f, NI - 1]
        low, high = stream_added(first, last, halo)
        if f in (4, 5):
            seam[f] = seam_rows(jnp.where(ix3 == 0, first + low, last + high))
        for pa in range(2):
            mixed = signed(low, high, pa)
            for pb in range(2):
                at = f % 2 * 4 + pa * 2 + pb
                for b, item in enumerate(azim_fold(mixed, pb)):
                    tmp_ref[at, b * NI : (b + 1) * NI, :] = item
                main = [tmp_ref[at, pl.ds(c, NI, stride=NI), :] for c in range(NI)]
                for pc in range(2):
                    rows = radial_fold(main, iz8, pc)
                    rows.append(jnp.zeros((NI, count), F32))
                    operand = jnp.concatenate(rows, axis=0).astype(BF)
                    xt_ref[pair, pa * 4 + pb * 2 + pc, :, lanes] = operand

    first_nodes = lax.broadcasted_iota(jnp.int32, (32, 2 * count), 0) < HO * HO

    def refine_seam(pa, pb, pc):
        sector = pa * 4 + pb * 2 + pc
        at = seam_at + (sector // 2) * SEAM_ROWS
        matrix = const_ref[at : at + SEAM_ROWS, pc * ROWS : pc * ROWS + 2 * 48]
        for pair in range(PAIRS):
            width = 2 * count if pair < PAIRS - 1 else count
            source = xt_ref[pair, sector, :, 0:width]
            added = dot(matrix, jnp.concatenate([source, source], axis=0))
            target = sector ^ 4
            along_ref[pair, target, :, 0:width] = (
                gs_ref[pair, 1, target, :, 0:width] + added[0:ROWS]
            )
            for q, slot in ((0, 0), (2, 1), (3, 2)):
                if q or pair < PAIRS - 1:
                    at = ROWS + 32 * (slot - 1) if q else 0
                    more = added[at : at + 32]
                    if q == 0:
                        more = jnp.where(first_nodes[:, 0:width], more * value_of_slope[pa], 0.0)
                    target = sector ^ FLIPS[q]
                    edge_ref[pair, slot, target, :, 0:width] = (
                        gs_ref[pair, q, target, 0:32, 0:width] + more
                    )

    for sector in range(8):
        refine_seam(sector // 4, sector // 2 % 2, sector % 2)

    row, a_edge, b_edge, c_edge = row_kinds(count)

    table = table_ref[...]
    packed = blocks[9]
    theirs = packed[16:40] + packed[40:64]
    lane_ix = positions((24, count))[0]
    at_low = 0.5 * (table + jnp.where(lane_ix == 0, theirs, roll(table, layer)))
    at_high = 0.5 * (table + jnp.where(lane_ix == 0, roll(table, -layer), theirs))

    def by_radius(source, at, side):
        return jnp.where(c_edge, line_of(source, at + 1 + side), line_of(source, at))

    for one in range(2):
        edge = at_low if one == 0 else at_high
        for two in range(2):
            at = one * 2 + two
            outside = by_radius(edge, 9, two)[0:32]
            edge_factor_ref[at] = jnp.where(a_edge[0:32], outside, factor_ref[4 + at, 0:32, :])
            outside = jnp.where(b_edge[0:32], line_of(edge, 13 + two), line_of(edge, 12))
            edge_factor_ref[4 + at] = jnp.where(a_edge[0:32], outside, factor_ref[8 + at, 0:32, :])

    def with_added(parts):
        halves = []
        for part in parts:
            stacked = part.reshape(EXT, NI, count)
            halves.append(jnp.concatenate([part, seam_rows(radial_added(stacked))], axis=0))
        return jnp.concatenate(halves, axis=1).astype(BF)

    def lift(at, rows, operand):
        return dot(const_ref[at : at + rows, 0 : 2 * SEAM], operand)

    stream = []
    for i in range(2):
        shared = jnp.where(ix == 0, end_high, end_low) * seam[4 + i]
        stream.append(blocks[7 + i] + shared)
    lifted = lift(lift_x_at, ROWS, with_added(stream))
    for one in range(2):
        for two in range(2):
            at = one * 2 + two
            scale = jnp.where(
                b_edge, by_radius(theirs, 3 + 3 * one, two), by_radius(theirs, 0, two)
            )[0:32]
            for i in range(2):
                part = lifted[at * 32 : at * 32 + 32, i * count : (i + 1) * count]
                normal_x_ref[i, at] = part * scale

    iy3 = positions((1, 1, count))[1]
    iy2 = iy3[0]
    azim = []
    for i, f in enumerate((3, 5)):
        factor = jnp.where(iy3 == 0, end_high, end_low)
        values = ext_ref[f]
        halo = blocks[f].reshape(EXT, NI, count)
        near = jnp.where(
            iy3 == 0, values[:, 0] + values[:, NI], values[:, NI - 1] + values[:, NI + 1]
        )
        own = ends_ref[i] + factor * near
        near = jnp.where(iy2 == 0, halo[0] + halo[NI], halo[NI - 1] + halo[NI + 1])
        other = blocks[9][8 * i : 8 * i + 8] + factor[0] * near
        low, high = stream_added(own[0], own[NI - 1], other)
        azim.append(jnp.concatenate([rows2(own), low, high], axis=0))
    span = 8 * len(GROUPS)
    lifted = lift(lift_y_at, 4 * span, with_added(azim))
    for one in range(2):
        edge = at_low if one == 0 else at_high
        for two in range(2):
            at = one * 2 + two
            scale = jnp.where(a_edge, by_radius(edge, 15, two), by_radius(table, 15, two))
            for i in range(2):
                for k, start in enumerate(GROUPS):
                    rows = slice(at * span + 8 * k, at * span + 8 * k + 8)
                    part = lifted[rows, i * count : (i + 1) * count]
                    normal_y_ref[i, at, start : start + 8] = part * scale[start : start + 8]

    def parts_of(f, q, at, edge):
        pair, side = PLACE[f]
        lanes = slice(side * count, (side + 1) * count)
        if q == 1:
            return [along_ref[pair, sector, at, lanes] for sector in range(8)]
        if edge:
            slot = (0, None, 1, 2)[q]
            return [edge_ref[pair, slot, sector, at, lanes] for sector in range(8)]
        return [gs_ref[pair, q, sector, at, lanes] for sector in range(8)]

    chunk = 16

    def vorticity(at, start, edge):
        shape = (chunk, count)
        lane_ix, lane_iy, lane_iz = positions(shape)
        rows = lax.broadcasted_iota(jnp.int32, shape, 0) + start
        on_a = rows < HO * HO
        on_b = lax.rem(rows, HO * HO) < HO
        on_c = lax.rem(rows, HO) == 0

        def factor_at(which):
            if edge and which >= 4:
                return edge_factor_ref[which - 4, at, :]
            return factor_ref[which, at, :]

        def nodal(f, q, factor):
            g = unfold(parts_of(f, q, at, edge))
            for s in range(8):
                nodal_ref[kept(f - 3, q - 1), s, at, :] = g[s]
            return [g[s] * factor_at(factor(s)) for s in range(8)]

        def along_x(i, f):
            g = nodal(f, 1, lambda s: s % 4)
            if edge:
                for two in range(4):
                    low, high = g[two], g[4 + two]
                    normal = normal_x_ref[i, two, at, :]
                    near = lane_ix == 0
                    first = 0.5 * (low + jnp.where(near, normal, roll(high, layer)))
                    last = 0.5 * (high + jnp.where(near, roll(low, -layer), normal))
                    g[two] = jnp.where(on_a, first, low)
                    g[4 + two] = jnp.where(on_a, last, high)
            return g

        def along_y(i, f):
            g = nodal(f, 2, lambda s: 4 + s // 4 * 2 + s % 2)
            for two in range(4):
                here = two // 2 * 4 + two % 2
                low, high = g[here], g[here + 2]
                normal = normal_y_ref[i, two, at, :]
                first = 0.5 * (low + jnp.where(lane_iy == 0, normal, roll(high, EZ)))
                last = 0.5 * (high + jnp.where(lane_iy == EY - 1, normal, roll(low, -EZ)))
                g[here] = jnp.where(on_b, first, low)
                g[here + 2] = jnp.where(on_b, last, high)
            return g

        def along_z(f):
            g = nodal(f, 3, lambda s: 8 + s // 2)
            lower = on_c & (lane_iz > 0)
            upper = on_c & (lane_iz < EZ - 1)
            for two in range(4):
                low, high = g[2 * two], g[2 * two + 1]
                g[2 * two] = jnp.where(lower, 0.5 * (low + roll(high, 1)), low)
                g[2 * two + 1] = jnp.where(upper, 0.5 * (high + roll(low, -1)), high)
            return g

        pairs = (
            (lambda: along_y(1, 5), lambda: along_z(4)),
            (lambda: along_z(3), lambda: along_x(1, 5)),
            (lambda: along_x(0, 4), lambda: along_y(0, 3)),
        )
        for i, (plus, minus) in enumerate(pairs):
            one, two = plus(), minus()
            folded = unfold([0.125 * (one[s] - two[s]) for s in range(8)])
            for sector in range(8):
                vort_ref[i, sector, at, :] = folded[sector].astype(BF)

    for step in range(2):
        vorticity(slice(step * chunk, (step + 1) * chunk), step * chunk, True)

    def vorticity_step(step, carry):
        start = pl.multiple_of(step * chunk, chunk)
        vorticity(pl.ds(start, chunk), start, False)
        return carry

    lax.fori_loop(2, ROWS // chunk, vorticity_step, 0)

    metric = [metric_ref[i : i + 1] for i in range(3)]
    inv = inv_ref[0]
    scaled = [inv * metric[i] for i in range(3)]
    taken = ((1, 2), (2, 0), (0, 1))
    terms = (((1, 0), (2, 1)), ((2, 0), (0, 1)), ((0, 0), (1, 1)))
    for target in range(8):
        slope = []
        for axis in range(3):
            flip = FLIPS[1 + axis]
            sector = target ^ flip
            source = jnp.concatenate([vort_ref[i, sector] for i in taken[axis]], axis=1)
            source = jnp.concatenate([source, source], axis=0)
            at = second_at + (2 * axis + (1 if sector & flip else 0)) * ROWS
            slope.append(dot(const_ref[at : at + ROWS, :], source))
        for i in range(3):
            (one, half), (two, other) = terms[i]
            plus = scaled[one] * slope[one][:, half * count : (half + 1) * count]
            minus = scaled[two] * slope[two][:, other * count : (other + 1) * count]
            if i == 0:
                linear_ref[i, target] = along_ref[3, target, :, 0:count] * metric[0] + (plus - minus)
            else:
                near = edge_ref[3, i, target, :, 0:count] * metric[i]
                far = gs_ref[3, 1 + i, target, 32:, 0:count] * metric[i]
                linear_ref[i, target, 0:32, :] = near + (plus - minus)[0:32]
                linear_ref[i, target, 32:, :] = far + (plus - minus)[32:]

    def body(edge, step, total):
        at = pl.ds(pl.multiple_of(step * 8, 8), 8)
        for side in range(2):
            total = total + quad_ref[at, :] * energy_of(at, side, edge)
        return total

    def energy_of(at, side, edge):
        def unfold_half(parts):
            return unfold4([signed(parts[s], parts[4 + s], side) for s in range(4)])

        def part(f, q):
            return unfold_half(parts_of(f, q, at, edge))

        base = [[item * metric[j] for item in part(j, 0)] for j in range(3)]
        dual = [part(3 + j, 0) for j in range(3)]
        energy = spread = None
        for i in range(3):
            total = unfold_half([linear_ref[i, s, at, :] for s in range(8)])
            for j in range(3):
                if i == j:
                    slope = part(3 + i, 1 + j)
                else:
                    slope = [nodal_ref[kept(i, j), side * 4 + s, at, :] for s in range(4)]
                total = [total[s] - base[j][s] * slope[s] for s in range(4)]
                if i == j:
                    more = [slope[s] * metric[i] for s in range(4)]
                    spread = more if i == 0 else [spread[s] + more[s] for s in range(4)]
            inner = None
            for j in range(3):
                slope = part(j, 1 + i)
                more = [dual[j][s] * slope[s] for s in range(4)]
                inner = more if j == 0 else [inner[s] + more[s] for s in range(4)]
            total = [total[s] + metric[i] * inner[s] for s in range(4)]
            more = [item * item for item in total]
            energy = more if i == 0 else [energy[s] + more[s] for s in range(4)]
        energy = [energy[s] + spread[s] * spread[s] for s in range(4)]
        return (energy[0] + energy[1]) + (energy[2] + energy[3])

    total = jnp.zeros((8, count), F32)
    total = lax.fori_loop(0, 4, functools.partial(body, True), total, unroll=2)
    total = lax.fori_loop(4, ROWS // 8, functools.partial(body, False), total, unroll=2)
    weighted = jnp.sum(total, axis=0, keepdims=True)
    result = jnp.sqrt(weighted / 8.0) / float(ORDER_OUT**2)
    high, mid, low = split3(result)
    stacked = jnp.concatenate(
        [high.astype(F32), mid.astype(F32), low.astype(F32), jnp.zeros((13, count), F32)], axis=0
    )
    moved = dot(stacked.astype(BF), slots_ref[...])
    out_ref[...] = moved[0:1] + moved[1:2] + moved[2:3]


def kept(component, axis):
    return component * 2 + (axis if axis < component else axis - 1)


def unfold4(parts):
    plus0, minus0 = parts[0] + parts[1], parts[0] - parts[1]
    plus1, minus1 = parts[2] + parts[3], parts[2] - parts[3]
    return [plus0 + plus1, minus0 + minus1, plus0 - plus1, minus0 - minus1]


def unfold(parts):
    plus = unfold4([parts[s] + parts[4 + s] for s in range(4)])
    minus = unfold4([parts[s] - parts[4 + s] for s in range(4)])
    return plus + minus


MIB = 1024 * 1024


def per_device(fields, elem_map, metric, inv_reynolds):
    refine, const, weights, (line, ends_value) = tables()
    count = fields.shape[-1]
    vmem = pl.BlockSpec(memory_space=pltpu.VMEM)

    def params(mib):
        return pltpu.CompilerParams(vmem_limit_bytes=mib * MIB)

    def struct(shape, dtype=F32):
        return jax.ShapeDtypeStruct(shape, dtype)

    hbm = pl.BlockSpec(memory_space=pltpu.HBM)
    inputs = [
        pltpu.with_memory_space_constraint(item, pltpu.HBM)
        for item in (fields, elem_map, metric, jnp.asarray(refine), jnp.asarray(const))
    ]
    slots, local_metric, message, near_fields, refine = pl.pallas_call(
        functools.partial(first_kernel, line),
        out_shape=(
            struct((count, count), BF),
            struct((8, count)),
            struct((9 * 64 + 16, count), BF),
            struct(fields.shape, BF),
            struct(refine.shape, BF),
        ),
        in_specs=[hbm] * 4,
        out_specs=(vmem,) * 5,
        scratch_shapes=[
            pltpu.VMEM(elem_map.shape, jnp.int32),
            pltpu.VMEM(metric.shape, F32),
            pltpu.SemaphoreType.DMA((17,)),
        ],
        compiler_params=params(6),
        name="first",
    )(*inputs[:4])

    coarse = pl.pallas_call(
        own_kernel,
        out_shape=struct((7, NI, NI, NI, count)),
        in_specs=[vmem] * 2,
        out_specs=vmem,
        compiler_params=params(6),
        cost_estimate=pl.CostEstimate(
            flops=2 * fields.size * count, bytes_accessed=3 * 10**6, transcendentals=0
        ),
        name="own",
    )(near_fields, slots)

    azim = lax.axis_size("azim")
    if azim == 2:
        halo = lax.ppermute(message, "azim", [(0, 1), (1, 0)])
    else:
        ahead = lax.ppermute(message, "azim", [(i, (i + 1) % azim) for i in range(azim)])
        behind = lax.ppermute(message, "azim", [((i + 1) % azim, i) for i in range(azim)])
        iy = (jnp.arange(count) // EZ) % EY
        halo = jnp.where(iy >= EY // 2, ahead, behind)

    streams = lax.axis_size("strm")
    even_ring = streams % 2 == 0
    extended, ends, table, to_a, to_b = pl.pallas_call(
        functools.partial(second_kernel, line, even_ring),
        out_shape=(
            struct((7, NI, EXT, NI, count)),
            struct((2, NI, NI, count)),
            struct((24, count)),
            struct((5 * SEAM, count), BF),
            struct((5 * SEAM, count), BF),
        ),
        in_specs=[vmem] * 3,
        out_specs=(vmem,) * 5,
        compiler_params=params(12),
        name="second",
    )(coarse, local_metric, halo)

    if even_ring:
        near = [(i, i ^ 1) for i in range(streams)]
        far = []
        for i in range(1, streams, 2):
            far += [(i, (i + 1) % streams), ((i + 1) % streams, i)]
        got_a = lax.ppermute(to_a, "strm", near)
        got_b = lax.ppermute(to_b, "strm", far)
    else:
        got_b = lax.ppermute(to_a, "strm", [(i, (i + 1) % streams) for i in range(streams)])
        got_a = lax.ppermute(to_b, "strm", [((i + 1) % streams, i) for i in range(streams)])

    raw, const, factor, quad = pl.pallas_call(
        functools.partial(third_kernel, weights),
        out_shape=(
            struct((PAIRS, 4, 8, ROWS, 2 * count)),
            struct(const.shape, BF),
            struct((12, ROWS, count)),
            struct((ROWS, count)),
        ),
        in_specs=[vmem] * 3 + [hbm],
        out_specs=(vmem,) * 4,
        scratch_shapes=[
            pltpu.VMEM((8, HO * HI * NI, count), F32),
            pltpu.VMEM((PAIRS, 8, ROWS, 2 * count), BF),
            pltpu.SemaphoreType.DMA((8,)),
        ],
        compiler_params=params(8),
        cost_estimate=pl.CostEstimate(
            flops=4 * 10**9, bytes_accessed=20 * 10**6, transcendentals=0
        ),
        name="third",
    )(extended, table, refine, inputs[4])

    result = pl.pallas_call(
        functools.partial(fourth_kernel, ends_value, even_ring),
        out_shape=struct((1, count)),
        in_specs=[pl.BlockSpec(memory_space=pltpu.SMEM)] + [vmem] * 11,
        out_specs=vmem,
        scratch_shapes=[
            pltpu.VMEM((8, NI * NI, count), F32),
            pltpu.VMEM((PAIRS, 8, ROWS, 2 * count), F32),
            pltpu.VMEM((PAIRS, 3, 8, 32, 2 * count), F32),
            pltpu.VMEM((3, 8, ROWS, count), BF),
            pltpu.VMEM((3, 8, ROWS, count), F32),
            pltpu.VMEM((8, 32, count), F32),
            pltpu.VMEM((2, 4, 32, count), F32),
            pltpu.VMEM((2, 4, ROWS, count), F32),
            pltpu.VMEM((PAIRS, 8, 48, 2 * count), BF),
            pltpu.VMEM((6, 8, ROWS, count), F32),
        ],
        compiler_params=params(20),
        name="fourth",
    )(
        inv_reynolds,
        raw,
        factor,
        quad,
        extended,
        ends,
        table,
        local_metric,
        slots,
        got_a,
        got_b,
        const,
    )
    return result.reshape(count)


def solution(mesh):
    return jax.shard_map(
        per_device,
        mesh=mesh,
        in_specs=(
            P(None, None, ("grp", "strm", "azim")),
            P(("strm", "azim"), None),
            P(None, ("strm", "azim")),
            P("grp"),
        ),
        out_specs=P(("grp", "strm", "azim")),
        check_vma=False,
    )
```

```python
import functools

import jax
import jax.numpy as jnp
import numpy as np
from jax import lax
from jax.experimental import pallas as pl
from jax.experimental.pallas import tpu as pltpu
from jax.sharding import PartitionSpec as P

ORDER_IN = 7
ORDER_OUT = 9
EY = 8
EZ = 8
NI = ORDER_IN + 1
NO = ORDER_OUT + 1
HI = NI // 2
HO = NO // 2
ROWS = 128
SEAM_ROWS = ROWS + 2 * 32
GROUPS = sorted({row // 8 * 8 for row in range(HO**3) if row % (HO * HO) < HO})
EXT = NI + 2
SEAM = EXT * NI
BF = jnp.bfloat16
F32 = jnp.float32
PLACE = {3: (0, 0), 4: (0, 1), 5: (1, 0), 0: (1, 1), 1: (2, 0), 2: (2, 1), 6: (3, 0)}
PAIRS = 4
FLIPS = (0, 4, 2, 1)


def gll_table(extent):
    degree = extent - 1
    points = np.cos(np.pi * np.arange(extent) / degree)
    legendre = np.zeros((extent, extent))

    def fill():
        legendre[:, 0] = 1.0
        legendre[:, 1] = points
        for level in range(2, extent):
            legendre[:, level] = (
                (2 * level - 1) * points * legendre[:, level - 1]
                - (level - 1) * legendre[:, level - 2]
            ) / level

    for sweep in range(100):
        fill()
        points = points - (points * legendre[:, degree] - legendre[:, degree - 1]) / (
            extent * legendre[:, degree]
        )
    fill()
    weights = 2.0 / (degree * extent * legendre[:, degree] ** 2)
    return (points[::-1].copy(), weights[::-1].copy())


def lagrange_matrix(source, target):
    result = np.ones((len(target), len(source)))
    for column in range(len(source)):
        for partner in range(len(source)):
            if partner != column:
                result[:, column] *= (target - source[partner]) / (source[column] - source[partner])
    return result


def derivative_matrix(points):
    extent = len(points)
    identity = np.eye(extent)
    spacing = points[:, None] - points[None, :] + identity
    barycen = 1.0 / np.prod(spacing, axis=1)
    matrix = barycen[None, :] / barycen[:, None] / spacing * (1.0 - identity)
    return matrix - identity * matrix.sum(axis=1)[:, None]


def bf16_parts(matrix):
    high = matrix.astype(jnp.bfloat16)
    low = (matrix - high.astype(np.float64)).astype(jnp.bfloat16)
    return high, low


def pad_rows(matrix, rows):
    return np.concatenate([matrix, np.zeros((rows - matrix.shape[0],) + matrix.shape[1:])])


def two_terms(matrix):
    return np.concatenate(bf16_parts(matrix), axis=-1)


@functools.cache
def tables():
    coarse, unused = gll_table(NI)
    fine, weights = gll_table(NO)
    interp = lagrange_matrix(coarse, fine)
    slopes = derivative_matrix(fine)
    ends = np.eye(NO)[:, [0, NO - 1]]
    value = np.concatenate([interp, ends], axis=1)
    both = slopes @ value

    def folded(matrix, parity):
        sign = 1.0 - 2.0 * parity
        if matrix.shape[1] == EXT and matrix is not slopes:
            left = matrix[:HO, [0, 1, 2, 3, 8]]
            right = matrix[:HO, [7, 6, 5, 4, 9]]
        else:
            left = matrix[:HO, :HO]
            right = matrix[:HO, ::-1][:, :HO]
        return left + sign * right

    refine, seams = [], []
    for sector in range(8):
        pa, pb, pc = sector // 4, sector // 2 % 2, sector % 2
        blocks, ends_of = [], []
        for ta, tb, tc in (
            (value, value, value),
            (both, value, value),
            (value, both, value),
            (value, value, both),
        ):
            block = 0.125 * np.einsum(
                "ap,bq,cr->abcrpq", folded(ta, pa), folded(tb, pb), folded(tc, pc)
            ).reshape(HO**3, HO, HO, HO)
            own = np.zeros((HO**3, HO, 24))
            own[:, :, : HO * HI] = block[:, :, :HI].reshape(HO**3, HO, HO * HI)
            own = np.pad(own.reshape(HO**3, -1), ((0, 0), (0, ROWS - 24 * HO)))
            blocks.append(pad_rows(own, ROWS))
            added = np.zeros((HO**3, 48))
            added[:, : 8 * HO] = np.pad(block[:, :, HI], ((0, 0), (0, 0), (0, 3))).reshape(HO**3, -1)
            ends_of.append(added)
        refine.append(two_terms(np.concatenate(blocks)))
        rows = [pad_rows(ends_of[1], ROWS)]
        rows += [pad_rows(ends_of[q][: HO * HO], 32) for q in (2, 3)]
        seams.append(np.pad(two_terms(np.concatenate(rows)), ((0, 0), (0, ROWS - 96))))
    refine = np.stack(refine)
    seams = [np.concatenate(seams[2 * i : 2 * i + 2], axis=1) for i in range(4)]

    second = []
    eye = np.eye(HO)
    for axis in range(3):
        for parity in range(2):
            factors = [eye, eye, eye]
            factors[axis] = folded(slopes, parity)
            block = np.kron(np.kron(factors[0], factors[1]), factors[2])
            edge = ROWS - HO**3
            second.append(two_terms(np.pad(block, ((0, edge), (0, edge)))))
    second = np.stack(second)

    def half(side):
        return value[:HO] if side == 0 else value[::-1][:HO]

    lift_x, lift_y = [], []
    for side in range(2):
        for radial in range(2):
            plain = np.zeros((HO, EXT, HO, NI))
            added = np.zeros((HO, EXT, HO, NI))
            plain[...] = np.einsum("ap,cr->apcr", half(side), half(radial)[:, :NI])
            added[..., 0] = np.einsum("ap,c->apc", half(side), half(radial)[:, NI])
            added[..., NI - 1] = np.einsum("ap,c->apc", half(side), half(radial)[:, NI + 1])
            face = np.stack([plain, added]).transpose(1, 3, 0, 2, 4).reshape(HO, HO, 2 * SEAM)
            lift_x.append(pad_rows(face.reshape(HO * HO, -1), 32))
            spread = np.zeros((HO, HO, HO, 2 * SEAM))
            spread[:, 0] = face
            spread = pad_rows(spread.reshape(HO**3, -1), ROWS)
            lift_y.append(np.concatenate([spread[at : at + 8] for at in GROUPS]))

    def one_term(parts):
        matrix = np.concatenate(parts)
        edge = 2 * ROWS - matrix.shape[1]
        return np.pad(matrix, ((0, 0), (0, edge))).astype(jnp.bfloat16)

    refine = refine.reshape(-1, 2 * ROWS)
    const = np.concatenate(
        seams + [second.reshape(-1, 2 * ROWS), one_term(lift_x), one_term(lift_y)]
    )
    half_weights = [float(v) for v in weights[:HO]]
    line = []
    for end, far in ((0, NO - 1), (NO - 1, 0)):
        weights_in = slopes[end].copy()
        weights_in[[0, NO - 1]] = 0.0
        line.append(([float(v) for v in weights_in @ interp], float(slopes[end, far])))
    ratio = [1.0 / float(both[0, NI] + sign * both[0, NI + 1]) for sign in (1.0, -1.0)]
    ends = (float(slopes[0, 0]), float(slopes[NO - 1, NO - 1]), ratio)
    return refine, const, half_weights, (line, ends)


def dot(a, b, contract_last=False):
    dims = (((1,), (1 if contract_last else 0,)), ((), ()))
    return lax.dot_general(a, b, dims, preferred_element_type=F32)


def is_even(even_ring):
    return lax.rem(lax.axis_index("strm"), 2) == 0 if even_ring else True


def rows3(x):
    return x.reshape(NI, NI, x.shape[-1])


def seam_rows(x):
    return x.reshape(SEAM, x.shape[-1])


def rows2(x):
    return x.reshape(NI * NI, x.shape[-1])


def roll(x, shift):
    count = x.shape[-1]
    return pltpu.roll(x, shift % count, x.ndim - 1)


def positions(shape):
    lane = lax.broadcasted_iota(jnp.int32, shape, len(shape) - 1)
    return lax.div(lane, EY * EZ), lax.rem(lax.div(lane, EZ), EY), lax.rem(lane, EZ)


def split3(x):
    high = x.astype(BF)
    rest = x - high.astype(F32)
    mid = rest.astype(BF)
    low = (rest - mid.astype(F32)).astype(BF)
    return high, mid, low


def radial_added(x):
    axis = x.ndim - 2
    shape = (1,) * axis + x.shape[-2:]
    node = lax.broadcasted_iota(jnp.int32, shape, axis)
    iz = positions(shape)[2]
    last = x.shape[-2] - 1
    before = pltpu.roll(roll(x, 1), 1, axis)
    after = pltpu.roll(roll(x, -1), last, axis)
    low = (node == 0) & (iz > 0)
    high = (node == last) & (iz < EZ - 1)
    other = jnp.where(low, before, jnp.where(high, after, x))
    return 0.5 * (other - x)


def end_lines(line, planes, step):
    (near, near_far), (high, high_far) = line
    first, last = planes[0], planes[-1]
    one = near_far * 0.5 * (last + roll(first, -step))
    two = high_far * 0.5 * (first + roll(last, step))
    for i, plane in enumerate(planes):
        one = one + near[i] * plane
        two = two + high[i] * plane
    return one, two


def chunks(source, target, sem, count=8):
    step = source.shape[0] // count
    return [
        pltpu.make_async_copy(
            source.at[i * step : (i + 1) * step], target.at[i * step : (i + 1) * step], sem.at[i]
        )
        for i in range(count)
    ]


def first_kernel(
    line,
    fields_hbm,
    emap_hbm,
    metric_hbm,
    table_hbm,
    slots_ref,
    metric_out,
    msg_ref,
    fields,
    table_ref,
    emap,
    metric,
    sem,
):
    count = fields.shape[-1]
    order = (3, 5, 4, 0, 1, 2, 6)
    small = [
        pltpu.make_async_copy(emap_hbm, emap, sem.at[7]),
        pltpu.make_async_copy(metric_hbm, metric, sem.at[8]),
    ]
    large = [pltpu.make_async_copy(fields_hbm.at[f], fields.at[f], sem.at[f]) for f in order]
    tables_copies = chunks(table_hbm, table_ref, sem.at[pl.ds(9, 8)])
    for copy in small + large + tables_copies:
        copy.start()
    for copy in small + large:
        copy.wait()
    local = lax.broadcasted_iota(jnp.int32, (count, count), 0)
    slots = (local == emap[...]).astype(F32).astype(BF)
    slots_ref[...] = slots
    iy = positions((1, 1, count))[1]
    for f in order:
        if f in (3, 5):
            values = dot(fields[f], slots, True).reshape(NI, NI, NI, count)
            first, last = values[:, 0], values[:, NI - 1]
        else:
            planes = fields[f].reshape(NI, NI, NI, count)
            planes = jnp.concatenate([planes[:, 0], planes[:, NI - 1]], axis=0)
            planes = dot(planes.reshape(2 * NI * NI, count), slots, True)
            first, last = rows3(planes[0:64]), rows3(planes[64:128])
        face = jnp.where(iy == 0, first, last)
        msg_ref[f * 64 : f * 64 + 64, :] = rows2(face).astype(BF)
        if f in (3, 5):
            low, high = end_lines(line, [values[:, b] for b in range(NI)], EZ)
            at = (7 + (f == 5)) * 64
            msg_ref[at : at + 64, :] = rows2(jnp.where(iy == 0, low, high)).astype(BF)
    high, mid, low = split3(metric[...])
    pad = jnp.zeros((7, count), F32)
    stacked = jnp.concatenate([high.astype(F32), mid.astype(F32), low.astype(F32), pad], axis=0)
    moved = dot(stacked.astype(BF), slots, True)
    local = moved[0:3] + moved[3:6] + moved[6:9]
    metric_out[...] = jnp.concatenate([local, jnp.zeros((5, count), F32)], axis=0)
    high = local.astype(BF).astype(F32)
    tail = jnp.concatenate([high, local - high, jnp.zeros((10, count), F32)], axis=0)
    msg_ref[9 * 64 : 9 * 64 + 16, :] = tail.astype(BF)
    for copy in tables_copies:
        copy.wait()


def own_kernel(fields_ref, slots_ref, coarse_ref):
    count = fields_ref.shape[-1]
    for f in range(7):
        values = dot(fields_ref[f], slots_ref[...], True)
        coarse_ref[f] = values.reshape(NI, NI, NI, count)


def from_azim(x, iy):
    gap = (EY - 1) * EZ
    return jnp.where(iy == 0, roll(x, -gap), roll(x, gap))


def metric_classes(x, halo, shift, at_low, at_high):
    low = 0.5 * (x + jnp.where(at_low, halo, roll(x, shift)))
    high = 0.5 * (x + jnp.where(at_high, halo, roll(x, -shift)))
    return [x, low, high]


def radial_classes(x, iz):
    low = jnp.where(iz > 0, 0.5 * (x + roll(x, 1)), x)
    high = jnp.where(iz < EZ - 1, 0.5 * (x + roll(x, -1)), x)
    return [x, low, high]


def second_kernel(
    line, even_ring, coarse_ref, metric_ref, halo_ref, ext_ref, ends_ref, table_ref, a_ref, b_ref
):
    count = coarse_ref.shape[-1]
    layer = EY * EZ
    ix, iy, iz = positions((1, 1, count))
    blocks = []
    lines = []
    for f in range(7):
        values = coarse_ref[f]
        first, last = values[:, 0], values[:, NI - 1]
        halo = from_azim(rows3(halo_ref[f * 64 : f * 64 + 64, :].astype(F32)), iy)
        low = 0.5 * (jnp.where(iy == 0, halo, roll(last, EZ)) - first)
        high = 0.5 * (jnp.where(iy == EY - 1, halo, roll(first, -EZ)) - last)
        values = jnp.concatenate([values, low[:, None], high[:, None]], axis=1)
        ext_ref[f] = values
        blocks.append(seam_rows(jnp.where(ix == 0, values[0], values[NI - 1])))
        if f in (4, 5):
            low, high = end_lines(line, [values[a] for a in range(NI)], layer)
            lines.append(seam_rows(jnp.where(ix == 0, low, high)))
    blocks += lines
    extra = []
    for i in range(2):
        ends = from_azim(rows3(halo_ref[(7 + i) * 64 : (8 + i) * 64, :].astype(F32)), iy)
        ends_ref[i] = ends
        extra.append(jnp.where(ix[0] == 0, ends[0], ends[NI - 1]))

    ix, iy, iz = positions((1, count))
    packed = halo_ref[9 * 64 : 9 * 64 + 16, :].astype(F32)
    other = from_azim(packed[0:3] + packed[3:6], iy)
    own = metric_ref[...]
    lows, highs = iy == 0, iy == EY - 1
    rows = []
    for item in metric_classes(own[0:1], other[0:1], EZ, lows, highs):
        rows += radial_classes(item, iz)
    rows += radial_classes(own[1:2], iz)
    rows += metric_classes(own[2:3], other[2:3], EZ, lows, highs)
    rows += radial_classes(other[1:2], iz)
    table = jnp.concatenate(rows + [jnp.zeros((24 - len(rows), count), F32)], axis=0)
    table_ref[...] = table
    high = table.astype(BF).astype(F32)
    spare = jnp.zeros((SEAM - 64, count), F32)
    blocks.append(jnp.concatenate(extra + [high, table - high, spare], axis=0))

    ix = positions((SEAM, count))[0]
    even = is_even(even_ring)
    half = len(blocks) // 2
    for i in range(half):
        one, two = blocks[i], blocks[half + i]
        down = jnp.where(ix == 0, one, roll(two, layer))
        up = jnp.where(ix == 0, roll(one, layer), two)
        rows = slice(i * SEAM, (i + 1) * SEAM)
        a_ref[rows, :] = jnp.where(even, up, down).astype(BF)
        b_ref[rows, :] = jnp.where(even, down, up).astype(BF)


def signed(one, two, parity):
    return one + two if parity == 0 else one - two


def radial_fold(rows, iz, parity):
    last = NI - 1
    low = jnp.where(iz > 0, roll(rows[last], 1) - rows[0], 0.0)
    high = jnp.where(iz < EZ - 1, roll(rows[0], -1) - rows[last], 0.0)
    return [signed(rows[c], rows[last - c], parity) for c in range(HI)] + [
        0.5 * signed(low, high, parity)
    ]


def azim_fold(plane, parity):
    return [
        signed(
            plane[b if b < HI else NI], plane[NI - 1 - b if b < HI else NI + 1], parity
        )
        for b in range(HO)
    ]


def row_kinds(count):
    row = lax.broadcasted_iota(jnp.int32, (ROWS, count), 0)
    return row, row < HO * HO, lax.rem(row, HO * HO) < HO, lax.rem(row, HO) == 0


def line_of(source, at):
    return source[at : at + 1]


def row_tables(weights, table, factor_ref, quad_ref):
    count = table.shape[-1]
    row, a_edge, b_edge, c_edge = row_kinds(count)

    def weight_of(index):
        result = jnp.full((ROWS, count), weights[0], F32)
        for i in range(1, HO):
            result = jnp.where(index == i, weights[i], result)
        return result

    a_pos = lax.div(row, HO * HO)
    b_pos = lax.rem(lax.div(row, HO), HO)
    quad = weight_of(a_pos) * weight_of(b_pos) * weight_of(lax.rem(row, HO))
    quad_ref[...] = jnp.where(row < HO**3, quad, 0.0)

    def by_radius(at, side):
        return jnp.where(c_edge, line_of(table, at + 1 + side), line_of(table, at))

    for one in range(2):
        for two in range(2):
            at = one * 2 + two
            factor_ref[at] = jnp.where(b_edge, by_radius(3 + 3 * one, two), by_radius(0, two))
            factor_ref[4 + at] = by_radius(9, two)
            factor_ref[8 + at] = jnp.where(b_edge, line_of(table, 13 + two), line_of(table, 12))


def third_kernel(
    weights,
    ext_ref,
    table_ref,
    const_ref,
    later_hbm,
    gs_ref,
    later_ref,
    factor_ref,
    quad_ref,
    tmp_ref,
    xs_ref,
    sem,
):
    count = ext_ref.shape[-1]
    width = HO * HI
    iz = positions((width, count))[2]
    zeros = jnp.zeros((HI, count), F32)

    copies = chunks(later_hbm, later_ref, sem)
    for copy in copies:
        copy.start()
    row_tables(weights, table_ref[...], factor_ref, quad_ref)
    for f in range(7):
        pair, side = PLACE[f]
        lanes = slice(side * count, (side + 1) * count)
        values = ext_ref[f]
        for pa in range(2):
            mixed = [signed(values[a], values[NI - 1 - a], pa) for a in range(HI)]
            for pb in range(2):
                at = f % 2 * 4 + pa * 2 + pb
                for a in range(HI):
                    for b, item in enumerate(azim_fold(mixed[a], pb)):
                        row = (a * HO + b) * NI
                        tmp_ref[at, row : row + NI, :] = item
                main = [tmp_ref[at, pl.ds(c, width, stride=NI), :] for c in range(NI)]
                for pc in range(2):
                    rows = []
                    for item in radial_fold(main, iz, pc):
                        rows += [item, zeros]
                    rows.append(jnp.zeros((8, count), F32))
                    operand = jnp.concatenate(rows, axis=0).astype(BF)
                    xs_ref[pair, pa * 4 + pb * 2 + pc, :, lanes] = operand

    def refine(sector, carry):
        for pair in range(PAIRS):
            width = 2 * count if pair < PAIRS - 1 else count
            source = xs_ref[pair, sector, :, 0:width]
            source = jnp.concatenate([source, source], axis=0)
            for q in range(0 if pair < PAIRS - 1 else 1, 4):
                rows = pl.ds(sector * 4 * ROWS + q * ROWS, ROWS)
                gs_ref[pair, q, sector ^ FLIPS[q], :, 0:width] = dot(const_ref[rows, :], source)
        return carry

    lax.fori_loop(0, 8, refine, 0, unroll=2)
    for copy in copies:
        copy.wait()


def fourth_kernel(
    ends_value,
    even_ring,
    inv_ref,
    gs_ref,
    factor_ref,
    quad_ref,
    ext_ref,
    ends_ref,
    table_ref,
    metric_ref,
    slots_ref,
    ra_ref,
    rb_ref,
    const_ref,
    out_ref,
    tmp_ref,
    along_ref,
    edge_ref,
    vort_ref,
    linear_ref,
    edge_factor_ref,
    normal_x_ref,
    normal_y_ref,
    xt_ref,
    nodal_ref,
):
    count = ext_ref.shape[-1]
    layer = EY * EZ
    even = is_even(even_ring)
    ix = positions((SEAM, count))[0]
    end_low, end_high, value_of_slope = ends_value
    seam_at = 0
    second_at = seam_at + 4 * SEAM_ROWS
    lift_x_at = second_at + 6 * ROWS
    lift_y_at = lift_x_at + ROWS

    def block(i):
        rows = slice(i % 5 * SEAM, (i % 5 + 1) * SEAM)
        one = ra_ref[rows, :].astype(F32)
        two = rb_ref[rows, :].astype(F32)
        down = jnp.where(even, two, one)
        up = jnp.where(even, one, two)
        if i < 5:
            return jnp.where(ix == 0, down, roll(up, layer))
        return jnp.where(ix == 0, roll(down, layer), up)

    ix3 = positions((1, 1, count))[0]
    iz8 = positions((NI, count))[2]

    def stream_added(first, last, halo):
        lane = positions((1,) * (first.ndim - 1) + (count,))[0]
        low = 0.5 * (jnp.where(lane == 0, halo, roll(last, layer)) - first)
        high = 0.5 * (jnp.where(lane == 0, roll(first, -layer), halo) - last)
        return low, high

    seam = {}
    tmp_ref[...] = jnp.zeros(tmp_ref.shape, F32)

    def seam_operand(f):
        pair, side = PLACE[f]
        lanes = slice(side * count, (side + 1) * count)
        halo = block(f).reshape(EXT, NI, count)
        first, last = ext_ref[f, 0], ext_ref[f, NI - 1]
        low, high = stream_added(first, last, halo)
        if f in (4, 5):
            seam[f] = seam_rows(jnp.where(ix3 == 0, first + low, last + high))
        for pa in range(2):
            mixed = signed(low, high, pa)
            for pb in range(2):
                at = f % 2 * 4 + pa * 2 + pb
                for b, item in enumerate(azim_fold(mixed, pb)):
                    tmp_ref[at, b * NI : (b + 1) * NI, :] = item
                main = [tmp_ref[at, pl.ds(c, NI, stride=NI), :] for c in range(NI)]
                for pc in range(2):
                    rows = radial_fold(main, iz8, pc)
                    rows.append(jnp.zeros((NI, count), F32))
                    operand = jnp.concatenate(rows, axis=0).astype(BF)
                    xt_ref[pair, pa * 4 + pb * 2 + pc, :, lanes] = operand

    first_nodes = lax.broadcasted_iota(jnp.int32, (32, 2 * count), 0) < HO * HO

    def refine_seam(pair, sector):
        at = seam_at + (sector // 2) * SEAM_ROWS
        half = sector % 2 * ROWS
        matrix = const_ref[at : at + SEAM_ROWS, half : half + 2 * 48]
        width = 2 * count if pair < PAIRS - 1 else count
        source = xt_ref[pair, sector, :, 0:width]
        added = dot(matrix, jnp.concatenate([source, source], axis=0))
        target = sector ^ 4
        along_ref[pair, target, :, 0:width] = gs_ref[pair, 1, target, :, 0:width] + added[0:ROWS]
        for q, slot in ((0, 0), (2, 1), (3, 2)):
            if q == 0 and pair == PAIRS - 1:
                continue
            if q == 0:
                more = added[0:32] * value_of_slope[sector // 4]
                more = jnp.where(first_nodes[:, 0:width], more, 0.0)
            else:
                more = added[ROWS + 32 * (slot - 1) : ROWS + 32 * slot]
            target = sector ^ FLIPS[q]
            edge_ref[pair, slot, target, :, 0:width] = gs_ref[pair, q, target, 0:32, 0:width] + more

    for pair in range(PAIRS):
        for f in range(7):
            if PLACE[f][0] == pair:
                seam_operand(f)
        for sector in range(8):
            refine_seam(pair, sector)

    row, a_edge, b_edge, c_edge = row_kinds(count)

    table = table_ref[...]
    packed = block(9)
    theirs = packed[16:40] + packed[40:64]
    lane_ix = positions((24, count))[0]
    at_low = 0.5 * (table + jnp.where(lane_ix == 0, theirs, roll(table, layer)))
    at_high = 0.5 * (table + jnp.where(lane_ix == 0, roll(table, -layer), theirs))

    def by_radius(source, at, side):
        return jnp.where(c_edge, line_of(source, at + 1 + side), line_of(source, at))

    for one in range(2):
        edge = at_low if one == 0 else at_high
        for two in range(2):
            at = one * 2 + two
            outside = by_radius(edge, 9, two)[0:32]
            edge_factor_ref[at] = jnp.where(a_edge[0:32], outside, factor_ref[4 + at, 0:32, :])
            outside = jnp.where(b_edge[0:32], line_of(edge, 13 + two), line_of(edge, 12))
            edge_factor_ref[4 + at] = jnp.where(a_edge[0:32], outside, factor_ref[8 + at, 0:32, :])

    def with_added(parts):
        halves = []
        for part in parts:
            stacked = part.reshape(EXT, NI, count)
            halves.append(jnp.concatenate([part, seam_rows(radial_added(stacked))], axis=0))
        return jnp.concatenate(halves, axis=1).astype(BF)

    def lift(at, rows, operand):
        return dot(const_ref[at : at + rows, 0 : 2 * SEAM], operand)

    stream = []
    for i in range(2):
        shared = jnp.where(ix == 0, end_high, end_low) * seam[4 + i]
        stream.append(block(7 + i) + shared)
    lifted = lift(lift_x_at, ROWS, with_added(stream))
    for one in range(2):
        for two in range(2):
            at = one * 2 + two
            scale = jnp.where(
                b_edge, by_radius(theirs, 3 + 3 * one, two), by_radius(theirs, 0, two)
            )[0:32]
            for i in range(2):
                part = lifted[at * 32 : at * 32 + 32, i * count : (i + 1) * count]
                normal_x_ref[i, at] = part * scale

    iy3 = positions((1, 1, count))[1]
    iy2 = iy3[0]
    azim = []
    for i, f in enumerate((3, 5)):
        factor = jnp.where(iy3 == 0, end_high, end_low)
        values = ext_ref[f]
        halo = block(f).reshape(EXT, NI, count)
        near = jnp.where(
            iy3 == 0, values[:, 0] + values[:, NI], values[:, NI - 1] + values[:, NI + 1]
        )
        own = ends_ref[i] + factor * near
        near = jnp.where(iy2 == 0, halo[0] + halo[NI], halo[NI - 1] + halo[NI + 1])
        other = packed[8 * i : 8 * i + 8] + factor[0] * near
        low, high = stream_added(own[0], own[NI - 1], other)
        azim.append(jnp.concatenate([rows2(own), low, high], axis=0))
    span = 8 * len(GROUPS)
    lifted = lift(lift_y_at, 4 * span, with_added(azim))
    for one in range(2):
        edge = at_low if one == 0 else at_high
        for two in range(2):
            at = one * 2 + two
            scale = jnp.where(a_edge, by_radius(edge, 15, two), by_radius(table, 15, two))
            for i in range(2):
                for k, start in enumerate(GROUPS):
                    rows = slice(at * span + 8 * k, at * span + 8 * k + 8)
                    part = lifted[rows, i * count : (i + 1) * count]
                    normal_y_ref[i, at, start : start + 8] = part * scale[start : start + 8]

    def parts_of(f, q, at, edge):
        pair, side = PLACE[f]
        lanes = slice(side * count, (side + 1) * count)
        if q == 1:
            return [along_ref[pair, sector, at, lanes] for sector in range(8)]
        if edge:
            slot = (0, None, 1, 2)[q]
            return [edge_ref[pair, slot, sector, at, lanes] for sector in range(8)]
        return [gs_ref[pair, q, sector, at, lanes] for sector in range(8)]

    chunk = 16

    def vorticity(at, start, edge):
        shape = (chunk, count)
        lane_ix, lane_iy, lane_iz = positions(shape)
        rows = lax.broadcasted_iota(jnp.int32, shape, 0) + start
        on_a = rows < HO * HO
        on_b = lax.rem(rows, HO * HO) < HO
        on_c = lax.rem(rows, HO) == 0

        def factor_at(which):
            if edge and which >= 4:
                return edge_factor_ref[which - 4, at, :]
            return factor_ref[which, at, :]

        def nodal(f, q, factor):
            g = unfold(parts_of(f, q, at, edge))
            for s in range(8):
                nodal_ref[kept(f - 3, q - 1), s, at, :] = g[s]
            return [g[s] * factor_at(factor(s)) for s in range(8)]

        def along_x(i, f):
            g = nodal(f, 1, lambda s: s % 4)
            if edge:
                for two in range(4):
                    low, high = g[two], g[4 + two]
                    normal = normal_x_ref[i, two, at, :]
                    near = lane_ix == 0
                    first = 0.5 * (low + jnp.where(near, normal, roll(high, layer)))
                    last = 0.5 * (high + jnp.where(near, roll(low, -layer), normal))
                    g[two] = jnp.where(on_a, first, low)
                    g[4 + two] = jnp.where(on_a, last, high)
            return g

        def along_y(i, f):
            g = nodal(f, 2, lambda s: 4 + s // 4 * 2 + s % 2)
            for two in range(4):
                here = two // 2 * 4 + two % 2
                low, high = g[here], g[here + 2]
                normal = normal_y_ref[i, two, at, :]
                first = 0.5 * (low + jnp.where(lane_iy == 0, normal, roll(high, EZ)))
                last = 0.5 * (high + jnp.where(lane_iy == EY - 1, normal, roll(low, -EZ)))
                g[here] = jnp.where(on_b, first, low)
                g[here + 2] = jnp.where(on_b, last, high)
            return g

        def along_z(f):
            g = nodal(f, 3, lambda s: 8 + s // 2)
            lower = on_c & (lane_iz > 0)
            upper = on_c & (lane_iz < EZ - 1)
            for two in range(4):
                low, high = g[2 * two], g[2 * two + 1]
                g[2 * two] = jnp.where(lower, 0.5 * (low + roll(high, 1)), low)
                g[2 * two + 1] = jnp.where(upper, 0.5 * (high + roll(low, -1)), high)
            return g

        pairs = (
            (lambda: along_y(1, 5), lambda: along_z(4)),
            (lambda: along_z(3), lambda: along_x(1, 5)),
            (lambda: along_x(0, 4), lambda: along_y(0, 3)),
        )
        for i, (plus, minus) in enumerate(pairs):
            one, two = plus(), minus()
            folded = unfold([0.125 * (one[s] - two[s]) for s in range(8)])
            for sector in range(8):
                vort_ref[i, sector, at, :] = folded[sector].astype(BF)

    for step in range(2):
        vorticity(slice(step * chunk, (step + 1) * chunk), step * chunk, True)

    def vorticity_step(step, carry):
        start = pl.multiple_of(step * chunk, chunk)
        vorticity(pl.ds(start, chunk), start, False)
        return carry

    lax.fori_loop(2, ROWS // chunk, vorticity_step, 0)

    metric = [metric_ref[i : i + 1] for i in range(3)]
    inv = inv_ref[0]
    scaled = [inv * metric[i] for i in range(3)]
    taken = ((1, 2), (2, 0), (0, 1))
    terms = (((1, 0), (2, 1)), ((2, 0), (0, 1)), ((0, 0), (1, 1)))
    for target in range(8):
        slope = []
        for axis in range(3):
            flip = FLIPS[1 + axis]
            sector = target ^ flip
            source = jnp.concatenate([vort_ref[i, sector] for i in taken[axis]], axis=1)
            source = jnp.concatenate([source, source], axis=0)
            at = second_at + (2 * axis + (1 if sector & flip else 0)) * ROWS
            slope.append(dot(const_ref[at : at + ROWS, :], source))
        for i in range(3):
            (one, half), (two, other) = terms[i]
            plus = scaled[one] * slope[one][:, half * count : (half + 1) * count]
            minus = scaled[two] * slope[two][:, other * count : (other + 1) * count]
            if i == 0:
                linear_ref[i, target] = along_ref[3, target, :, 0:count] * metric[0] + (plus - minus)
            else:
                near = edge_ref[3, i, target, :, 0:count] * metric[i]
                far = gs_ref[3, 1 + i, target, 32:, 0:count] * metric[i]
                linear_ref[i, target, 0:32, :] = near + (plus - minus)[0:32]
                linear_ref[i, target, 32:, :] = far + (plus - minus)[32:]

    def body(edge, step, total):
        at = pl.ds(pl.multiple_of(step * 8, 8), 8)
        for side in range(2):
            total = total + quad_ref[at, :] * energy_of(at, side, edge)
        return total

    def energy_of(at, side, edge):
        def unfold_half(parts):
            return unfold4([signed(parts[s], parts[4 + s], side) for s in range(4)])

        def part(f, q):
            return unfold_half(parts_of(f, q, at, edge))

        base = [[item * metric[j] for item in part(j, 0)] for j in range(3)]
        dual = [part(3 + j, 0) for j in range(3)]
        energy = spread = None
        for i in range(3):
            total = unfold_half([linear_ref[i, s, at, :] for s in range(8)])
            for j in range(3):
                if i == j:
                    slope = part(3 + i, 1 + j)
                else:
                    slope = [nodal_ref[kept(i, j), side * 4 + s, at, :] for s in range(4)]
                total = [total[s] - base[j][s] * slope[s] for s in range(4)]
                if i == j:
                    more = [slope[s] * metric[i] for s in range(4)]
                    spread = more if i == 0 else [spread[s] + more[s] for s in range(4)]
            inner = None
            for j in range(3):
                slope = part(j, 1 + i)
                more = [dual[j][s] * slope[s] for s in range(4)]
                inner = more if j == 0 else [inner[s] + more[s] for s in range(4)]
            total = [total[s] + metric[i] * inner[s] for s in range(4)]
            more = [item * item for item in total]
            energy = more if i == 0 else [energy[s] + more[s] for s in range(4)]
        energy = [energy[s] + spread[s] * spread[s] for s in range(4)]
        return (energy[0] + energy[1]) + (energy[2] + energy[3])

    total = jnp.zeros((8, count), F32)
    total = lax.fori_loop(0, 4, functools.partial(body, True), total, unroll=2)
    total = lax.fori_loop(4, ROWS // 8, functools.partial(body, False), total, unroll=2)
    weighted = jnp.sum(total, axis=0, keepdims=True)
    result = jnp.sqrt(weighted / 8.0) / float(ORDER_OUT**2)
    high, mid, low = split3(result)
    stacked = jnp.concatenate(
        [high.astype(F32), mid.astype(F32), low.astype(F32), jnp.zeros((13, count), F32)], axis=0
    )
    moved = dot(stacked.astype(BF), slots_ref[...])
    out_ref[...] = moved[0:1] + moved[1:2] + moved[2:3]


def kept(component, axis):
    return component * 2 + (axis if axis < component else axis - 1)


def unfold4(parts):
    plus0, minus0 = parts[0] + parts[1], parts[0] - parts[1]
    plus1, minus1 = parts[2] + parts[3], parts[2] - parts[3]
    return [plus0 + plus1, minus0 + minus1, plus0 - plus1, minus0 - minus1]


def unfold(parts):
    plus = unfold4([parts[s] + parts[4 + s] for s in range(4)])
    minus = unfold4([parts[s] - parts[4 + s] for s in range(4)])
    return plus + minus


MIB = 1024 * 1024


def per_device(fields, elem_map, metric, inv_reynolds):
    refine, const, weights, (line, ends_value) = tables()
    count = fields.shape[-1]
    vmem = pl.BlockSpec(memory_space=pltpu.VMEM)

    def params(mib):
        return pltpu.CompilerParams(vmem_limit_bytes=mib * MIB)

    def struct(shape, dtype=F32):
        return jax.ShapeDtypeStruct(shape, dtype)

    hbm = pl.BlockSpec(memory_space=pltpu.HBM)
    inputs = [
        pltpu.with_memory_space_constraint(item, pltpu.HBM)
        for item in (fields, elem_map, metric, jnp.asarray(refine), jnp.asarray(const))
    ]
    slots, local_metric, message, near_fields, refine = pl.pallas_call(
        functools.partial(first_kernel, line),
        out_shape=(
            struct((count, count), BF),
            struct((8, count)),
            struct((9 * 64 + 16, count), BF),
            struct(fields.shape, BF),
            struct(refine.shape, BF),
        ),
        in_specs=[hbm] * 4,
        out_specs=(vmem,) * 5,
        scratch_shapes=[
            pltpu.VMEM(elem_map.shape, jnp.int32),
            pltpu.VMEM(metric.shape, F32),
            pltpu.SemaphoreType.DMA((17,)),
        ],
        compiler_params=params(6),
        name="first",
    )(*inputs[:4])

    coarse = pl.pallas_call(
        own_kernel,
        out_shape=struct((7, NI, NI, NI, count)),
        in_specs=[vmem] * 2,
        out_specs=vmem,
        compiler_params=params(6),
        cost_estimate=pl.CostEstimate(
            flops=2 * fields.size * count, bytes_accessed=3 * 10**6, transcendentals=0
        ),
        name="own",
    )(near_fields, slots)

    azim = lax.axis_size("azim")
    if azim == 2:
        halo = lax.ppermute(message, "azim", [(0, 1), (1, 0)])
    else:
        ahead = lax.ppermute(message, "azim", [(i, (i + 1) % azim) for i in range(azim)])
        behind = lax.ppermute(message, "azim", [((i + 1) % azim, i) for i in range(azim)])
        iy = (jnp.arange(count) // EZ) % EY
        halo = jnp.where(iy >= EY // 2, ahead, behind)

    streams = lax.axis_size("strm")
    even_ring = streams % 2 == 0
    extended, ends, table, to_a, to_b = pl.pallas_call(
        functools.partial(second_kernel, line, even_ring),
        out_shape=(
            struct((7, NI, EXT, NI, count)),
            struct((2, NI, NI, count)),
            struct((24, count)),
            struct((5 * SEAM, count), BF),
            struct((5 * SEAM, count), BF),
        ),
        in_specs=[vmem] * 3,
        out_specs=(vmem,) * 5,
        compiler_params=params(12),
        name="second",
    )(coarse, local_metric, halo)

    if even_ring:
        near = [(i, i ^ 1) for i in range(streams)]
        far = []
        for i in range(1, streams, 2):
            far += [(i, (i + 1) % streams), ((i + 1) % streams, i)]
        got_a = lax.ppermute(to_a, "strm", near)
        got_b = lax.ppermute(to_b, "strm", far)
    else:
        got_b = lax.ppermute(to_a, "strm", [(i, (i + 1) % streams) for i in range(streams)])
        got_a = lax.ppermute(to_b, "strm", [((i + 1) % streams, i) for i in range(streams)])

    raw, const, factor, quad = pl.pallas_call(
        functools.partial(third_kernel, weights),
        out_shape=(
            struct((PAIRS, 4, 8, ROWS, 2 * count)),
            struct(const.shape, BF),
            struct((12, ROWS, count)),
            struct((ROWS, count)),
        ),
        in_specs=[vmem] * 3 + [hbm],
        out_specs=(vmem,) * 4,
        scratch_shapes=[
            pltpu.VMEM((8, HO * HI * NI, count), F32),
            pltpu.VMEM((PAIRS, 8, ROWS, 2 * count), BF),
            pltpu.SemaphoreType.DMA((8,)),
        ],
        compiler_params=params(8),
        cost_estimate=pl.CostEstimate(
            flops=4 * 10**9, bytes_accessed=20 * 10**6, transcendentals=0
        ),
        name="third",
    )(extended, table, refine, inputs[4])

    result = pl.pallas_call(
        functools.partial(fourth_kernel, ends_value, even_ring),
        out_shape=struct((1, count)),
        in_specs=[pl.BlockSpec(memory_space=pltpu.SMEM)] + [vmem] * 11,
        out_specs=vmem,
        scratch_shapes=[
            pltpu.VMEM((8, NI * NI, count), F32),
            pltpu.VMEM((PAIRS, 8, ROWS, 2 * count), F32),
            pltpu.VMEM((PAIRS, 3, 8, 32, 2 * count), F32),
            pltpu.VMEM((3, 8, ROWS, count), BF),
            pltpu.VMEM((3, 8, ROWS, count), F32),
            pltpu.VMEM((8, 32, count), F32),
            pltpu.VMEM((2, 4, 32, count), F32),
            pltpu.VMEM((2, 4, ROWS, count), F32),
            pltpu.VMEM((PAIRS, 8, 48, 2 * count), BF),
            pltpu.VMEM((6, 8, ROWS, count), F32),
        ],
        compiler_params=params(20),
        name="fourth",
    )(
        inv_reynolds,
        raw,
        factor,
        quad,
        extended,
        ends,
        table,
        local_metric,
        slots,
        got_a,
        got_b,
        const,
    )
    return result.reshape(count)


def solution(mesh):
    return jax.shard_map(
        per_device,
        mesh=mesh,
        in_specs=(
            P(None, None, ("grp", "strm", "azim")),
            P(("strm", "azim"), None),
            P(None, ("strm", "azim")),
            P("grp"),
        ),
        out_specs=P(("grp", "strm", "azim")),
        check_vma=False,
    )
```

```python
import functools

import jax
import jax.numpy as jnp
import numpy as np
from jax import lax
from jax.experimental import pallas as pl
from jax.experimental.pallas import tpu as pltpu
from jax.sharding import PartitionSpec as P

ORDER_IN = 7
ORDER_OUT = 9
EY = 8
EZ = 8
NI = ORDER_IN + 1
NO = ORDER_OUT + 1
HI = NI // 2
HO = NO // 2
ROWS = 128
SEAM_ROWS = ROWS + 2 * 32
GROUPS = sorted({row // 8 * 8 for row in range(HO**3) if row % (HO * HO) < HO})
EXT = NI + 2
SEAM = EXT * NI
BF = jnp.bfloat16
F32 = jnp.float32
PLACE = {3: (0, 0), 4: (0, 1), 5: (1, 0), 0: (1, 1), 1: (2, 0), 2: (2, 1), 6: (3, 0)}
PAIRS = 4
FLIPS = (0, 4, 2, 1)


def gll_table(extent):
    degree = extent - 1
    points = np.cos(np.pi * np.arange(extent) / degree)
    legendre = np.zeros((extent, extent))

    def fill():
        legendre[:, 0] = 1.0
        legendre[:, 1] = points
        for level in range(2, extent):
            legendre[:, level] = (
                (2 * level - 1) * points * legendre[:, level - 1]
                - (level - 1) * legendre[:, level - 2]
            ) / level

    for sweep in range(100):
        fill()
        points = points - (points * legendre[:, degree] - legendre[:, degree - 1]) / (
            extent * legendre[:, degree]
        )
    fill()
    weights = 2.0 / (degree * extent * legendre[:, degree] ** 2)
    return (points[::-1].copy(), weights[::-1].copy())


def lagrange_matrix(source, target):
    result = np.ones((len(target), len(source)))
    for column in range(len(source)):
        for partner in range(len(source)):
            if partner != column:
                result[:, column] *= (target - source[partner]) / (source[column] - source[partner])
    return result


def derivative_matrix(points):
    extent = len(points)
    identity = np.eye(extent)
    spacing = points[:, None] - points[None, :] + identity
    barycen = 1.0 / np.prod(spacing, axis=1)
    matrix = barycen[None, :] / barycen[:, None] / spacing * (1.0 - identity)
    return matrix - identity * matrix.sum(axis=1)[:, None]


def bf16_parts(matrix):
    high = matrix.astype(jnp.bfloat16)
    low = (matrix - high.astype(np.float64)).astype(jnp.bfloat16)
    return high, low


def pad_rows(matrix, rows):
    return np.concatenate([matrix, np.zeros((rows - matrix.shape[0],) + matrix.shape[1:])])


def two_terms(matrix):
    return np.concatenate(bf16_parts(matrix), axis=-1)


@functools.cache
def tables():
    coarse, unused = gll_table(NI)
    fine, weights = gll_table(NO)
    interp = lagrange_matrix(coarse, fine)
    slopes = derivative_matrix(fine)
    ends = np.eye(NO)[:, [0, NO - 1]]
    value = np.concatenate([interp, ends], axis=1)
    both = slopes @ value

    def folded(matrix, parity):
        sign = 1.0 - 2.0 * parity
        if matrix.shape[1] == EXT and matrix is not slopes:
            left = matrix[:HO, [0, 1, 2, 3, 8]]
            right = matrix[:HO, [7, 6, 5, 4, 9]]
        else:
            left = matrix[:HO, :HO]
            right = matrix[:HO, ::-1][:, :HO]
        return left + sign * right

    refine, seams = [], []
    for sector in range(8):
        pa, pb, pc = sector // 4, sector // 2 % 2, sector % 2
        blocks, ends_of = [], []
        for ta, tb, tc in (
            (value, value, value),
            (both, value, value),
            (value, both, value),
            (value, value, both),
        ):
            block = 0.125 * np.einsum(
                "ap,bq,cr->abcrpq", folded(ta, pa), folded(tb, pb), folded(tc, pc)
            ).reshape(HO**3, HO, HO, HO)
            own = np.zeros((HO**3, HO, 24))
            own[:, :, : HO * HI] = block[:, :, :HI].reshape(HO**3, HO, HO * HI)
            own = np.pad(own.reshape(HO**3, -1), ((0, 0), (0, ROWS - 24 * HO)))
            blocks.append(pad_rows(own, ROWS))
            added = np.zeros((HO**3, 48))
            added[:, : 8 * HO] = np.pad(block[:, :, HI], ((0, 0), (0, 0), (0, 3))).reshape(HO**3, -1)
            ends_of.append(added)
        refine.append(two_terms(np.concatenate(blocks)))
        rows = [pad_rows(ends_of[1], ROWS)]
        rows += [pad_rows(ends_of[q][: HO * HO], 32) for q in (2, 3)]
        seams.append(np.pad(two_terms(np.concatenate(rows)), ((0, 0), (0, ROWS - 96))))
    refine = np.stack(refine)
    seams = [np.concatenate(seams[2 * i : 2 * i + 2], axis=1) for i in range(4)]

    second = []
    eye = np.eye(HO)
    for axis in range(3):
        for parity in range(2):
            factors = [eye, eye, eye]
            factors[axis] = folded(slopes, parity)
            block = np.kron(np.kron(factors[0], factors[1]), factors[2])
            edge = ROWS - HO**3
            second.append(two_terms(np.pad(block, ((0, edge), (0, edge)))))
    second = np.stack(second)

    def half(side):
        return value[:HO] if side == 0 else value[::-1][:HO]

    lift_x, lift_y = [], []
    for side in range(2):
        for radial in range(2):
            plain = np.zeros((HO, EXT, HO, NI))
            added = np.zeros((HO, EXT, HO, NI))
            plain[...] = np.einsum("ap,cr->apcr", half(side), half(radial)[:, :NI])
            added[..., 0] = np.einsum("ap,c->apc", half(side), half(radial)[:, NI])
            added[..., NI - 1] = np.einsum("ap,c->apc", half(side), half(radial)[:, NI + 1])
            face = np.stack([plain, added]).transpose(1, 3, 0, 2, 4).reshape(HO, HO, 2 * SEAM)
            lift_x.append(pad_rows(face.reshape(HO * HO, -1), 32))
            spread = np.zeros((HO, HO, HO, 2 * SEAM))
            spread[:, 0] = face
            spread = pad_rows(spread.reshape(HO**3, -1), ROWS)
            lift_y.append(np.concatenate([spread[at : at + 8] for at in GROUPS]))

    def one_term(parts):
        matrix = np.concatenate(parts)
        edge = 2 * ROWS - matrix.shape[1]
        return np.pad(matrix, ((0, 0), (0, edge))).astype(jnp.bfloat16)

    refine = refine.reshape(-1, 2 * ROWS)
    const = np.concatenate(
        seams + [second.reshape(-1, 2 * ROWS), one_term(lift_x), one_term(lift_y)]
    )
    half_weights = [float(v) for v in weights[:HO]]
    line = []
    for end, far in ((0, NO - 1), (NO - 1, 0)):
        weights_in = slopes[end].copy()
        weights_in[[0, NO - 1]] = 0.0
        line.append(([float(v) for v in weights_in @ interp], float(slopes[end, far])))
    ratio = [1.0 / float(both[0, NI] + sign * both[0, NI + 1]) for sign in (1.0, -1.0)]
    ends = (float(slopes[0, 0]), float(slopes[NO - 1, NO - 1]), ratio)
    return refine, const, half_weights, (line, ends)


def dot(a, b, contract_last=False):
    dims = (((1,), (1 if contract_last else 0,)), ((), ()))
    return lax.dot_general(a, b, dims, preferred_element_type=F32)


def is_even(even_ring):
    return lax.rem(lax.axis_index("strm"), 2) == 0 if even_ring else True


def rows3(x):
    return x.reshape(NI, NI, x.shape[-1])


def seam_rows(x):
    return x.reshape(SEAM, x.shape[-1])


def rows2(x):
    return x.reshape(NI * NI, x.shape[-1])


def roll(x, shift):
    count = x.shape[-1]
    return pltpu.roll(x, shift % count, x.ndim - 1)


def positions(shape):
    lane = lax.broadcasted_iota(jnp.int32, shape, len(shape) - 1)
    return lax.div(lane, EY * EZ), lax.rem(lax.div(lane, EZ), EY), lax.rem(lane, EZ)


def split3(x):
    high = x.astype(BF)
    rest = x - high.astype(F32)
    mid = rest.astype(BF)
    low = (rest - mid.astype(F32)).astype(BF)
    return high, mid, low


def radial_added(x):
    axis = x.ndim - 2
    shape = (1,) * axis + x.shape[-2:]
    node = lax.broadcasted_iota(jnp.int32, shape, axis)
    iz = positions(shape)[2]
    last = x.shape[-2] - 1
    before = pltpu.roll(roll(x, 1), 1, axis)
    after = pltpu.roll(roll(x, -1), last, axis)
    low = (node == 0) & (iz > 0)
    high = (node == last) & (iz < EZ - 1)
    other = jnp.where(low, before, jnp.where(high, after, x))
    return 0.5 * (other - x)


def end_lines(line, planes, step):
    (near, near_far), (high, high_far) = line
    first, last = planes[0], planes[-1]
    one = near_far * 0.5 * (last + roll(first, -step))
    two = high_far * 0.5 * (first + roll(last, step))
    for i, plane in enumerate(planes):
        one = one + near[i] * plane
        two = two + high[i] * plane
    return one, two


def chunks(source, target, sem, count=8):
    step = source.shape[0] // count
    return [
        pltpu.make_async_copy(
            source.at[i * step : (i + 1) * step], target.at[i * step : (i + 1) * step], sem.at[i]
        )
        for i in range(count)
    ]


def first_kernel(
    line,
    fields_hbm,
    emap_hbm,
    metric_hbm,
    table_hbm,
    slots_ref,
    metric_out,
    msg_ref,
    fields,
    table_ref,
    emap,
    metric,
    sem,
):
    count = fields.shape[-1]
    order = (3, 5, 4, 0, 1, 2, 6)
    small = [
        pltpu.make_async_copy(emap_hbm, emap, sem.at[7]),
        pltpu.make_async_copy(metric_hbm, metric, sem.at[8]),
    ]
    large = [pltpu.make_async_copy(fields_hbm.at[f], fields.at[f], sem.at[f]) for f in order]
    tables_copies = chunks(table_hbm, table_ref, sem.at[pl.ds(9, 8)])
    for copy in small + large + tables_copies:
        copy.start()
    for copy in small + large:
        copy.wait()
    local = lax.broadcasted_iota(jnp.int32, (count, count), 0)
    slots = (local == emap[...]).astype(F32).astype(BF)
    slots_ref[...] = slots
    iy = positions((1, 1, count))[1]
    for f in order:
        if f in (3, 5):
            values = dot(fields[f], slots, True).reshape(NI, NI, NI, count)
            first, last = values[:, 0], values[:, NI - 1]
        else:
            planes = fields[f].reshape(NI, NI, NI, count)
            planes = jnp.concatenate([planes[:, 0], planes[:, NI - 1]], axis=0)
            planes = dot(planes.reshape(2 * NI * NI, count), slots, True)
            first, last = rows3(planes[0:64]), rows3(planes[64:128])
        face = jnp.where(iy == 0, first, last)
        msg_ref[f * 64 : f * 64 + 64, :] = rows2(face).astype(BF)
        if f in (3, 5):
            low, high = end_lines(line, [values[:, b] for b in range(NI)], EZ)
            at = (7 + (f == 5)) * 64
            msg_ref[at : at + 64, :] = rows2(jnp.where(iy == 0, low, high)).astype(BF)
    high, mid, low = split3(metric[...])
    pad = jnp.zeros((7, count), F32)
    stacked = jnp.concatenate([high.astype(F32), mid.astype(F32), low.astype(F32), pad], axis=0)
    moved = dot(stacked.astype(BF), slots, True)
    local = moved[0:3] + moved[3:6] + moved[6:9]
    metric_out[...] = jnp.concatenate([local, jnp.zeros((5, count), F32)], axis=0)
    high = local.astype(BF).astype(F32)
    tail = jnp.concatenate([high, local - high, jnp.zeros((10, count), F32)], axis=0)
    msg_ref[9 * 64 : 9 * 64 + 16, :] = tail.astype(BF)
    for copy in tables_copies:
        copy.wait()


def own_kernel(fields_ref, slots_ref, coarse_ref):
    count = fields_ref.shape[-1]
    for f in range(7):
        values = dot(fields_ref[f], slots_ref[...], True)
        coarse_ref[f] = values.reshape(NI, NI, NI, count)


def from_azim(x, iy):
    gap = (EY - 1) * EZ
    return jnp.where(iy == 0, roll(x, -gap), roll(x, gap))


def metric_classes(x, halo, shift, at_low, at_high):
    low = 0.5 * (x + jnp.where(at_low, halo, roll(x, shift)))
    high = 0.5 * (x + jnp.where(at_high, halo, roll(x, -shift)))
    return [x, low, high]


def radial_classes(x, iz):
    low = jnp.where(iz > 0, 0.5 * (x + roll(x, 1)), x)
    high = jnp.where(iz < EZ - 1, 0.5 * (x + roll(x, -1)), x)
    return [x, low, high]


def second_kernel(
    line, even_ring, coarse_ref, metric_ref, halo_ref, ext_ref, ends_ref, table_ref, a_ref, b_ref
):
    count = coarse_ref.shape[-1]
    layer = EY * EZ
    ix, iy, iz = positions((1, 1, count))
    blocks = []
    lines = []
    for f in range(7):
        values = coarse_ref[f]
        first, last = values[:, 0], values[:, NI - 1]
        halo = from_azim(rows3(halo_ref[f * 64 : f * 64 + 64, :].astype(F32)), iy)
        low = 0.5 * (jnp.where(iy == 0, halo, roll(last, EZ)) - first)
        high = 0.5 * (jnp.where(iy == EY - 1, halo, roll(first, -EZ)) - last)
        values = jnp.concatenate([values, low[:, None], high[:, None]], axis=1)
        ext_ref[f] = values
        blocks.append(seam_rows(jnp.where(ix == 0, values[0], values[NI - 1])))
        if f in (4, 5):
            low, high = end_lines(line, [values[a] for a in range(NI)], layer)
            lines.append(seam_rows(jnp.where(ix == 0, low, high)))
    blocks += lines
    extra = []
    for i in range(2):
        ends = from_azim(rows3(halo_ref[(7 + i) * 64 : (8 + i) * 64, :].astype(F32)), iy)
        ends_ref[i] = ends
        extra.append(jnp.where(ix[0] == 0, ends[0], ends[NI - 1]))

    ix, iy, iz = positions((1, count))
    packed = halo_ref[9 * 64 : 9 * 64 + 16, :].astype(F32)
    other = from_azim(packed[0:3] + packed[3:6], iy)
    own = metric_ref[...]
    lows, highs = iy == 0, iy == EY - 1
    rows = []
    for item in metric_classes(own[0:1], other[0:1], EZ, lows, highs):
        rows += radial_classes(item, iz)
    rows += radial_classes(own[1:2], iz)
    rows += metric_classes(own[2:3], other[2:3], EZ, lows, highs)
    rows += radial_classes(other[1:2], iz)
    table = jnp.concatenate(rows + [jnp.zeros((24 - len(rows), count), F32)], axis=0)
    table_ref[...] = table
    high = table.astype(BF).astype(F32)
    spare = jnp.zeros((SEAM - 64, count), F32)
    blocks.append(jnp.concatenate(extra + [high, table - high, spare], axis=0))

    ix = positions((SEAM, count))[0]
    even = is_even(even_ring)
    half = len(blocks) // 2
    for i in range(half):
        one, two = blocks[i], blocks[half + i]
        down = jnp.where(ix == 0, one, roll(two, layer))
        up = jnp.where(ix == 0, roll(one, layer), two)
        rows = slice(i * SEAM, (i + 1) * SEAM)
        a_ref[rows, :] = jnp.where(even, up, down).astype(BF)
        b_ref[rows, :] = jnp.where(even, down, up).astype(BF)


def signed(one, two, parity):
    return one + two if parity == 0 else one - two


def radial_fold(rows, iz, parity):
    last = NI - 1
    low = jnp.where(iz > 0, roll(rows[last], 1) - rows[0], 0.0)
    high = jnp.where(iz < EZ - 1, roll(rows[0], -1) - rows[last], 0.0)
    return [signed(rows[c], rows[last - c], parity) for c in range(HI)] + [
        0.5 * signed(low, high, parity)
    ]


def azim_fold(plane, parity):
    return [
        signed(
            plane[b if b < HI else NI], plane[NI - 1 - b if b < HI else NI + 1], parity
        )
        for b in range(HO)
    ]


def row_kinds(count):
    row = lax.broadcasted_iota(jnp.int32, (ROWS, count), 0)
    return row, row < HO * HO, lax.rem(row, HO * HO) < HO, lax.rem(row, HO) == 0


def line_of(source, at):
    return source[at : at + 1]


def row_tables(weights, table, factor_ref, quad_ref):
    count = table.shape[-1]
    row, a_edge, b_edge, c_edge = row_kinds(count)

    def weight_of(index):
        result = jnp.full((ROWS, count), weights[0], F32)
        for i in range(1, HO):
            result = jnp.where(index == i, weights[i], result)
        return result

    a_pos = lax.div(row, HO * HO)
    b_pos = lax.rem(lax.div(row, HO), HO)
    quad = weight_of(a_pos) * weight_of(b_pos) * weight_of(lax.rem(row, HO))
    quad_ref[...] = jnp.where(row < HO**3, quad, 0.0)

    def by_radius(at, side):
        return jnp.where(c_edge, line_of(table, at + 1 + side), line_of(table, at))

    for one in range(2):
        for two in range(2):
            at = one * 2 + two
            factor_ref[at] = jnp.where(b_edge, by_radius(3 + 3 * one, two), by_radius(0, two))
            factor_ref[4 + at] = by_radius(9, two)
            factor_ref[8 + at] = jnp.where(b_edge, line_of(table, 13 + two), line_of(table, 12))


def third_kernel(
    weights,
    ext_ref,
    table_ref,
    const_ref,
    later_hbm,
    gs_ref,
    later_ref,
    factor_ref,
    quad_ref,
    tmp_ref,
    xs_ref,
    sem,
):
    count = ext_ref.shape[-1]
    width = HO * HI
    iz = positions((width, count))[2]
    zeros = jnp.zeros((HI, count), F32)

    copies = chunks(later_hbm, later_ref, sem)
    for copy in copies:
        copy.start()
    row_tables(weights, table_ref[...], factor_ref, quad_ref)
    for f in range(7):
        pair, side = PLACE[f]
        lanes = slice(side * count, (side + 1) * count)
        values = ext_ref[f]
        for pa in range(2):
            mixed = [signed(values[a], values[NI - 1 - a], pa) for a in range(HI)]
            for pb in range(2):
                at = f % 2 * 4 + pa * 2 + pb
                for a in range(HI):
                    for b, item in enumerate(azim_fold(mixed[a], pb)):
                        row = (a * HO + b) * NI
                        tmp_ref[at, row : row + NI, :] = item
                main = [tmp_ref[at, pl.ds(c, width, stride=NI), :] for c in range(NI)]
                for pc in range(2):
                    rows = []
                    for item in radial_fold(main, iz, pc):
                        rows += [item, zeros]
                    rows.append(jnp.zeros((8, count), F32))
                    operand = jnp.concatenate(rows, axis=0).astype(BF)
                    xs_ref[pair, pa * 4 + pb * 2 + pc, :, lanes] = operand

    def refine(sector, carry):
        for pair in range(PAIRS):
            width = 2 * count if pair < PAIRS - 1 else count
            source = xs_ref[pair, sector, :, 0:width]
            source = jnp.concatenate([source, source], axis=0)
            for q in range(0 if pair < PAIRS - 1 else 1, 4):
                rows = pl.ds(sector * 4 * ROWS + q * ROWS, ROWS)
                gs_ref[pair, q, sector ^ FLIPS[q], :, 0:width] = dot(const_ref[rows, :], source)
        return carry

    lax.fori_loop(0, 8, refine, 0, unroll=4)
    for copy in copies:
        copy.wait()


def fourth_kernel(
    ends_value,
    even_ring,
    inv_ref,
    gs_ref,
    factor_ref,
    quad_ref,
    ext_ref,
    ends_ref,
    table_ref,
    metric_ref,
    slots_ref,
    ra_ref,
    rb_ref,
    const_ref,
    out_ref,
    tmp_ref,
    along_ref,
    edge_ref,
    vort_ref,
    linear_ref,
    edge_factor_ref,
    normal_x_ref,
    normal_y_ref,
    xt_ref,
    nodal_ref,
):
    count = ext_ref.shape[-1]
    layer = EY * EZ
    even = is_even(even_ring)
    ix = positions((SEAM, count))[0]
    end_low, end_high, value_of_slope = ends_value
    seam_at = 0
    second_at = seam_at + 4 * SEAM_ROWS
    lift_x_at = second_at + 6 * ROWS
    lift_y_at = lift_x_at + ROWS

    def block(i):
        rows = slice(i % 5 * SEAM, (i % 5 + 1) * SEAM)
        one = ra_ref[rows, :].astype(F32)
        two = rb_ref[rows, :].astype(F32)
        down = jnp.where(even, two, one)
        up = jnp.where(even, one, two)
        if i < 5:
            return jnp.where(ix == 0, down, roll(up, layer))
        return jnp.where(ix == 0, roll(down, layer), up)

    ix3 = positions((1, 1, count))[0]
    iz8 = positions((NI, count))[2]

    def stream_added(first, last, halo):
        lane = positions((1,) * (first.ndim - 1) + (count,))[0]
        low = 0.5 * (jnp.where(lane == 0, halo, roll(last, layer)) - first)
        high = 0.5 * (jnp.where(lane == 0, roll(first, -layer), halo) - last)
        return low, high

    seam = {}
    tmp_ref[...] = jnp.zeros(tmp_ref.shape, F32)

    def seam_operand(f):
        pair, side = PLACE[f]
        lanes = slice(side * count, (side + 1) * count)
        halo = block(f).reshape(EXT, NI, count)
        first, last = ext_ref[f, 0], ext_ref[f, NI - 1]
        low, high = stream_added(first, last, halo)
        if f in (4, 5):
            seam[f] = seam_rows(jnp.where(ix3 == 0, first + low, last + high))
        for pa in range(2):
            mixed = signed(low, high, pa)
            for pb in range(2):
                at = f % 2 * 4 + pa * 2 + pb
                for b, item in enumerate(azim_fold(mixed, pb)):
                    tmp_ref[at, b * NI : (b + 1) * NI, :] = item
                main = [tmp_ref[at, pl.ds(c, NI, stride=NI), :] for c in range(NI)]
                for pc in range(2):
                    rows = radial_fold(main, iz8, pc)
                    rows.append(jnp.zeros((NI, count), F32))
                    operand = jnp.concatenate(rows, axis=0).astype(BF)
                    xt_ref[pair, pa * 4 + pb * 2 + pc, :, lanes] = operand

    first_nodes = lax.broadcasted_iota(jnp.int32, (32, 2 * count), 0) < HO * HO

    def refine_seam(pair, sector):
        at = seam_at + (sector // 2) * SEAM_ROWS
        half = sector % 2 * ROWS
        matrix = const_ref[at : at + SEAM_ROWS, half : half + 2 * 48]
        width = 2 * count if pair < PAIRS - 1 else count
        source = xt_ref[pair, sector, :, 0:width]
        added = dot(matrix, jnp.concatenate([source, source], axis=0))
        target = sector ^ 4
        along_ref[pair, target, :, 0:width] = gs_ref[pair, 1, target, :, 0:width] + added[0:ROWS]
        for q, slot in ((0, 0), (2, 1), (3, 2)):
            if q == 0 and pair == PAIRS - 1:
                continue
            if q == 0:
                more = added[0:32] * value_of_slope[sector // 4]
                more = jnp.where(first_nodes[:, 0:width], more, 0.0)
            else:
                more = added[ROWS + 32 * (slot - 1) : ROWS + 32 * slot]
            target = sector ^ FLIPS[q]
            edge_ref[pair, slot, target, :, 0:width] = gs_ref[pair, q, target, 0:32, 0:width] + more

    for pair in range(PAIRS):
        for f in range(7):
            if PLACE[f][0] == pair:
                seam_operand(f)
        for sector in range(8):
            refine_seam(pair, sector)

    row, a_edge, b_edge, c_edge = row_kinds(count)

    table = table_ref[...]
    packed = block(9)
    theirs = packed[16:40] + packed[40:64]
    lane_ix = positions((24, count))[0]
    at_low = 0.5 * (table + jnp.where(lane_ix == 0, theirs, roll(table, layer)))
    at_high = 0.5 * (table + jnp.where(lane_ix == 0, roll(table, -layer), theirs))

    def by_radius(source, at, side):
        return jnp.where(c_edge, line_of(source, at + 1 + side), line_of(source, at))

    for one in range(2):
        edge = at_low if one == 0 else at_high
        for two in range(2):
            at = one * 2 + two
            outside = by_radius(edge, 9, two)[0:32]
            edge_factor_ref[at] = jnp.where(a_edge[0:32], outside, factor_ref[4 + at, 0:32, :])
            outside = jnp.where(b_edge[0:32], line_of(edge, 13 + two), line_of(edge, 12))
            edge_factor_ref[4 + at] = jnp.where(a_edge[0:32], outside, factor_ref[8 + at, 0:32, :])

    def with_added(parts):
        halves = []
        for part in parts:
            stacked = part.reshape(EXT, NI, count)
            halves.append(jnp.concatenate([part, seam_rows(radial_added(stacked))], axis=0))
        return jnp.concatenate(halves, axis=1).astype(BF)

    def lift(at, rows, operand):
        return dot(const_ref[at : at + rows, 0 : 2 * SEAM], operand)

    stream = []
    for i in range(2):
        shared = jnp.where(ix == 0, end_high, end_low) * seam[4 + i]
        stream.append(block(7 + i) + shared)
    lifted = lift(lift_x_at, ROWS, with_added(stream))
    for one in range(2):
        for two in range(2):
            at = one * 2 + two
            scale = jnp.where(
                b_edge, by_radius(theirs, 3 + 3 * one, two), by_radius(theirs, 0, two)
            )[0:32]
            for i in range(2):
                part = lifted[at * 32 : at * 32 + 32, i * count : (i + 1) * count]
                normal_x_ref[i, at] = part * scale

    iy3 = positions((1, 1, count))[1]
    iy2 = iy3[0]
    azim = []
    for i, f in enumerate((3, 5)):
        factor = jnp.where(iy3 == 0, end_high, end_low)
        values = ext_ref[f]
        halo = block(f).reshape(EXT, NI, count)
        near = jnp.where(
            iy3 == 0, values[:, 0] + values[:, NI], values[:, NI - 1] + values[:, NI + 1]
        )
        own = ends_ref[i] + factor * near
        near = jnp.where(iy2 == 0, halo[0] + halo[NI], halo[NI - 1] + halo[NI + 1])
        other = packed[8 * i : 8 * i + 8] + factor[0] * near
        low, high = stream_added(own[0], own[NI - 1], other)
        azim.append(jnp.concatenate([rows2(own), low, high], axis=0))
    span = 8 * len(GROUPS)
    lifted = lift(lift_y_at, 4 * span, with_added(azim))
    for one in range(2):
        edge = at_low if one == 0 else at_high
        for two in range(2):
            at = one * 2 + two
            scale = jnp.where(a_edge, by_radius(edge, 15, two), by_radius(table, 15, two))
            for i in range(2):
                for k, start in enumerate(GROUPS):
                    rows = slice(at * span + 8 * k, at * span + 8 * k + 8)
                    part = lifted[rows, i * count : (i + 1) * count]
                    normal_y_ref[i, at, start : start + 8] = part * scale[start : start + 8]

    def parts_of(f, q, at, edge):
        pair, side = PLACE[f]
        lanes = slice(side * count, (side + 1) * count)
        if q == 1:
            return [along_ref[pair, sector, at, lanes] for sector in range(8)]
        if edge:
            slot = (0, None, 1, 2)[q]
            return [edge_ref[pair, slot, sector, at, lanes] for sector in range(8)]
        return [gs_ref[pair, q, sector, at, lanes] for sector in range(8)]

    chunk = 16

    def vorticity(at, start, edge):
        shape = (chunk, count)
        lane_ix, lane_iy, lane_iz = positions(shape)
        rows = lax.broadcasted_iota(jnp.int32, shape, 0) + start
        on_a = rows < HO * HO
        on_b = lax.rem(rows, HO * HO) < HO
        on_c = lax.rem(rows, HO) == 0

        def factor_at(which):
            if edge and which >= 4:
                return edge_factor_ref[which - 4, at, :]
            return factor_ref[which, at, :]

        def nodal(f, q, factor):
            g = unfold(parts_of(f, q, at, edge))
            for s in range(8):
                nodal_ref[kept(f - 3, q - 1), s, at, :] = g[s]
            return [g[s] * factor_at(factor(s)) for s in range(8)]

        def along_x(i, f):
            g = nodal(f, 1, lambda s: s % 4)
            if edge:
                for two in range(4):
                    low, high = g[two], g[4 + two]
                    normal = normal_x_ref[i, two, at, :]
                    near = lane_ix == 0
                    first = 0.5 * (low + jnp.where(near, normal, roll(high, layer)))
                    last = 0.5 * (high + jnp.where(near, roll(low, -layer), normal))
                    g[two] = jnp.where(on_a, first, low)
                    g[4 + two] = jnp.where(on_a, last, high)
            return g

        def along_y(i, f):
            g = nodal(f, 2, lambda s: 4 + s // 4 * 2 + s % 2)
            for two in range(4):
                here = two // 2 * 4 + two % 2
                low, high = g[here], g[here + 2]
                normal = normal_y_ref[i, two, at, :]
                first = 0.5 * (low + jnp.where(lane_iy == 0, normal, roll(high, EZ)))
                last = 0.5 * (high + jnp.where(lane_iy == EY - 1, normal, roll(low, -EZ)))
                g[here] = jnp.where(on_b, first, low)
                g[here + 2] = jnp.where(on_b, last, high)
            return g

        def along_z(f):
            g = nodal(f, 3, lambda s: 8 + s // 2)
            lower = on_c & (lane_iz > 0)
            upper = on_c & (lane_iz < EZ - 1)
            for two in range(4):
                low, high = g[2 * two], g[2 * two + 1]
                g[2 * two] = jnp.where(lower, 0.5 * (low + roll(high, 1)), low)
                g[2 * two + 1] = jnp.where(upper, 0.5 * (high + roll(low, -1)), high)
            return g

        pairs = (
            (lambda: along_y(1, 5), lambda: along_z(4)),
            (lambda: along_z(3), lambda: along_x(1, 5)),
            (lambda: along_x(0, 4), lambda: along_y(0, 3)),
        )
        for i, (plus, minus) in enumerate(pairs):
            one, two = plus(), minus()
            folded = unfold([0.125 * (one[s] - two[s]) for s in range(8)])
            for sector in range(8):
                vort_ref[i, sector, at, :] = folded[sector].astype(BF)

    for step in range(2):
        vorticity(slice(step * chunk, (step + 1) * chunk), step * chunk, True)

    def vorticity_step(step, carry):
        start = pl.multiple_of(step * chunk, chunk)
        vorticity(pl.ds(start, chunk), start, False)
        return carry

    lax.fori_loop(2, ROWS // chunk, vorticity_step, 0, unroll=2)

    metric = [metric_ref[i : i + 1] for i in range(3)]
    inv = inv_ref[0]
    scaled = [inv * metric[i] for i in range(3)]
    taken = ((1, 2), (2, 0), (0, 1))
    terms = (((1, 0), (2, 1)), ((2, 0), (0, 1)), ((0, 0), (1, 1)))
    for target in range(8):
        slope = []
        for axis in range(3):
            flip = FLIPS[1 + axis]
            sector = target ^ flip
            source = jnp.concatenate([vort_ref[i, sector] for i in taken[axis]], axis=1)
            source = jnp.concatenate([source, source], axis=0)
            at = second_at + (2 * axis + (1 if sector & flip else 0)) * ROWS
            slope.append(dot(const_ref[at : at + ROWS, :], source))
        for i in range(3):
            (one, half), (two, other) = terms[i]
            plus = scaled[one] * slope[one][:, half * count : (half + 1) * count]
            minus = scaled[two] * slope[two][:, other * count : (other + 1) * count]
            if i == 0:
                linear_ref[i, target] = along_ref[3, target, :, 0:count] * metric[0] + (plus - minus)
            else:
                near = edge_ref[3, i, target, :, 0:count] * metric[i]
                far = gs_ref[3, 1 + i, target, 32:, 0:count] * metric[i]
                linear_ref[i, target, 0:32, :] = near + (plus - minus)[0:32]
                linear_ref[i, target, 32:, :] = far + (plus - minus)[32:]

    def body(edge, step, total):
        at = pl.ds(pl.multiple_of(step * 8, 8), 8)
        for side in range(2):
            total = total + quad_ref[at, :] * energy_of(at, side, edge)
        return total

    def energy_of(at, side, edge):
        def unfold_half(parts):
            return unfold4([signed(parts[s], parts[4 + s], side) for s in range(4)])

        def part(f, q):
            return unfold_half(parts_of(f, q, at, edge))

        base = [[item * metric[j] for item in part(j, 0)] for j in range(3)]
        dual = [part(3 + j, 0) for j in range(3)]
        energy = spread = None
        for i in range(3):
            total = unfold_half([linear_ref[i, s, at, :] for s in range(8)])
            for j in range(3):
                if i == j:
                    slope = part(3 + i, 1 + j)
                else:
                    slope = [nodal_ref[kept(i, j), side * 4 + s, at, :] for s in range(4)]
                total = [total[s] - base[j][s] * slope[s] for s in range(4)]
                if i == j:
                    more = [slope[s] * metric[i] for s in range(4)]
                    spread = more if i == 0 else [spread[s] + more[s] for s in range(4)]
            inner = None
            for j in range(3):
                slope = part(j, 1 + i)
                more = [dual[j][s] * slope[s] for s in range(4)]
                inner = more if j == 0 else [inner[s] + more[s] for s in range(4)]
            total = [total[s] + metric[i] * inner[s] for s in range(4)]
            more = [item * item for item in total]
            energy = more if i == 0 else [energy[s] + more[s] for s in range(4)]
        energy = [energy[s] + spread[s] * spread[s] for s in range(4)]
        return (energy[0] + energy[1]) + (energy[2] + energy[3])

    total = jnp.zeros((8, count), F32)
    total = lax.fori_loop(0, 4, functools.partial(body, True), total, unroll=2)
    total = lax.fori_loop(4, ROWS // 8, functools.partial(body, False), total, unroll=2)
    weighted = jnp.sum(total, axis=0, keepdims=True)
    result = jnp.sqrt(weighted / 8.0) / float(ORDER_OUT**2)
    high, mid, low = split3(result)
    stacked = jnp.concatenate(
        [high.astype(F32), mid.astype(F32), low.astype(F32), jnp.zeros((13, count), F32)], axis=0
    )
    moved = dot(stacked.astype(BF), slots_ref[...])
    out_ref[...] = moved[0:1] + moved[1:2] + moved[2:3]


def kept(component, axis):
    return component * 2 + (axis if axis < component else axis - 1)


def unfold4(parts):
    plus0, minus0 = parts[0] + parts[1], parts[0] - parts[1]
    plus1, minus1 = parts[2] + parts[3], parts[2] - parts[3]
    return [plus0 + plus1, minus0 + minus1, plus0 - plus1, minus0 - minus1]


def unfold(parts):
    plus = unfold4([parts[s] + parts[4 + s] for s in range(4)])
    minus = unfold4([parts[s] - parts[4 + s] for s in range(4)])
    return plus + minus


MIB = 1024 * 1024


def per_device(fields, elem_map, metric, inv_reynolds):
    refine, const, weights, (line, ends_value) = tables()
    count = fields.shape[-1]
    vmem = pl.BlockSpec(memory_space=pltpu.VMEM)

    def params(mib):
        return pltpu.CompilerParams(vmem_limit_bytes=mib * MIB)

    def struct(shape, dtype=F32):
        return jax.ShapeDtypeStruct(shape, dtype)

    hbm = pl.BlockSpec(memory_space=pltpu.HBM)
    inputs = [
        pltpu.with_memory_space_constraint(item, pltpu.HBM)
        for item in (fields, elem_map, metric, jnp.asarray(refine), jnp.asarray(const))
    ]
    slots, local_metric, message, near_fields, refine = pl.pallas_call(
        functools.partial(first_kernel, line),
        out_shape=(
            struct((count, count), BF),
            struct((8, count)),
            struct((9 * 64 + 16, count), BF),
            struct(fields.shape, BF),
            struct(refine.shape, BF),
        ),
        in_specs=[hbm] * 4,
        out_specs=(vmem,) * 5,
        scratch_shapes=[
            pltpu.VMEM(elem_map.shape, jnp.int32),
            pltpu.VMEM(metric.shape, F32),
            pltpu.SemaphoreType.DMA((17,)),
        ],
        compiler_params=params(6),
        name="first",
    )(*inputs[:4])

    coarse = pl.pallas_call(
        own_kernel,
        out_shape=struct((7, NI, NI, NI, count)),
        in_specs=[vmem] * 2,
        out_specs=vmem,
        compiler_params=params(6),
        cost_estimate=pl.CostEstimate(
            flops=2 * fields.size * count, bytes_accessed=3 * 10**6, transcendentals=0
        ),
        name="own",
    )(near_fields, slots)

    azim = lax.axis_size("azim")
    if azim == 2:
        halo = lax.ppermute(message, "azim", [(0, 1), (1, 0)])
    else:
        ahead = lax.ppermute(message, "azim", [(i, (i + 1) % azim) for i in range(azim)])
        behind = lax.ppermute(message, "azim", [((i + 1) % azim, i) for i in range(azim)])
        iy = (jnp.arange(count) // EZ) % EY
        halo = jnp.where(iy >= EY // 2, ahead, behind)

    streams = lax.axis_size("strm")
    even_ring = streams % 2 == 0
    extended, ends, table, to_a, to_b = pl.pallas_call(
        functools.partial(second_kernel, line, even_ring),
        out_shape=(
            struct((7, NI, EXT, NI, count)),
            struct((2, NI, NI, count)),
            struct((24, count)),
            struct((5 * SEAM, count), BF),
            struct((5 * SEAM, count), BF),
        ),
        in_specs=[vmem] * 3,
        out_specs=(vmem,) * 5,
        compiler_params=params(12),
        name="second",
    )(coarse, local_metric, halo)

    if even_ring:
        near = [(i, i ^ 1) for i in range(streams)]
        far = []
        for i in range(1, streams, 2):
            far += [(i, (i + 1) % streams), ((i + 1) % streams, i)]
        got_a = lax.ppermute(to_a, "strm", near)
        got_b = lax.ppermute(to_b, "strm", far)
    else:
        got_b = lax.ppermute(to_a, "strm", [(i, (i + 1) % streams) for i in range(streams)])
        got_a = lax.ppermute(to_b, "strm", [((i + 1) % streams, i) for i in range(streams)])

    raw, const, factor, quad = pl.pallas_call(
        functools.partial(third_kernel, weights),
        out_shape=(
            struct((PAIRS, 4, 8, ROWS, 2 * count)),
            struct(const.shape, BF),
            struct((12, ROWS, count)),
            struct((ROWS, count)),
        ),
        in_specs=[vmem] * 3 + [hbm],
        out_specs=(vmem,) * 4,
        scratch_shapes=[
            pltpu.VMEM((8, HO * HI * NI, count), F32),
            pltpu.VMEM((PAIRS, 8, ROWS, 2 * count), BF),
            pltpu.SemaphoreType.DMA((8,)),
        ],
        compiler_params=params(8),
        cost_estimate=pl.CostEstimate(
            flops=4 * 10**9, bytes_accessed=20 * 10**6, transcendentals=0
        ),
        name="third",
    )(extended, table, refine, inputs[4])

    result = pl.pallas_call(
        functools.partial(fourth_kernel, ends_value, even_ring),
        out_shape=struct((1, count)),
        in_specs=[pl.BlockSpec(memory_space=pltpu.SMEM)] + [vmem] * 11,
        out_specs=vmem,
        scratch_shapes=[
            pltpu.VMEM((8, NI * NI, count), F32),
            pltpu.VMEM((PAIRS, 8, ROWS, 2 * count), F32),
            pltpu.VMEM((PAIRS, 3, 8, 32, 2 * count), F32),
            pltpu.VMEM((3, 8, ROWS, count), BF),
            pltpu.VMEM((3, 8, ROWS, count), F32),
            pltpu.VMEM((8, 32, count), F32),
            pltpu.VMEM((2, 4, 32, count), F32),
            pltpu.VMEM((2, 4, ROWS, count), F32),
            pltpu.VMEM((PAIRS, 8, 48, 2 * count), BF),
            pltpu.VMEM((6, 8, ROWS, count), F32),
        ],
        compiler_params=params(20),
        name="fourth",
    )(
        inv_reynolds,
        raw,
        factor,
        quad,
        extended,
        ends,
        table,
        local_metric,
        slots,
        got_a,
        got_b,
        const,
    )
    return result.reshape(count)


def solution(mesh):
    return jax.shard_map(
        per_device,
        mesh=mesh,
        in_specs=(
            P(None, None, ("grp", "strm", "azim")),
            P(("strm", "azim"), None),
            P(None, ("strm", "azim")),
            P("grp"),
        ),
        out_specs=P(("grp", "strm", "azim")),
        check_vma=False,
    )
```

```python
import functools

import jax
import jax.numpy as jnp
import numpy as np
from jax import lax
from jax.experimental import pallas as pl
from jax.experimental.pallas import tpu as pltpu
from jax.sharding import PartitionSpec as P

ORDER_IN = 7
ORDER_OUT = 9
EY = 8
EZ = 8
NI = ORDER_IN + 1
NO = ORDER_OUT + 1
HI = NI // 2
HO = NO // 2
ROWS = 128
SEAM_ROWS = ROWS + 2 * 32
GROUPS = sorted({row // 8 * 8 for row in range(HO**3) if row % (HO * HO) < HO})
EXT = NI + 2
SEAM = EXT * NI
BF = jnp.bfloat16
F32 = jnp.float32
PLACE = {3: (0, 0), 4: (0, 1), 5: (1, 0), 0: (1, 1), 1: (2, 0), 2: (2, 1), 6: (3, 0)}
PAIRS = 4
FLIPS = (0, 4, 2, 1)


def gll_table(extent):
    degree = extent - 1
    points = np.cos(np.pi * np.arange(extent) / degree)
    legendre = np.zeros((extent, extent))

    def fill():
        legendre[:, 0] = 1.0
        legendre[:, 1] = points
        for level in range(2, extent):
            legendre[:, level] = (
                (2 * level - 1) * points * legendre[:, level - 1]
                - (level - 1) * legendre[:, level - 2]
            ) / level

    for sweep in range(100):
        fill()
        points = points - (points * legendre[:, degree] - legendre[:, degree - 1]) / (
            extent * legendre[:, degree]
        )
    fill()
    weights = 2.0 / (degree * extent * legendre[:, degree] ** 2)
    return (points[::-1].copy(), weights[::-1].copy())


def lagrange_matrix(source, target):
    result = np.ones((len(target), len(source)))
    for column in range(len(source)):
        for partner in range(len(source)):
            if partner != column:
                result[:, column] *= (target - source[partner]) / (source[column] - source[partner])
    return result


def derivative_matrix(points):
    extent = len(points)
    identity = np.eye(extent)
    spacing = points[:, None] - points[None, :] + identity
    barycen = 1.0 / np.prod(spacing, axis=1)
    matrix = barycen[None, :] / barycen[:, None] / spacing * (1.0 - identity)
    return matrix - identity * matrix.sum(axis=1)[:, None]


def bf16_parts(matrix):
    high = matrix.astype(jnp.bfloat16)
    low = (matrix - high.astype(np.float64)).astype(jnp.bfloat16)
    return high, low


def pad_rows(matrix, rows):
    return np.concatenate([matrix, np.zeros((rows - matrix.shape[0],) + matrix.shape[1:])])


def two_terms(matrix):
    return np.concatenate(bf16_parts(matrix), axis=-1)


@functools.cache
def tables():
    coarse, unused = gll_table(NI)
    fine, weights = gll_table(NO)
    interp = lagrange_matrix(coarse, fine)
    slopes = derivative_matrix(fine)
    ends = np.eye(NO)[:, [0, NO - 1]]
    value = np.concatenate([interp, ends], axis=1)
    both = slopes @ value

    def folded(matrix, parity):
        sign = 1.0 - 2.0 * parity
        if matrix.shape[1] == EXT and matrix is not slopes:
            left = matrix[:HO, [0, 1, 2, 3, 8]]
            right = matrix[:HO, [7, 6, 5, 4, 9]]
        else:
            left = matrix[:HO, :HO]
            right = matrix[:HO, ::-1][:, :HO]
        return left + sign * right

    refine, seams = [], []
    for sector in range(8):
        pa, pb, pc = sector // 4, sector // 2 % 2, sector % 2
        blocks, ends_of = [], []
        for ta, tb, tc in (
            (value, value, value),
            (both, value, value),
            (value, both, value),
            (value, value, both),
        ):
            block = 0.125 * np.einsum(
                "ap,bq,cr->abcrpq", folded(ta, pa), folded(tb, pb), folded(tc, pc)
            ).reshape(HO**3, HO, HO, HO)
            own = np.zeros((HO**3, HO, 24))
            own[:, :, : HO * HI] = block[:, :, :HI].reshape(HO**3, HO, HO * HI)
            own = np.pad(own.reshape(HO**3, -1), ((0, 0), (0, ROWS - 24 * HO)))
            blocks.append(pad_rows(own, ROWS))
            added = np.zeros((HO**3, 48))
            added[:, : 8 * HO] = np.pad(block[:, :, HI], ((0, 0), (0, 0), (0, 3))).reshape(HO**3, -1)
            ends_of.append(added)
        refine.append(two_terms(np.concatenate(blocks)))
        rows = [pad_rows(ends_of[1], ROWS)]
        rows += [pad_rows(ends_of[q][: HO * HO], 32) for q in (2, 3)]
        seams.append(np.pad(two_terms(np.concatenate(rows)), ((0, 0), (0, ROWS - 96))))
    refine = np.stack(refine)
    seams = [np.concatenate(seams[2 * i : 2 * i + 2], axis=1) for i in range(4)]

    second = []
    eye = np.eye(HO)
    for axis in range(3):
        for parity in range(2):
            factors = [eye, eye, eye]
            factors[axis] = folded(slopes, parity)
            block = np.kron(np.kron(factors[0], factors[1]), factors[2])
            edge = ROWS - HO**3
            second.append(two_terms(np.pad(block, ((0, edge), (0, edge)))))
    second = np.stack(second)

    def half(side):
        return value[:HO] if side == 0 else value[::-1][:HO]

    lift_x, lift_y = [], []
    for side in range(2):
        for radial in range(2):
            plain = np.zeros((HO, EXT, HO, NI))
            added = np.zeros((HO, EXT, HO, NI))
            plain[...] = np.einsum("ap,cr->apcr", half(side), half(radial)[:, :NI])
            added[..., 0] = np.einsum("ap,c->apc", half(side), half(radial)[:, NI])
            added[..., NI - 1] = np.einsum("ap,c->apc", half(side), half(radial)[:, NI + 1])
            face = np.stack([plain, added]).transpose(1, 3, 0, 2, 4).reshape(HO, HO, 2 * SEAM)
            lift_x.append(pad_rows(face.reshape(HO * HO, -1), 32))
            spread = np.zeros((HO, HO, HO, 2 * SEAM))
            spread[:, 0] = face
            spread = pad_rows(spread.reshape(HO**3, -1), ROWS)
            lift_y.append(np.concatenate([spread[at : at + 8] for at in GROUPS]))

    def one_term(parts):
        matrix = np.concatenate(parts)
        edge = 2 * ROWS - matrix.shape[1]
        return np.pad(matrix, ((0, 0), (0, edge))).astype(jnp.bfloat16)

    refine = refine.reshape(-1, 2 * ROWS)
    const = np.concatenate(
        seams + [second.reshape(-1, 2 * ROWS), one_term(lift_x), one_term(lift_y)]
    )
    half_weights = [float(v) for v in weights[:HO]]
    line = []
    for end, far in ((0, NO - 1), (NO - 1, 0)):
        weights_in = slopes[end].copy()
        weights_in[[0, NO - 1]] = 0.0
        line.append(([float(v) for v in weights_in @ interp], float(slopes[end, far])))
    ratio = [1.0 / float(both[0, NI] + sign * both[0, NI + 1]) for sign in (1.0, -1.0)]
    ends = (float(slopes[0, 0]), float(slopes[NO - 1, NO - 1]), ratio)
    return refine, const, half_weights, (line, ends)


def dot(a, b, contract_last=False):
    dims = (((1,), (1 if contract_last else 0,)), ((), ()))
    return lax.dot_general(a, b, dims, preferred_element_type=F32)


def is_even(even_ring):
    return lax.rem(lax.axis_index("strm"), 2) == 0 if even_ring else True


def rows3(x):
    return x.reshape(NI, NI, x.shape[-1])


def seam_rows(x):
    return x.reshape(SEAM, x.shape[-1])


def rows2(x):
    return x.reshape(NI * NI, x.shape[-1])


def roll(x, shift):
    count = x.shape[-1]
    return pltpu.roll(x, shift % count, x.ndim - 1)


def positions(shape):
    lane = lax.broadcasted_iota(jnp.int32, shape, len(shape) - 1)
    return lax.div(lane, EY * EZ), lax.rem(lax.div(lane, EZ), EY), lax.rem(lane, EZ)


def split3(x):
    high = x.astype(BF)
    rest = x - high.astype(F32)
    mid = rest.astype(BF)
    low = (rest - mid.astype(F32)).astype(BF)
    return high, mid, low


def radial_added(x):
    axis = x.ndim - 2
    shape = (1,) * axis + x.shape[-2:]
    node = lax.broadcasted_iota(jnp.int32, shape, axis)
    iz = positions(shape)[2]
    last = x.shape[-2] - 1
    before = pltpu.roll(roll(x, 1), 1, axis)
    after = pltpu.roll(roll(x, -1), last, axis)
    low = (node == 0) & (iz > 0)
    high = (node == last) & (iz < EZ - 1)
    other = jnp.where(low, before, jnp.where(high, after, x))
    return 0.5 * (other - x)


def end_lines(line, planes, step):
    (near, near_far), (high, high_far) = line
    first, last = planes[0], planes[-1]
    one = near_far * 0.5 * (last + roll(first, -step))
    two = high_far * 0.5 * (first + roll(last, step))
    for i, plane in enumerate(planes):
        one = one + near[i] * plane
        two = two + high[i] * plane
    return one, two


def chunks(source, target, sem, count=8):
    step = source.shape[0] // count
    return [
        pltpu.make_async_copy(
            source.at[i * step : (i + 1) * step], target.at[i * step : (i + 1) * step], sem.at[i]
        )
        for i in range(count)
    ]


def first_kernel(
    line,
    fields_hbm,
    emap_hbm,
    metric_hbm,
    table_hbm,
    slots_ref,
    metric_out,
    msg_ref,
    fields,
    table_ref,
    emap,
    metric,
    sem,
):
    count = fields.shape[-1]
    order = (3, 5, 4, 0, 1, 2, 6)
    small = [
        pltpu.make_async_copy(emap_hbm, emap, sem.at[7]),
        pltpu.make_async_copy(metric_hbm, metric, sem.at[8]),
    ]
    large = [pltpu.make_async_copy(fields_hbm.at[f], fields.at[f], sem.at[f]) for f in order]
    tables_copies = chunks(table_hbm, table_ref, sem.at[pl.ds(9, 8)])
    for copy in small + large + tables_copies:
        copy.start()
    for copy in small + large:
        copy.wait()
    local = lax.broadcasted_iota(jnp.int32, (count, count), 0)
    slots = (local == emap[...]).astype(F32).astype(BF)
    slots_ref[...] = slots
    iy = positions((1, 1, count))[1]
    for f in order:
        if f in (3, 5):
            values = dot(fields[f], slots, True).reshape(NI, NI, NI, count)
            first, last = values[:, 0], values[:, NI - 1]
        else:
            planes = fields[f].reshape(NI, NI, NI, count)
            planes = jnp.concatenate([planes[:, 0], planes[:, NI - 1]], axis=0)
            planes = dot(planes.reshape(2 * NI * NI, count), slots, True)
            first, last = rows3(planes[0:64]), rows3(planes[64:128])
        face = jnp.where(iy == 0, first, last)
        msg_ref[f * 64 : f * 64 + 64, :] = rows2(face).astype(BF)
        if f in (3, 5):
            low, high = end_lines(line, [values[:, b] for b in range(NI)], EZ)
            at = (7 + (f == 5)) * 64
            msg_ref[at : at + 64, :] = rows2(jnp.where(iy == 0, low, high)).astype(BF)
    high, mid, low = split3(metric[...])
    pad = jnp.zeros((7, count), F32)
    stacked = jnp.concatenate([high.astype(F32), mid.astype(F32), low.astype(F32), pad], axis=0)
    moved = dot(stacked.astype(BF), slots, True)
    local = moved[0:3] + moved[3:6] + moved[6:9]
    metric_out[...] = jnp.concatenate([local, jnp.zeros((5, count), F32)], axis=0)
    high = local.astype(BF).astype(F32)
    tail = jnp.concatenate([high, local - high, jnp.zeros((10, count), F32)], axis=0)
    msg_ref[9 * 64 : 9 * 64 + 16, :] = tail.astype(BF)
    for copy in tables_copies:
        copy.wait()


def own_kernel(fields_ref, slots_ref, coarse_ref):
    count = fields_ref.shape[-1]
    for f in range(7):
        values = dot(fields_ref[f], slots_ref[...], True)
        coarse_ref[f] = values.reshape(NI, NI, NI, count)


def from_azim(x, iy):
    gap = (EY - 1) * EZ
    return jnp.where(iy == 0, roll(x, -gap), roll(x, gap))


def metric_classes(x, halo, shift, at_low, at_high):
    low = 0.5 * (x + jnp.where(at_low, halo, roll(x, shift)))
    high = 0.5 * (x + jnp.where(at_high, halo, roll(x, -shift)))
    return [x, low, high]


def radial_classes(x, iz):
    low = jnp.where(iz > 0, 0.5 * (x + roll(x, 1)), x)
    high = jnp.where(iz < EZ - 1, 0.5 * (x + roll(x, -1)), x)
    return [x, low, high]


def second_kernel(
    line, even_ring, coarse_ref, metric_ref, halo_ref, ext_ref, ends_ref, table_ref, a_ref, b_ref
):
    count = coarse_ref.shape[-1]
    layer = EY * EZ
    ix, iy, iz = positions((1, 1, count))
    blocks = []
    lines = []
    for f in range(7):
        values = coarse_ref[f]
        first, last = values[:, 0], values[:, NI - 1]
        halo = from_azim(rows3(halo_ref[f * 64 : f * 64 + 64, :].astype(F32)), iy)
        low = 0.5 * (jnp.where(iy == 0, halo, roll(last, EZ)) - first)
        high = 0.5 * (jnp.where(iy == EY - 1, halo, roll(first, -EZ)) - last)
        values = jnp.concatenate([values, low[:, None], high[:, None]], axis=1)
        ext_ref[f] = values
        blocks.append(seam_rows(jnp.where(ix == 0, values[0], values[NI - 1])))
        if f in (4, 5):
            low, high = end_lines(line, [values[a] for a in range(NI)], layer)
            lines.append(seam_rows(jnp.where(ix == 0, low, high)))
    blocks += lines
    extra = []
    for i in range(2):
        ends = from_azim(rows3(halo_ref[(7 + i) * 64 : (8 + i) * 64, :].astype(F32)), iy)
        ends_ref[i] = ends
        extra.append(jnp.where(ix[0] == 0, ends[0], ends[NI - 1]))

    ix, iy, iz = positions((1, count))
    packed = halo_ref[9 * 64 : 9 * 64 + 16, :].astype(F32)
    other = from_azim(packed[0:3] + packed[3:6], iy)
    own = metric_ref[...]
    lows, highs = iy == 0, iy == EY - 1
    rows = []
    for item in metric_classes(own[0:1], other[0:1], EZ, lows, highs):
        rows += radial_classes(item, iz)
    rows += radial_classes(own[1:2], iz)
    rows += metric_classes(own[2:3], other[2:3], EZ, lows, highs)
    rows += radial_classes(other[1:2], iz)
    table = jnp.concatenate(rows + [jnp.zeros((24 - len(rows), count), F32)], axis=0)
    table_ref[...] = table
    high = table.astype(BF).astype(F32)
    spare = jnp.zeros((SEAM - 64, count), F32)
    blocks.append(jnp.concatenate(extra + [high, table - high, spare], axis=0))

    ix = positions((SEAM, count))[0]
    even = is_even(even_ring)
    half = len(blocks) // 2
    for i in range(half):
        one, two = blocks[i], blocks[half + i]
        down = jnp.where(ix == 0, one, roll(two, layer))
        up = jnp.where(ix == 0, roll(one, layer), two)
        rows = slice(i * SEAM, (i + 1) * SEAM)
        a_ref[rows, :] = jnp.where(even, up, down).astype(BF)
        b_ref[rows, :] = jnp.where(even, down, up).astype(BF)


def signed(one, two, parity):
    return one + two if parity == 0 else one - two


def radial_fold(rows, iz, parity):
    last = NI - 1
    low = jnp.where(iz > 0, roll(rows[last], 1) - rows[0], 0.0)
    high = jnp.where(iz < EZ - 1, roll(rows[0], -1) - rows[last], 0.0)
    return [signed(rows[c], rows[last - c], parity) for c in range(HI)] + [
        0.5 * signed(low, high, parity)
    ]


def azim_fold(plane, parity):
    return [
        signed(
            plane[b if b < HI else NI], plane[NI - 1 - b if b < HI else NI + 1], parity
        )
        for b in range(HO)
    ]


def row_kinds(count):
    row = lax.broadcasted_iota(jnp.int32, (ROWS, count), 0)
    return row, row < HO * HO, lax.rem(row, HO * HO) < HO, lax.rem(row, HO) == 0


def line_of(source, at):
    return source[at : at + 1]


def row_tables(weights, table, factor_ref, quad_ref):
    count = table.shape[-1]
    row, a_edge, b_edge, c_edge = row_kinds(count)

    def weight_of(index):
        result = jnp.full((ROWS, count), weights[0], F32)
        for i in range(1, HO):
            result = jnp.where(index == i, weights[i], result)
        return result

    a_pos = lax.div(row, HO * HO)
    b_pos = lax.rem(lax.div(row, HO), HO)
    quad = weight_of(a_pos) * weight_of(b_pos) * weight_of(lax.rem(row, HO))
    quad_ref[...] = jnp.where(row < HO**3, quad, 0.0)

    def by_radius(at, side):
        return jnp.where(c_edge, line_of(table, at + 1 + side), line_of(table, at))

    for one in range(2):
        for two in range(2):
            at = one * 2 + two
            factor_ref[at] = jnp.where(b_edge, by_radius(3 + 3 * one, two), by_radius(0, two))
            factor_ref[4 + at] = by_radius(9, two)
            factor_ref[8 + at] = jnp.where(b_edge, line_of(table, 13 + two), line_of(table, 12))


def third_kernel(
    weights,
    ext_ref,
    table_ref,
    const_ref,
    later_hbm,
    gs_ref,
    later_ref,
    factor_ref,
    quad_ref,
    tmp_ref,
    xs_ref,
    sem,
):
    count = ext_ref.shape[-1]
    width = HO * HI
    iz = positions((width, count))[2]
    zeros = jnp.zeros((HI, count), F32)

    copies = chunks(later_hbm, later_ref, sem)
    for copy in copies:
        copy.start()
    row_tables(weights, table_ref[...], factor_ref, quad_ref)
    for f in range(7):
        pair, side = PLACE[f]
        lanes = slice(side * count, (side + 1) * count)
        values = ext_ref[f]
        for pa in range(2):
            mixed = [signed(values[a], values[NI - 1 - a], pa) for a in range(HI)]
            for pb in range(2):
                at = f % 2 * 4 + pa * 2 + pb
                for a in range(HI):
                    for b, item in enumerate(azim_fold(mixed[a], pb)):
                        row = (a * HO + b) * NI
                        tmp_ref[at, row : row + NI, :] = item
                main = [tmp_ref[at, pl.ds(c, width, stride=NI), :] for c in range(NI)]
                for pc in range(2):
                    rows = []
                    for item in radial_fold(main, iz, pc):
                        rows += [item, zeros]
                    rows.append(jnp.zeros((8, count), F32))
                    operand = jnp.concatenate(rows, axis=0).astype(BF)
                    xs_ref[pair, pa * 4 + pb * 2 + pc, :, lanes] = operand

    def refine(sector, carry):
        for pair in range(PAIRS):
            width = 2 * count if pair < PAIRS - 1 else count
            source = xs_ref[pair, sector, :, 0:width]
            source = jnp.concatenate([source, source], axis=0)
            for q in range(0 if pair < PAIRS - 1 else 1, 4):
                rows = pl.ds(sector * 4 * ROWS + q * ROWS, ROWS)
                gs_ref[pair, q, sector ^ FLIPS[q], :, 0:width] = dot(const_ref[rows, :], source)
        return carry

    lax.fori_loop(0, 8, refine, 0, unroll=4)
    for copy in copies:
        copy.wait()


def fourth_kernel(
    ends_value,
    even_ring,
    inv_ref,
    gs_ref,
    factor_ref,
    quad_ref,
    ext_ref,
    ends_ref,
    table_ref,
    metric_ref,
    slots_ref,
    ra_ref,
    rb_ref,
    const_ref,
    out_ref,
    tmp_ref,
    along_ref,
    edge_ref,
    vort_ref,
    linear_ref,
    edge_factor_ref,
    normal_x_ref,
    normal_y_ref,
    xt_ref,
    nodal_ref,
):
    count = ext_ref.shape[-1]
    layer = EY * EZ
    even = is_even(even_ring)
    ix = positions((SEAM, count))[0]
    end_low, end_high, value_of_slope = ends_value
    seam_at = 0
    second_at = seam_at + 4 * SEAM_ROWS
    lift_x_at = second_at + 6 * ROWS
    lift_y_at = lift_x_at + ROWS

    def block(i):
        rows = slice(i % 5 * SEAM, (i % 5 + 1) * SEAM)
        one = ra_ref[rows, :].astype(F32)
        two = rb_ref[rows, :].astype(F32)
        down = jnp.where(even, two, one)
        up = jnp.where(even, one, two)
        if i < 5:
            return jnp.where(ix == 0, down, roll(up, layer))
        return jnp.where(ix == 0, roll(down, layer), up)

    ix3 = positions((1, 1, count))[0]
    iz8 = positions((NI, count))[2]

    def stream_added(first, last, halo):
        lane = positions((1,) * (first.ndim - 1) + (count,))[0]
        low = 0.5 * (jnp.where(lane == 0, halo, roll(last, layer)) - first)
        high = 0.5 * (jnp.where(lane == 0, roll(first, -layer), halo) - last)
        return low, high

    seam = {}
    tmp_ref[...] = jnp.zeros(tmp_ref.shape, F32)

    def seam_operand(f):
        pair, side = PLACE[f]
        lanes = slice(side * count, (side + 1) * count)
        halo = block(f).reshape(EXT, NI, count)
        first, last = ext_ref[f, 0], ext_ref[f, NI - 1]
        low, high = stream_added(first, last, halo)
        if f in (4, 5):
            seam[f] = seam_rows(jnp.where(ix3 == 0, first + low, last + high))
        for pa in range(2):
            mixed = signed(low, high, pa)
            for pb in range(2):
                at = f % 2 * 4 + pa * 2 + pb
                for b, item in enumerate(azim_fold(mixed, pb)):
                    tmp_ref[at, b * NI : (b + 1) * NI, :] = item
                main = [tmp_ref[at, pl.ds(c, NI, stride=NI), :] for c in range(NI)]
                for pc in range(2):
                    rows = radial_fold(main, iz8, pc)
                    rows.append(jnp.zeros((NI, count), F32))
                    operand = jnp.concatenate(rows, axis=0).astype(BF)
                    xt_ref[pair, pa * 4 + pb * 2 + pc, :, lanes] = operand

    first_nodes = lax.broadcasted_iota(jnp.int32, (32, 2 * count), 0) < HO * HO

    def refine_seam(pair, sector):
        at = seam_at + (sector // 2) * SEAM_ROWS
        half = sector % 2 * ROWS
        matrix = const_ref[at : at + SEAM_ROWS, half : half + 2 * 48]
        width = 2 * count if pair < PAIRS - 1 else count
        source = xt_ref[pair, sector, :, 0:width]
        added = dot(matrix, jnp.concatenate([source, source], axis=0))
        target = sector ^ 4
        along_ref[pair, target, :, 0:width] = gs_ref[pair, 1, target, :, 0:width] + added[0:ROWS]
        for q, slot in ((0, 0), (2, 1), (3, 2)):
            if q == 0 and pair == PAIRS - 1:
                continue
            if q == 0:
                more = added[0:32] * value_of_slope[sector // 4]
                more = jnp.where(first_nodes[:, 0:width], more, 0.0)
            else:
                more = added[ROWS + 32 * (slot - 1) : ROWS + 32 * slot]
            target = sector ^ FLIPS[q]
            edge_ref[pair, slot, target, :, 0:width] = gs_ref[pair, q, target, 0:32, 0:width] + more

    for pair in range(PAIRS):
        for f in range(7):
            if PLACE[f][0] == pair:
                seam_operand(f)
        for sector in range(8):
            refine_seam(pair, sector)

    row, a_edge, b_edge, c_edge = row_kinds(count)

    table = table_ref[...]
    packed = block(9)
    theirs = packed[16:40] + packed[40:64]
    lane_ix = positions((24, count))[0]
    at_low = 0.5 * (table + jnp.where(lane_ix == 0, theirs, roll(table, layer)))
    at_high = 0.5 * (table + jnp.where(lane_ix == 0, roll(table, -layer), theirs))

    def by_radius(source, at, side):
        return jnp.where(c_edge, line_of(source, at + 1 + side), line_of(source, at))

    for one in range(2):
        edge = at_low if one == 0 else at_high
        for two in range(2):
            at = one * 2 + two
            outside = by_radius(edge, 9, two)[0:32]
            edge_factor_ref[at] = jnp.where(a_edge[0:32], outside, factor_ref[4 + at, 0:32, :])
            outside = jnp.where(b_edge[0:32], line_of(edge, 13 + two), line_of(edge, 12))
            edge_factor_ref[4 + at] = jnp.where(a_edge[0:32], outside, factor_ref[8 + at, 0:32, :])

    def with_added(parts):
        halves = []
        for part in parts:
            stacked = part.reshape(EXT, NI, count)
            halves.append(jnp.concatenate([part, seam_rows(radial_added(stacked))], axis=0))
        return jnp.concatenate(halves, axis=1).astype(BF)

    def lift(at, rows, operand):
        return dot(const_ref[at : at + rows, 0 : 2 * SEAM], operand)

    stream = []
    for i in range(2):
        shared = jnp.where(ix == 0, end_high, end_low) * seam[4 + i]
        stream.append(block(7 + i) + shared)
    lifted = lift(lift_x_at, ROWS, with_added(stream))
    for one in range(2):
        for two in range(2):
            at = one * 2 + two
            scale = jnp.where(
                b_edge, by_radius(theirs, 3 + 3 * one, two), by_radius(theirs, 0, two)
            )[0:32]
            for i in range(2):
                part = lifted[at * 32 : at * 32 + 32, i * count : (i + 1) * count]
                normal_x_ref[i, at] = part * scale

    iy3 = positions((1, 1, count))[1]
    iy2 = iy3[0]
    azim = []
    for i, f in enumerate((3, 5)):
        factor = jnp.where(iy3 == 0, end_high, end_low)
        values = ext_ref[f]
        halo = block(f).reshape(EXT, NI, count)
        near = jnp.where(
            iy3 == 0, values[:, 0] + values[:, NI], values[:, NI - 1] + values[:, NI + 1]
        )
        own = ends_ref[i] + factor * near
        near = jnp.where(iy2 == 0, halo[0] + halo[NI], halo[NI - 1] + halo[NI + 1])
        other = packed[8 * i : 8 * i + 8] + factor[0] * near
        low, high = stream_added(own[0], own[NI - 1], other)
        azim.append(jnp.concatenate([rows2(own), low, high], axis=0))
    span = 8 * len(GROUPS)
    lifted = lift(lift_y_at, 4 * span, with_added(azim))
    for one in range(2):
        edge = at_low if one == 0 else at_high
        for two in range(2):
            at = one * 2 + two
            scale = jnp.where(a_edge, by_radius(edge, 15, two), by_radius(table, 15, two))
            for i in range(2):
                for k, start in enumerate(GROUPS):
                    rows = slice(at * span + 8 * k, at * span + 8 * k + 8)
                    part = lifted[rows, i * count : (i + 1) * count]
                    normal_y_ref[i, at, start : start + 8] = part * scale[start : start + 8]

    def parts_of(f, q, at, edge):
        pair, side = PLACE[f]
        lanes = slice(side * count, (side + 1) * count)
        if q == 1:
            return [along_ref[pair, sector, at, lanes] for sector in range(8)]
        if edge:
            slot = (0, None, 1, 2)[q]
            return [edge_ref[pair, slot, sector, at, lanes] for sector in range(8)]
        return [gs_ref[pair, q, sector, at, lanes] for sector in range(8)]

    chunk = 16

    def vorticity(at, start, edge):
        shape = (chunk, count)
        lane_ix, lane_iy, lane_iz = positions(shape)
        rows = lax.broadcasted_iota(jnp.int32, shape, 0) + start
        on_a = rows < HO * HO
        on_b = lax.rem(rows, HO * HO) < HO
        on_c = lax.rem(rows, HO) == 0

        def factor_at(which):
            if edge and which >= 4:
                return edge_factor_ref[which - 4, at, :]
            return factor_ref[which, at, :]

        def nodal(f, q, factor):
            g = unfold(parts_of(f, q, at, edge))
            for s in range(8):
                nodal_ref[kept(f - 3, q - 1), s, at, :] = g[s]
            return [g[s] * factor_at(factor(s)) for s in range(8)]

        def along_x(i, f):
            g = nodal(f, 1, lambda s: s % 4)
            if edge:
                for two in range(4):
                    low, high = g[two], g[4 + two]
                    normal = normal_x_ref[i, two, at, :]
                    near = lane_ix == 0
                    first = 0.5 * (low + jnp.where(near, normal, roll(high, layer)))
                    last = 0.5 * (high + jnp.where(near, roll(low, -layer), normal))
                    g[two] = jnp.where(on_a, first, low)
                    g[4 + two] = jnp.where(on_a, last, high)
            return g

        def along_y(i, f):
            g = nodal(f, 2, lambda s: 4 + s // 4 * 2 + s % 2)
            for two in range(4):
                here = two // 2 * 4 + two % 2
                low, high = g[here], g[here + 2]
                normal = normal_y_ref[i, two, at, :]
                first = 0.5 * (low + jnp.where(lane_iy == 0, normal, roll(high, EZ)))
                last = 0.5 * (high + jnp.where(lane_iy == EY - 1, normal, roll(low, -EZ)))
                g[here] = jnp.where(on_b, first, low)
                g[here + 2] = jnp.where(on_b, last, high)
            return g

        def along_z(f):
            g = nodal(f, 3, lambda s: 8 + s // 2)
            lower = on_c & (lane_iz > 0)
            upper = on_c & (lane_iz < EZ - 1)
            for two in range(4):
                low, high = g[2 * two], g[2 * two + 1]
                g[2 * two] = jnp.where(lower, 0.5 * (low + roll(high, 1)), low)
                g[2 * two + 1] = jnp.where(upper, 0.5 * (high + roll(low, -1)), high)
            return g

        pairs = (
            (lambda: along_y(1, 5), lambda: along_z(4)),
            (lambda: along_z(3), lambda: along_x(1, 5)),
            (lambda: along_x(0, 4), lambda: along_y(0, 3)),
        )
        for i, (plus, minus) in enumerate(pairs):
            one, two = plus(), minus()
            folded = unfold([0.125 * (one[s] - two[s]) for s in range(8)])
            for sector in range(8):
                vort_ref[i, sector, at, :] = folded[sector].astype(BF)

    for step in range(2):
        vorticity(slice(step * chunk, (step + 1) * chunk), step * chunk, True)

    def vorticity_step(step, carry):
        start = pl.multiple_of(step * chunk, chunk)
        vorticity(pl.ds(start, chunk), start, False)
        return carry

    lax.fori_loop(2, ROWS // chunk, vorticity_step, 0, unroll=3)

    metric = [metric_ref[i : i + 1] for i in range(3)]
    inv = inv_ref[0]
    scaled = [inv * metric[i] for i in range(3)]
    taken = ((1, 2), (2, 0), (0, 1))
    terms = (((1, 0), (2, 1)), ((2, 0), (0, 1)), ((0, 0), (1, 1)))
    for target in range(8):
        slope = []
        for axis in range(3):
            flip = FLIPS[1 + axis]
            sector = target ^ flip
            source = jnp.concatenate([vort_ref[i, sector] for i in taken[axis]], axis=1)
            source = jnp.concatenate([source, source], axis=0)
            at = second_at + (2 * axis + (1 if sector & flip else 0)) * ROWS
            slope.append(dot(const_ref[at : at + ROWS, :], source))
        for i in range(3):
            (one, half), (two, other) = terms[i]
            plus = scaled[one] * slope[one][:, half * count : (half + 1) * count]
            minus = scaled[two] * slope[two][:, other * count : (other + 1) * count]
            if i == 0:
                linear_ref[i, target] = along_ref[3, target, :, 0:count] * metric[0] + (plus - minus)
            else:
                near = edge_ref[3, i, target, :, 0:count] * metric[i]
                far = gs_ref[3, 1 + i, target, 32:, 0:count] * metric[i]
                linear_ref[i, target, 0:32, :] = near + (plus - minus)[0:32]
                linear_ref[i, target, 32:, :] = far + (plus - minus)[32:]

    def body(edge, step, total):
        at = pl.ds(pl.multiple_of(step * 8, 8), 8)
        for side in range(2):
            total = total + quad_ref[at, :] * energy_of(at, side, edge)
        return total

    def energy_of(at, side, edge):
        def unfold_half(parts):
            return unfold4([signed(parts[s], parts[4 + s], side) for s in range(4)])

        def part(f, q):
            return unfold_half(parts_of(f, q, at, edge))

        base = [[item * metric[j] for item in part(j, 0)] for j in range(3)]
        dual = [part(3 + j, 0) for j in range(3)]
        energy = spread = None
        for i in range(3):
            total = unfold_half([linear_ref[i, s, at, :] for s in range(8)])
            for j in range(3):
                if i == j:
                    slope = part(3 + i, 1 + j)
                else:
                    slope = [nodal_ref[kept(i, j), side * 4 + s, at, :] for s in range(4)]
                total = [total[s] - base[j][s] * slope[s] for s in range(4)]
                if i == j:
                    more = [slope[s] * metric[i] for s in range(4)]
                    spread = more if i == 0 else [spread[s] + more[s] for s in range(4)]
            inner = None
            for j in range(3):
                slope = part(j, 1 + i)
                more = [dual[j][s] * slope[s] for s in range(4)]
                inner = more if j == 0 else [inner[s] + more[s] for s in range(4)]
            total = [total[s] + metric[i] * inner[s] for s in range(4)]
            more = [item * item for item in total]
            energy = more if i == 0 else [energy[s] + more[s] for s in range(4)]
        energy = [energy[s] + spread[s] * spread[s] for s in range(4)]
        return (energy[0] + energy[1]) + (energy[2] + energy[3])

    total = jnp.zeros((8, count), F32)
    total = lax.fori_loop(0, 4, functools.partial(body, True), total, unroll=2)
    total = lax.fori_loop(4, ROWS // 8, functools.partial(body, False), total, unroll=2)
    weighted = jnp.sum(total, axis=0, keepdims=True)
    result = jnp.sqrt(weighted / 8.0) / float(ORDER_OUT**2)
    high, mid, low = split3(result)
    stacked = jnp.concatenate(
        [high.astype(F32), mid.astype(F32), low.astype(F32), jnp.zeros((13, count), F32)], axis=0
    )
    moved = dot(stacked.astype(BF), slots_ref[...])
    out_ref[...] = moved[0:1] + moved[1:2] + moved[2:3]


def kept(component, axis):
    return component * 2 + (axis if axis < component else axis - 1)


def unfold4(parts):
    plus0, minus0 = parts[0] + parts[1], parts[0] - parts[1]
    plus1, minus1 = parts[2] + parts[3], parts[2] - parts[3]
    return [plus0 + plus1, minus0 + minus1, plus0 - plus1, minus0 - minus1]


def unfold(parts):
    plus = unfold4([parts[s] + parts[4 + s] for s in range(4)])
    minus = unfold4([parts[s] - parts[4 + s] for s in range(4)])
    return plus + minus


MIB = 1024 * 1024


def per_device(fields, elem_map, metric, inv_reynolds):
    refine, const, weights, (line, ends_value) = tables()
    count = fields.shape[-1]
    vmem = pl.BlockSpec(memory_space=pltpu.VMEM)

    def params(mib):
        return pltpu.CompilerParams(vmem_limit_bytes=mib * MIB)

    def struct(shape, dtype=F32):
        return jax.ShapeDtypeStruct(shape, dtype)

    hbm = pl.BlockSpec(memory_space=pltpu.HBM)
    inputs = [
        pltpu.with_memory_space_constraint(item, pltpu.HBM)
        for item in (fields, elem_map, metric, jnp.asarray(refine), jnp.asarray(const))
    ]
    slots, local_metric, message, near_fields, refine = pl.pallas_call(
        functools.partial(first_kernel, line),
        out_shape=(
            struct((count, count), BF),
            struct((8, count)),
            struct((9 * 64 + 16, count), BF),
            struct(fields.shape, BF),
            struct(refine.shape, BF),
        ),
        in_specs=[hbm] * 4,
        out_specs=(vmem,) * 5,
        scratch_shapes=[
            pltpu.VMEM(elem_map.shape, jnp.int32),
            pltpu.VMEM(metric.shape, F32),
            pltpu.SemaphoreType.DMA((17,)),
        ],
        compiler_params=params(6),
        name="first",
    )(*inputs[:4])

    coarse = pl.pallas_call(
        own_kernel,
        out_shape=struct((7, NI, NI, NI, count)),
        in_specs=[vmem] * 2,
        out_specs=vmem,
        compiler_params=params(6),
        cost_estimate=pl.CostEstimate(
            flops=2 * fields.size * count, bytes_accessed=3 * 10**6, transcendentals=0
        ),
        name="own",
    )(near_fields, slots)

    azim = lax.axis_size("azim")
    if azim == 2:
        halo = lax.ppermute(message, "azim", [(0, 1), (1, 0)])
    else:
        ahead = lax.ppermute(message, "azim", [(i, (i + 1) % azim) for i in range(azim)])
        behind = lax.ppermute(message, "azim", [((i + 1) % azim, i) for i in range(azim)])
        iy = (jnp.arange(count) // EZ) % EY
        halo = jnp.where(iy >= EY // 2, ahead, behind)

    streams = lax.axis_size("strm")
    even_ring = streams % 2 == 0
    extended, ends, table, to_a, to_b = pl.pallas_call(
        functools.partial(second_kernel, line, even_ring),
        out_shape=(
            struct((7, NI, EXT, NI, count)),
            struct((2, NI, NI, count)),
            struct((24, count)),
            struct((5 * SEAM, count), BF),
            struct((5 * SEAM, count), BF),
        ),
        in_specs=[vmem] * 3,
        out_specs=(vmem,) * 5,
        compiler_params=params(12),
        name="second",
    )(coarse, local_metric, halo)

    if even_ring:
        near = [(i, i ^ 1) for i in range(streams)]
        far = []
        for i in range(1, streams, 2):
            far += [(i, (i + 1) % streams), ((i + 1) % streams, i)]
        got_a = lax.ppermute(to_a, "strm", near)
        got_b = lax.ppermute(to_b, "strm", far)
    else:
        got_b = lax.ppermute(to_a, "strm", [(i, (i + 1) % streams) for i in range(streams)])
        got_a = lax.ppermute(to_b, "strm", [((i + 1) % streams, i) for i in range(streams)])

    raw, const, factor, quad = pl.pallas_call(
        functools.partial(third_kernel, weights),
        out_shape=(
            struct((PAIRS, 4, 8, ROWS, 2 * count)),
            struct(const.shape, BF),
            struct((12, ROWS, count)),
            struct((ROWS, count)),
        ),
        in_specs=[vmem] * 3 + [hbm],
        out_specs=(vmem,) * 4,
        scratch_shapes=[
            pltpu.VMEM((8, HO * HI * NI, count), F32),
            pltpu.VMEM((PAIRS, 8, ROWS, 2 * count), BF),
            pltpu.SemaphoreType.DMA((8,)),
        ],
        compiler_params=params(8),
        cost_estimate=pl.CostEstimate(
            flops=4 * 10**9, bytes_accessed=20 * 10**6, transcendentals=0
        ),
        name="third",
    )(extended, table, refine, inputs[4])

    result = pl.pallas_call(
        functools.partial(fourth_kernel, ends_value, even_ring),
        out_shape=struct((1, count)),
        in_specs=[pl.BlockSpec(memory_space=pltpu.SMEM)] + [vmem] * 11,
        out_specs=vmem,
        scratch_shapes=[
            pltpu.VMEM((8, NI * NI, count), F32),
            pltpu.VMEM((PAIRS, 8, ROWS, 2 * count), F32),
            pltpu.VMEM((PAIRS, 3, 8, 32, 2 * count), F32),
            pltpu.VMEM((3, 8, ROWS, count), BF),
            pltpu.VMEM((3, 8, ROWS, count), F32),
            pltpu.VMEM((8, 32, count), F32),
            pltpu.VMEM((2, 4, 32, count), F32),
            pltpu.VMEM((2, 4, ROWS, count), F32),
            pltpu.VMEM((PAIRS, 8, 48, 2 * count), BF),
            pltpu.VMEM((6, 8, ROWS, count), F32),
        ],
        compiler_params=params(20),
        name="fourth",
    )(
        inv_reynolds,
        raw,
        factor,
        quad,
        extended,
        ends,
        table,
        local_metric,
        slots,
        got_a,
        got_b,
        const,
    )
    return result.reshape(count)


def solution(mesh):
    return jax.shard_map(
        per_device,
        mesh=mesh,
        in_specs=(
            P(None, None, ("grp", "strm", "azim")),
            P(("strm", "azim"), None),
            P(None, ("strm", "azim")),
            P("grp"),
        ),
        out_specs=P(("grp", "strm", "azim")),
        check_vma=False,
    )
```
